512 devices in a mesh: tm: 32 (over y, z_lo, core), chan: 16 (over z_hi, x).
Axes of the slice: x: 4, y: 8, z: 8 (z_hi: 4, z_lo: 2; z = z_hi * 2 + z_lo), core: 2. Of those that a mesh axis runs over, the one named last changes fastest.
Arguments:
- record: bfloat16 [2048, 49152], P('chan', 'tm'), may hold values from -250 to 250
- offsets: int32 [4], replicated, may hold values from 0 to 37152, as said below
- dead_mask: int32 [2048], P('chan'), may hold values 0 or 1
- sources: int32 [128], replicated, may hold values from 0 to 2047
Outputs:
- cross_spectra: float32 [640, 2, 128, 2048], P('tm', None, None, 'chan')
The draws below stay inside these ranges and needn't reach their ends.
Inputs may be any that keep to these rules, and one draw needn't show every extreme that they name: offsets[w] lies between w * 12000 and w * 12000 + 49152 - 4 * 12000; offsets[0] is 0 and the last window ends at the record's last sample.
All inputs are finite; a program needn't handle non-finite values. No bound on the sum of `dead_mask` on one device may be relied on, other than what follows from the above.
Results may differ from the reference program's by a relative error of at most 0.002.
The reference program's roundings to bfloat16 on the way count: a program that leaves them out, or rounds other values in their place, can miss the bound.
Values may be sent and summed in bfloat16 or wider, within the bound.
A program may use at most 128 MiB of HBM per device.

```python
import math
import jax
import jax.numpy as jnp
from jax import lax

W = 12000
F = 640
FLO = 6
NWIN = 4
NVS = 128
CH = 2048
NT = 49152


def draw_record(key, part):
    key_scale = jax.random.fold_in(key, 11)
    key_noise = jax.random.fold_in(key, 12)
    scale = jnp.exp(jax.random.uniform(key_scale, (CH, 1), jnp.float32, 0.0, math.log(10.0)))
    noise = jnp.clip(jax.random.normal(key_noise, (CH, NT), jnp.float32), -6.0, 6.0)
    values = noise * scale
    return values.astype(jnp.bfloat16)


def draw_offsets(key, part):
    key_perturbation = jax.random.fold_in(key, 21)
    slack = NT - NWIN * W
    jitter = jax.random.randint(key_perturbation, (NWIN,), 0, slack + 1)
    position = jnp.arange(NWIN, dtype=jnp.int32)
    jitter = jnp.where(position == 0, 0, jitter)
    jitter = jnp.where(position == NWIN - 1, slack, jitter)
    return (position * W + jitter).astype(jnp.int32)


def plant(entries, stream_key, low, largest):
    place = [jax.random.randint(jax.random.fold_in(stream_key, axis), (), 0, length) for axis, length in enumerate(entries.shape)]
    main_axis = entries.shape.index(max(entries.shape))
    next_to = place[:main_axis] + [(place[main_axis] + 1) % entries.shape[main_axis]] + place[main_axis + 1:]
    return entries.at[tuple(place)].set(low).at[tuple(next_to)].set(largest)


def setup_inputs(seed: int = 0) -> dict:
    key_of = jax.random.split(jax.random.key(seed), 5)
    record = draw_record(jax.random.fold_in(key_of[4], 71), 0)
    offsets = draw_offsets(jax.random.fold_in(key_of[4], 71), 0)
    dead_mask = plant((jax.random.randint(key_of[2], (CH,), 0, 16) < 15).astype(jnp.int32), jax.random.fold_in(key_of[2], 1), 0, 1)
    sources = plant(jax.random.randint(key_of[3], (NVS,), 0, CH), jax.random.fold_in(key_of[3], 1), 0, CH - 1).astype(jnp.int32)
    return {"record": record, "offsets": offsets, "dead_mask": dead_mask, "sources": sources}


def band_basis(first_bin, width, times):
    bins = first_bin + jnp.arange(width, dtype=jnp.int32)
    phase = times[:, None] * bins[None, :] % W
    angle = phase.astype(jnp.float32) * (2.0 * math.pi / W)
    return jnp.stack([jnp.cos(angle), -jnp.sin(angle)], axis=-1)

def whiten(fourier_coefficients, magnitude, level):
    denominator = magnitude + 0.1 * level[None] + 1e-06
    return (fourier_coefficients / denominator[:, :, None, :]).astype(jnp.bfloat16)

def reference(record, offsets, dead_mask, sources):
    times = jnp.arange(W, dtype=jnp.int32)
    windows = jnp.stack([lax.dynamic_slice_in_dim(record, offsets[window].astype(jnp.int32), W, 1) for window in range(NWIN)])
    rows = windows.reshape(NWIN * CH, W).astype(jnp.float32)
    pieces = []
    for first in range(0, F, 64):
        width = min(64, F - first)
        rounded = lax.optimization_barrier(band_basis(FLO + first, width, times).astype(jnp.bfloat16))
        basis = rounded.astype(jnp.float32).reshape(W, 2 * width)
        part = jnp.dot(rows, basis, preferred_element_type=jnp.float32, precision=lax.Precision.HIGHEST)
        pieces.append(part.reshape(NWIN, CH, width, 2))
    fourier_coefficients = jnp.transpose(jnp.concatenate(pieces, axis=2), (2, 0, 3, 1))
    magnitude = jnp.sqrt(fourier_coefficients[:, :, 0] ** 2 + fourier_coefficients[:, :, 1] ** 2)
    level = lax.optimization_barrier(jnp.sum(magnitude, axis=0)) / F
    white = whiten(fourier_coefficients, magnitude, level) * dead_mask.astype(jnp.bfloat16)[None, None, None, :]
    selected_bins = white[:, :, :, sources]
    left_channel = selected_bins.astype(jnp.float32).reshape(F, NWIN * 2, NVS)
    right_channel_real = white.astype(jnp.float32).reshape(F, NWIN * 2, CH)
    right_channel_imaginary = jnp.concatenate([white[:, :, 1:2], -white[:, :, 0:1]], axis=2).astype(jnp.float32).reshape(F, NWIN * 2, CH)
    real_component = jnp.einsum('qia,qie->qae', left_channel, right_channel_real, precision=lax.Precision.HIGHEST)
    imaginary_component = jnp.einsum('qia,qie->qae', left_channel, right_channel_imaginary, precision=lax.Precision.HIGHEST)
    return jnp.stack([real_component, imaginary_component], axis=1) / NWIN
```

```python
import functools
import math

import jax
import jax.numpy as jnp
from jax import lax
from jax.experimental import pallas as pl
from jax.experimental.pallas import tpu as pltpu
from jax.sharding import PartitionSpec as P

W = 12000
F = 640
FLO = 6
NWIN = 4
SLOTS = 2
FA = 64

MESH = pl.DeviceIdType.MESH


def _exchange_kernel(axis, n, gather, x_ref, o_ref, send_sem, recv_sem):
    me = lax.axis_index(axis)
    barrier = pltpu.get_barrier_semaphore()
    for i in range(1, n):
        peer = lax.rem(me + i, n)
        pl.semaphore_signal(barrier, inc=1, device_id={axis: peer}, device_id_type=MESH)
    pl.semaphore_wait(barrier, n - 1)

    def src_block(peer):
        return x_ref if gather else x_ref.at[peer]

    copies = []
    for i in range(1, n):
        peer = lax.rem(me + i, n)
        copy = pltpu.make_async_remote_copy(
            src_ref=src_block(peer),
            dst_ref=o_ref.at[me],
            send_sem=send_sem.at[peer],
            recv_sem=recv_sem.at[me],
            device_id={axis: peer},
            device_id_type=MESH,
        )
        copy.start()
        copies.append(copy)
    if gather:
        o_ref[me] = x_ref[...]
    else:
        o_ref[me] = x_ref[me]
    for copy in copies:
        copy.wait_send()
    for i in range(1, n):
        src = lax.rem(me + n - i, n)
        pltpu.make_async_remote_copy(
            src_ref=src_block(src),
            dst_ref=o_ref.at[src],
            send_sem=send_sem.at[src],
            recv_sem=recv_sem.at[src],
            device_id={axis: src},
            device_id_type=MESH,
        ).wait_recv()


def exchange(x, axis, n, gather, collective_id):
    out_shape = (n,) + (x.shape if gather else x.shape[1:])
    return pl.pallas_call(
        functools.partial(_exchange_kernel, axis, n, gather),
        out_shape=jax.ShapeDtypeStruct(out_shape, x.dtype),
        in_specs=[pl.BlockSpec(memory_space=pltpu.VMEM)],
        out_specs=pl.BlockSpec(memory_space=pltpu.VMEM),
        scratch_shapes=[pltpu.SemaphoreType.DMA((n,)), pltpu.SemaphoreType.DMA((n,))],
        compiler_params=pltpu.CompilerParams(collective_id=collective_id, has_side_effects=True),
    )(x)


def phasor(times, bins):
    phase = times[:, None] * bins[None, :] % W
    angle = phase.astype(jnp.float32) * (2.0 * math.pi / W)
    return jnp.cos(angle), -jnp.sin(angle)


def band_basis(times):
    coarse = FLO + FA * jnp.arange(F // FA, dtype=jnp.int32)
    fine = jnp.arange(FA, dtype=jnp.int32)
    ar, ai = phasor(times, coarse)
    br, bi = phasor(times, fine)
    ar, ai = ar[:, :, None], ai[:, :, None]
    br, bi = br[:, None, :], bi[:, None, :]
    re = ar * br - ai * bi
    im = ar * bi + ai * br
    basis = jnp.stack([re, im], axis=-1).reshape(times.shape[0], F, 2)
    return basis.astype(jnp.bfloat16)


def first_window(offsets, start):
    return jnp.sum((offsets + W <= start).astype(jnp.int32))


def shards(record, offsets, dead_mask, sources):
    n_tm = lax.axis_size("tm")
    n_chan = lax.axis_size("chan")
    bins_dev = F // n_tm
    channels, span = record.shape
    me = lax.axis_index("tm")
    start = me * span
    local_times = start + jnp.arange(span, dtype=jnp.int32)
    wa = first_window(offsets, start)

    partials = []
    for slot in range(SLOTS):
        window = wa + slot
        origin = offsets[jnp.minimum(window, NWIN - 1)]
        shifted = local_times - origin
        inside = (shifted >= 0) & (shifted < W) & (window < NWIN)
        basis = band_basis(jnp.where(inside, shifted, 0))
        masked = jnp.where(inside[None, :], record, jnp.zeros_like(record))
        partials.append(
            jnp.einsum("tkp,ct->kpc", basis, masked, preferred_element_type=jnp.float32)
        )
    blocks = jnp.stack(partials, axis=1).reshape(n_tm, bins_dev * SLOTS * 2, channels)
    received = exchange(blocks, "tm", n_tm, False, 0).reshape(
        n_tm, bins_dev, SLOTS, 2, channels
    )
    src_start = jnp.arange(n_tm, dtype=jnp.int32) * span
    src_wa = jnp.sum((offsets[None, :] + W <= src_start[:, None]).astype(jnp.int32), axis=1)
    src_win = src_wa[:, None] + jnp.arange(SLOTS, dtype=jnp.int32)[None, :]
    route = (src_win[None] == jnp.arange(NWIN, dtype=jnp.int32)[:, None, None]).astype(
        jnp.float32
    )
    spectrum = jnp.einsum(
        "wsj,skjpc->kwpc", route, received, precision=lax.Precision.HIGHEST
    )

    magnitude = jnp.sqrt(spectrum[:, :, 0] ** 2 + spectrum[:, :, 1] ** 2)
    level_part = jnp.sum(magnitude, axis=0)
    level_part = jnp.concatenate([level_part, jnp.zeros_like(level_part)], axis=0)
    level = jnp.sum(exchange(level_part, "tm", n_tm, True, 1), axis=0)[:NWIN] / F
    denominator = magnitude + 0.1 * level[None] + 1e-06
    white = (spectrum / denominator[:, :, None, :]).astype(jnp.bfloat16)
    white = white * dead_mask.astype(jnp.bfloat16)[None, None, None, :]

    local_index = sources - lax.axis_index("chan") * channels
    onehot = (jnp.arange(channels, dtype=jnp.int32)[:, None] == local_index[None, :]).astype(
        jnp.bfloat16
    )
    contrib = jnp.einsum("kwpc,cs->kwps", white, onehot, preferred_element_type=jnp.float32)
    contrib = contrib.astype(jnp.bfloat16).reshape(bins_dev * NWIN * 2, sources.shape[0])
    gathered = exchange(contrib, "chan", n_chan, True, 2)
    source_spec = jnp.sum(gathered.astype(jnp.float32), axis=0).astype(jnp.bfloat16)

    left_channel = source_spec.reshape(bins_dev, NWIN * 2, sources.shape[0])
    right_channel_real = white.reshape(bins_dev, NWIN * 2, channels)
    right_channel_imaginary = jnp.concatenate(
        [white[:, :, 1:2], -white[:, :, 0:1]], axis=2
    ).reshape(bins_dev, NWIN * 2, channels)
    real_component = jnp.einsum(
        "qia,qie->qae", left_channel, right_channel_real, preferred_element_type=jnp.float32
    )
    imaginary_component = jnp.einsum(
        "qia,qie->qae", left_channel, right_channel_imaginary, preferred_element_type=jnp.float32
    )
    return jnp.stack([real_component, imaginary_component], axis=1) / NWIN


def solution(mesh):
    return jax.shard_map(
        shards,
        mesh=mesh,
        in_specs=(P("chan", "tm"), P(), P("chan"), P()),
        out_specs=P("tm", None, None, "chan"),
        check_vma=False,
    )
```

```python
import functools
import math

import jax
import jax.numpy as jnp
from jax import lax
from jax.experimental import pallas as pl
from jax.experimental.pallas import tpu as pltpu
from jax.sharding import PartitionSpec as P

W = 12000
F = 640
FLO = 6
NWIN = 4
SLOTS = 2
FA = 64

MESH = pl.DeviceIdType.MESH


def window_plan(n_tm, span):
    total = n_tm * span
    slack = total - NWIN * W
    lows = [0] + [w * W for w in range(1, NWIN - 1)] + [total - W]
    highs = [0] + [w * W + slack for w in range(1, NWIN - 1)] + [total - W]
    first, count = [], []
    for d in range(n_tm):
        meets = [w for w in range(NWIN) if lows[w] < (d + 1) * span and highs[w] + W > d * span]
        assert meets and meets == list(range(meets[0], meets[0] + len(meets)))
        assert len(meets) <= SLOTS
        first.append(meets[0])
        count.append(len(meets))
    return first, count


def _any_of(me, members):
    hit = jnp.bool_(False)
    for m in members:
        hit = hit | (me == m)
    return hit


def _fused_kernel(n_tm, n_chan, bins_dev, first, count,
                  blocks_ref, onehot_ref, mask_ref,
                  white_ref, srcspec_ref,
                  recv, spec, lvl_send, lvl_recv, src_send, src_recv,
                  a2a_send_sem, a2a_recv_sem, lvl_send_sem, lvl_recv_sem,
                  src_send_sem, src_recv_sem):
    me = lax.axis_index("tm")
    mc = lax.axis_index("chan")
    two = [d for d in range(n_tm) if count[d] == 2]
    me_two = _any_of(me, two)

    barrier = pltpu.get_barrier_semaphore()
    for i in range(1, n_tm):
        pl.semaphore_signal(barrier, inc=1, device_id={"tm": lax.rem(me + i, n_tm)},
                            device_id_type=MESH)
    for i in range(1, n_chan):
        pl.semaphore_signal(barrier, inc=1, device_id={"chan": lax.rem(mc + i, n_chan)},
                            device_id_type=MESH)
    pl.semaphore_wait(barrier, n_tm - 1 + n_chan - 1)

    def a2a(peer, slot, src_dev):
        return pltpu.make_async_remote_copy(
            src_ref=blocks_ref.at[peer, slot],
            dst_ref=recv.at[src_dev, slot],
            send_sem=a2a_send_sem.at[peer, slot],
            recv_sem=a2a_recv_sem.at[src_dev, slot],
            device_id={"tm": peer},
            device_id_type=MESH,
        )

    for i in range(1, n_tm):
        peer = lax.rem(me + i, n_tm)
        a2a(peer, 0, me).start()

        @pl.when(me_two)
        def _():
            a2a(peer, 1, me).start()

    recv[me] = blocks_ref[me]
    for i in range(1, n_tm):
        peer = lax.rem(me + i, n_tm)
        a2a(peer, 0, me).wait_send()

        @pl.when(me_two)
        def _():
            a2a(peer, 1, me).wait_send()

    for s in range(n_tm):
        @pl.when(me != s)
        def _():
            a2a(s, 0, s).wait_recv()
            if count[s] == 2:
                a2a(s, 1, s).wait_recv()

    for w in range(NWIN):
        acc = None
        for s in range(n_tm):
            for j in range(count[s]):
                if first[s] + j == w:
                    part = recv[s, j]
                    acc = part if acc is None else acc + part
        spec[w] = acc

    rows = []
    for w in range(NWIN):
        re = spec[w, 0:bins_dev, :]
        im = spec[w, bins_dev:2 * bins_dev, :]
        mag = jnp.sqrt(re * re + im * im)
        rows.append(jnp.sum(mag, axis=0, keepdims=True))
    rows.append(jnp.zeros((8 - NWIN, rows[0].shape[1]), jnp.float32))
    lvl_send[...] = jnp.concatenate(rows, axis=0)

    def lvl(peer, src_dev):
        return pltpu.make_async_remote_copy(
            src_ref=lvl_send,
            dst_ref=lvl_recv.at[src_dev],
            send_sem=lvl_send_sem.at[peer],
            recv_sem=lvl_recv_sem.at[src_dev],
            device_id={"tm": peer},
            device_id_type=MESH,
        )

    for i in range(1, n_tm):
        lvl(lax.rem(me + i, n_tm), me).start()
    lvl_recv[me] = lvl_send[...]
    for i in range(1, n_tm):
        lvl(lax.rem(me + i, n_tm), me).wait_send()
    for i in range(1, n_tm):
        src = lax.rem(me + n_tm - i, n_tm)
        lvl(src, src).wait_recv()

    level = lvl_recv[0]
    for s in range(1, n_tm):
        level = level + lvl_recv[s]
    level = level / F

    mask = mask_ref[...]
    onehot = onehot_ref[...]
    for w in range(NWIN):
        re = spec[w, 0:bins_dev, :]
        im = spec[w, bins_dev:2 * bins_dev, :]
        mag = jnp.sqrt(re * re + im * im)
        den = mag + 0.1 * level[w:w + 1, :] + 1e-06
        for p, part in enumerate((re, im)):
            white = (part / den).astype(jnp.bfloat16).astype(jnp.float32) * mask
            white_ref[2 * w + p] = white
            src_send[2 * w + p] = jnp.dot(
                white.astype(jnp.bfloat16), onehot, preferred_element_type=jnp.float32
            )

    def srcc(peer, src_dev):
        return pltpu.make_async_remote_copy(
            src_ref=src_send,
            dst_ref=src_recv.at[src_dev],
            send_sem=src_send_sem.at[peer],
            recv_sem=src_recv_sem.at[src_dev],
            device_id={"chan": peer},
            device_id_type=MESH,
        )

    for i in range(1, n_chan):
        srcc(lax.rem(mc + i, n_chan), mc).start()
    src_recv[mc] = src_send[...]
    for i in range(1, n_chan):
        srcc(lax.rem(mc + i, n_chan), mc).wait_send()
    for i in range(1, n_chan):
        src = lax.rem(mc + n_chan - i, n_chan)
        srcc(src, src).wait_recv()

    total = src_recv[0]
    for s in range(1, n_chan):
        total = total + src_recv[s]
    srcspec_ref[...] = total


def fused_exchange(blocks, onehot, mask, n_tm, n_chan, bins_dev, first, count):
    channels = blocks.shape[-1]
    nsrc = onehot.shape[1]
    vmem = pl.BlockSpec(memory_space=pltpu.VMEM)
    return pl.pallas_call(
        functools.partial(_fused_kernel, n_tm, n_chan, bins_dev, first, count),
        out_shape=(
            jax.ShapeDtypeStruct((NWIN * 2, bins_dev, channels), jnp.float32),
            jax.ShapeDtypeStruct((NWIN * 2, bins_dev, nsrc), jnp.float32),
        ),
        in_specs=[vmem, vmem, vmem],
        out_specs=(vmem, vmem),
        scratch_shapes=[
            pltpu.VMEM(blocks.shape, jnp.float32),
            pltpu.VMEM((NWIN, 2 * bins_dev, channels), jnp.float32),
            pltpu.VMEM((8, channels), jnp.float32),
            pltpu.VMEM((n_tm, 8, channels), jnp.float32),
            pltpu.VMEM((NWIN * 2, bins_dev, nsrc), jnp.float32),
            pltpu.VMEM((n_chan, NWIN * 2, bins_dev, nsrc), jnp.float32),
            pltpu.SemaphoreType.DMA((n_tm, SLOTS)),
            pltpu.SemaphoreType.DMA((n_tm, SLOTS)),
            pltpu.SemaphoreType.DMA((n_tm,)),
            pltpu.SemaphoreType.DMA((n_tm,)),
            pltpu.SemaphoreType.DMA((n_chan,)),
            pltpu.SemaphoreType.DMA((n_chan,)),
        ],
        compiler_params=pltpu.CompilerParams(collective_id=0, has_side_effects=True),
    )(blocks, onehot, mask)


def phasor(times, bins):
    phase = times[:, None] * bins[None, :] % W
    angle = phase.astype(jnp.float32) * (2.0 * math.pi / W)
    return jnp.cos(angle), -jnp.sin(angle)


def band_basis(times):
    coarse = FLO + FA * jnp.arange(F // FA, dtype=jnp.int32)
    fine = jnp.arange(FA, dtype=jnp.int32)
    ar, ai = phasor(times, coarse)
    br, bi = phasor(times, fine)
    ar, ai = ar[:, :, None], ai[:, :, None]
    br, bi = br[:, None, :], bi[:, None, :]
    re = ar * br - ai * bi
    im = ar * bi + ai * br
    basis = jnp.stack([re, im], axis=-1).reshape(times.shape[0], F, 2)
    return basis.astype(jnp.bfloat16)


def shards(record, offsets, dead_mask, sources):
    n_tm = lax.axis_size("tm")
    n_chan = lax.axis_size("chan")
    bins_dev = F // n_tm
    channels, span = record.shape
    first, count = window_plan(n_tm, span)
    me = lax.axis_index("tm")
    start = me * span
    local_times = start + jnp.arange(span, dtype=jnp.int32)
    wa = jnp.asarray(first, jnp.int32)[me]

    partials = []
    for slot in range(SLOTS):
        window = wa + slot
        origin = offsets[jnp.minimum(window, NWIN - 1)]
        shifted = local_times - origin
        inside = (shifted >= 0) & (shifted < W) & (window < NWIN)
        basis = band_basis(jnp.where(inside, shifted, 0))
        masked = jnp.where(inside[None, :], record, jnp.zeros_like(record))
        part = jnp.einsum("tkp,ct->pkc", basis, masked, preferred_element_type=jnp.float32)
        part = part.reshape(2, n_tm, bins_dev, channels).transpose(1, 0, 2, 3)
        partials.append(part)
    blocks = jnp.stack(partials, axis=1).reshape(n_tm, SLOTS, 2 * bins_dev, channels)

    local_index = sources - lax.axis_index("chan") * channels
    onehot = (jnp.arange(channels, dtype=jnp.int32)[:, None] == local_index[None, :]).astype(
        jnp.bfloat16
    )
    mask = dead_mask.astype(jnp.float32)[None, :]
    white, source_spec = fused_exchange(
        blocks, onehot, mask, n_tm, n_chan, bins_dev, first, count
    )

    left = source_spec.astype(jnp.bfloat16).reshape(NWIN, 2, bins_dev, -1)
    right = white.astype(jnp.bfloat16).reshape(NWIN, 2, bins_dev, channels)
    right_imaginary = jnp.stack([right[:, 1], -right[:, 0]], axis=1)
    real_component = jnp.einsum(
        "wpks,wpkc->ksc", left, right, preferred_element_type=jnp.float32
    )
    imaginary_component = jnp.einsum(
        "wpks,wpkc->ksc", left, right_imaginary, preferred_element_type=jnp.float32
    )
    return jnp.stack([real_component, imaginary_component], axis=1) / NWIN


def solution(mesh):
    return jax.shard_map(
        shards,
        mesh=mesh,
        in_specs=(P("chan", "tm"), P(), P("chan"), P()),
        out_specs=P("tm", None, None, "chan"),
        check_vma=False,
    )
```

```python
import functools
import math

import jax
import jax.numpy as jnp
from jax import lax
from jax.experimental import pallas as pl
from jax.experimental.pallas import tpu as pltpu
from jax.sharding import PartitionSpec as P

W = 12000
F = 640
FLO = 6
NWIN = 4
SLOTS = 2
FA = 64

MESH = pl.DeviceIdType.MESH


def window_plan(n_tm, span):
    total = n_tm * span
    slack = total - NWIN * W
    lows = [0] + [w * W for w in range(1, NWIN - 1)] + [total - W]
    highs = [0] + [w * W + slack for w in range(1, NWIN - 1)] + [total - W]
    first, count = [], []
    for d in range(n_tm):
        meets = [w for w in range(NWIN) if lows[w] < (d + 1) * span and highs[w] + W > d * span]
        assert meets and meets == list(range(meets[0], meets[0] + len(meets)))
        assert len(meets) <= SLOTS
        first.append(meets[0])
        count.append(len(meets))
    return first, count


def _any_of(me, members):
    hit = jnp.bool_(False)
    for m in members:
        hit = hit | (me == m)
    return hit


def _fused_kernel(n_tm, n_chan, bins_dev, first, count,
                  blocks_ref, onehot_ref, mask_ref,
                  white_ref, srcspec_ref,
                  recv, spec, lvl_send, lvl_recv, src_send, src_recv,
                  a2a_send_sem, a2a_recv_sem, lvl_send_sem, lvl_recv_sem,
                  src_send_sem, src_recv_sem):
    me = lax.axis_index("tm")
    mc = lax.axis_index("chan")
    two = [d for d in range(n_tm) if count[d] == 2]
    me_two = _any_of(me, two)

    barrier = pltpu.get_barrier_semaphore()
    for i in range(1, n_tm):
        pl.semaphore_signal(barrier, inc=1, device_id={"tm": lax.rem(me + i, n_tm)},
                            device_id_type=MESH)
    for i in range(1, n_chan):
        pl.semaphore_signal(barrier, inc=1, device_id={"chan": lax.rem(mc + i, n_chan)},
                            device_id_type=MESH)
    pl.semaphore_wait(barrier, n_tm - 1 + n_chan - 1)

    def a2a(peer, slot, src_dev):
        return pltpu.make_async_remote_copy(
            src_ref=blocks_ref.at[peer, slot],
            dst_ref=recv.at[src_dev, slot],
            send_sem=a2a_send_sem.at[peer, slot],
            recv_sem=a2a_recv_sem.at[src_dev, slot],
            device_id={"tm": peer},
            device_id_type=MESH,
        )

    for i in range(1, n_tm):
        peer = lax.rem(me + i, n_tm)
        a2a(peer, 0, me).start()

        @pl.when(me_two)
        def _():
            a2a(peer, 1, me).start()

    recv[me] = blocks_ref[me]
    for i in range(1, n_tm):
        peer = lax.rem(me + i, n_tm)
        a2a(peer, 0, me).wait_send()

        @pl.when(me_two)
        def _():
            a2a(peer, 1, me).wait_send()

    for s in range(n_tm):
        @pl.when(me != s)
        def _():
            a2a(s, 0, s).wait_recv()
            if count[s] == 2:
                a2a(s, 1, s).wait_recv()

    for w in range(NWIN):
        acc = None
        for s in range(n_tm):
            for j in range(count[s]):
                if first[s] + j == w:
                    part = recv[s, j]
                    acc = part if acc is None else acc + part
        spec[w] = acc

    rows = []
    for w in range(NWIN):
        re = spec[w, pl.ds(0, bins_dev, stride=2), :]
        im = spec[w, pl.ds(1, bins_dev, stride=2), :]
        mag = jnp.sqrt(re * re + im * im)
        rows.append(jnp.sum(mag, axis=0, keepdims=True))
    rows.append(jnp.zeros((8 - NWIN, rows[0].shape[1]), jnp.float32))
    lvl_send[...] = jnp.concatenate(rows, axis=0)

    def lvl(peer, src_dev):
        return pltpu.make_async_remote_copy(
            src_ref=lvl_send,
            dst_ref=lvl_recv.at[src_dev],
            send_sem=lvl_send_sem.at[peer],
            recv_sem=lvl_recv_sem.at[src_dev],
            device_id={"tm": peer},
            device_id_type=MESH,
        )

    for i in range(1, n_tm):
        lvl(lax.rem(me + i, n_tm), me).start()
    lvl_recv[me] = lvl_send[...]
    for i in range(1, n_tm):
        lvl(lax.rem(me + i, n_tm), me).wait_send()
    for i in range(1, n_tm):
        src = lax.rem(me + n_tm - i, n_tm)
        lvl(src, src).wait_recv()

    level = lvl_recv[0]
    for s in range(1, n_tm):
        level = level + lvl_recv[s]
    level = level / F

    mask = mask_ref[...]
    onehot = onehot_ref[...]
    for w in range(NWIN):
        re = spec[w, pl.ds(0, bins_dev, stride=2), :]
        im = spec[w, pl.ds(1, bins_dev, stride=2), :]
        mag = jnp.sqrt(re * re + im * im)
        den = mag + 0.1 * level[w:w + 1, :] + 1e-06
        for p, part in enumerate((re, im)):
            white = (part / den).astype(jnp.bfloat16).astype(jnp.float32) * mask
            white_ref[2 * w + p] = white
            src_send[2 * w + p] = jnp.dot(
                white.astype(jnp.bfloat16), onehot, preferred_element_type=jnp.float32
            )

    def srcc(peer, src_dev):
        return pltpu.make_async_remote_copy(
            src_ref=src_send,
            dst_ref=src_recv.at[src_dev],
            send_sem=src_send_sem.at[peer],
            recv_sem=src_recv_sem.at[src_dev],
            device_id={"chan": peer},
            device_id_type=MESH,
        )

    for i in range(1, n_chan):
        srcc(lax.rem(mc + i, n_chan), mc).start()
    src_recv[mc] = src_send[...]
    for i in range(1, n_chan):
        srcc(lax.rem(mc + i, n_chan), mc).wait_send()
    for i in range(1, n_chan):
        src = lax.rem(mc + n_chan - i, n_chan)
        srcc(src, src).wait_recv()

    total = src_recv[0]
    for s in range(1, n_chan):
        total = total + src_recv[s]
    srcspec_ref[...] = total


def fused_exchange(blocks, onehot, mask, n_tm, n_chan, bins_dev, first, count):
    channels = blocks.shape[-1]
    nsrc = onehot.shape[1]
    vmem = pl.BlockSpec(memory_space=pltpu.VMEM)
    return pl.pallas_call(
        functools.partial(_fused_kernel, n_tm, n_chan, bins_dev, first, count),
        out_shape=(
            jax.ShapeDtypeStruct((NWIN * 2, bins_dev, channels), jnp.float32),
            jax.ShapeDtypeStruct((NWIN * 2, bins_dev, nsrc), jnp.float32),
        ),
        in_specs=[vmem, vmem, vmem],
        out_specs=(vmem, vmem),
        scratch_shapes=[
            pltpu.VMEM(blocks.shape, jnp.float32),
            pltpu.VMEM((NWIN, 2 * bins_dev, channels), jnp.float32),
            pltpu.VMEM((8, channels), jnp.float32),
            pltpu.VMEM((n_tm, 8, channels), jnp.float32),
            pltpu.VMEM((NWIN * 2, bins_dev, nsrc), jnp.float32),
            pltpu.VMEM((n_chan, NWIN * 2, bins_dev, nsrc), jnp.float32),
            pltpu.SemaphoreType.DMA((n_tm, SLOTS)),
            pltpu.SemaphoreType.DMA((n_tm, SLOTS)),
            pltpu.SemaphoreType.DMA((n_tm,)),
            pltpu.SemaphoreType.DMA((n_tm,)),
            pltpu.SemaphoreType.DMA((n_chan,)),
            pltpu.SemaphoreType.DMA((n_chan,)),
        ],
        compiler_params=pltpu.CompilerParams(collective_id=0, has_side_effects=True),
    )(blocks, onehot, mask)


def phasor(times, bins):
    phase = times[:, None] * bins[None, :] % W
    angle = phase.astype(jnp.float32) * (2.0 * math.pi / W)
    return jnp.cos(angle), -jnp.sin(angle)


def band_basis(times):
    coarse = FLO + FA * jnp.arange(F // FA, dtype=jnp.int32)
    fine = jnp.arange(FA, dtype=jnp.int32)
    ar, ai = phasor(times, coarse)
    br, bi = phasor(times, fine)
    ar, ai = ar[:, :, None], ai[:, :, None]
    br, bi = br[:, None, :], bi[:, None, :]
    re = ar * br - ai * bi
    im = ar * bi + ai * br
    basis = jnp.stack([re, im], axis=-1).reshape(times.shape[0], F, 2)
    return basis.astype(jnp.bfloat16)


def shards(record, offsets, dead_mask, sources):
    n_tm = lax.axis_size("tm")
    n_chan = lax.axis_size("chan")
    bins_dev = F // n_tm
    channels, span = record.shape
    first, count = window_plan(n_tm, span)
    me = lax.axis_index("tm")
    start = me * span
    local_times = start + jnp.arange(span, dtype=jnp.int32)
    wa = jnp.asarray(first, jnp.int32)[me]

    partials = []
    for slot in range(SLOTS):
        window = wa + slot
        origin = offsets[jnp.minimum(window, NWIN - 1)]
        shifted = local_times - origin
        inside = (shifted >= 0) & (shifted < W) & (window < NWIN)
        basis = band_basis(jnp.where(inside, shifted, 0))
        masked = jnp.where(inside[None, :], record, jnp.zeros_like(record))
        part = jnp.einsum("tkp,ct->kpc", basis, masked, preferred_element_type=jnp.float32)
        partials.append(part.reshape(n_tm, 2 * bins_dev, channels))
    blocks = jnp.stack(partials, axis=1).reshape(n_tm, SLOTS, 2 * bins_dev, channels)

    local_index = sources - lax.axis_index("chan") * channels
    onehot = (jnp.arange(channels, dtype=jnp.int32)[:, None] == local_index[None, :]).astype(
        jnp.bfloat16
    )
    mask = dead_mask.astype(jnp.float32)[None, :]
    white, source_spec = fused_exchange(
        blocks, onehot, mask, n_tm, n_chan, bins_dev, first, count
    )

    left = source_spec.astype(jnp.bfloat16).reshape(NWIN, 2, bins_dev, -1)
    right = white.astype(jnp.bfloat16).reshape(NWIN, 2, bins_dev, channels)
    right_imaginary = jnp.stack([right[:, 1], -right[:, 0]], axis=1)
    real_component = jnp.einsum(
        "wpks,wpkc->ksc", left, right, preferred_element_type=jnp.float32
    )
    imaginary_component = jnp.einsum(
        "wpks,wpkc->ksc", left, right_imaginary, preferred_element_type=jnp.float32
    )
    return jnp.stack([real_component, imaginary_component], axis=1) / NWIN


def solution(mesh):
    return jax.shard_map(
        shards,
        mesh=mesh,
        in_specs=(P("chan", "tm"), P(), P("chan"), P()),
        out_specs=P("tm", None, None, "chan"),
        check_vma=False,
    )
```

```python
import functools
import math

import jax
import jax.numpy as jnp
from jax import lax
from jax.experimental import pallas as pl
from jax.experimental.pallas import tpu as pltpu
from jax.sharding import PartitionSpec as P

W = 12000
F = 640
FLO = 6
NWIN = 4
SLOTS = 2
FA = 64

MESH = pl.DeviceIdType.MESH


def window_plan(n_tm, span):
    total = n_tm * span
    slack = total - NWIN * W
    lows = [0] + [w * W for w in range(1, NWIN - 1)] + [total - W]
    highs = [0] + [w * W + slack for w in range(1, NWIN - 1)] + [total - W]
    first, count = [], []
    for d in range(n_tm):
        meets = [w for w in range(NWIN) if lows[w] < (d + 1) * span and highs[w] + W > d * span]
        assert meets and meets == list(range(meets[0], meets[0] + len(meets)))
        assert len(meets) <= SLOTS
        first.append(meets[0])
        count.append(len(meets))
    return first, count


def _any_of(me, members):
    hit = jnp.bool_(False)
    for m in members:
        hit = hit | (me == m)
    return hit


def _fused_kernel(n_tm, n_chan, bins_dev, first, count,
                  blocks_ref, onehot_ref, mask_ref,
                  white_ref, srcspec_ref,
                  recv, spec, lvl_send, lvl_recv, src_send, src_recv,
                  a2a_send_sem, a2a_recv_sem, lvl_send_sem, lvl_recv_sem,
                  src_send_sem, src_recv_sem):
    me = lax.axis_index("tm")
    mc = lax.axis_index("chan")
    two = [d for d in range(n_tm) if count[d] == 2]
    me_two = _any_of(me, two)

    barrier = pltpu.get_barrier_semaphore()
    for i in range(1, n_tm):
        pl.semaphore_signal(barrier, inc=1, device_id={"tm": lax.rem(me + i, n_tm)},
                            device_id_type=MESH)
    for i in range(1, n_chan):
        pl.semaphore_signal(barrier, inc=1, device_id={"chan": lax.rem(mc + i, n_chan)},
                            device_id_type=MESH)
    pl.semaphore_wait(barrier, n_tm - 1 + n_chan - 1)

    def a2a(peer, slot, src_dev):
        return pltpu.make_async_remote_copy(
            src_ref=blocks_ref.at[peer, slot],
            dst_ref=recv.at[src_dev, slot],
            send_sem=a2a_send_sem.at[peer, slot],
            recv_sem=a2a_recv_sem.at[src_dev, slot],
            device_id={"tm": peer},
            device_id_type=MESH,
        )

    for i in range(1, n_tm):
        peer = lax.rem(me + i, n_tm)
        a2a(peer, 0, me).start()

        @pl.when(me_two)
        def _():
            a2a(peer, 1, me).start()

    recv[me] = blocks_ref[me]
    for i in range(1, n_tm):
        peer = lax.rem(me + i, n_tm)
        a2a(peer, 0, me).wait_send()

        @pl.when(me_two)
        def _():
            a2a(peer, 1, me).wait_send()

    for s in range(n_tm):
        @pl.when(me != s)
        def _():
            a2a(s, 0, s).wait_recv()
            if count[s] == 2:
                a2a(s, 1, s).wait_recv()

    for w in range(NWIN):
        acc = None
        for s in range(n_tm):
            for j in range(count[s]):
                if first[s] + j == w:
                    part = recv[s, j]
                    acc = part if acc is None else acc + part
        spec[w] = acc

    rows = []
    for w in range(NWIN):
        re = spec[w, 0:bins_dev, :]
        im = spec[w, bins_dev:2 * bins_dev, :]
        mag = jnp.sqrt(re * re + im * im)
        rows.append(jnp.sum(mag, axis=0, keepdims=True))
    rows.append(jnp.zeros((8 - NWIN, rows[0].shape[1]), jnp.float32))
    lvl_send[...] = jnp.concatenate(rows, axis=0)

    def lvl(peer, src_dev):
        return pltpu.make_async_remote_copy(
            src_ref=lvl_send,
            dst_ref=lvl_recv.at[src_dev],
            send_sem=lvl_send_sem.at[peer],
            recv_sem=lvl_recv_sem.at[src_dev],
            device_id={"tm": peer},
            device_id_type=MESH,
        )

    for i in range(1, n_tm):
        lvl(lax.rem(me + i, n_tm), me).start()
    lvl_recv[me] = lvl_send[...]
    for i in range(1, n_tm):
        lvl(lax.rem(me + i, n_tm), me).wait_send()
    for i in range(1, n_tm):
        src = lax.rem(me + n_tm - i, n_tm)
        lvl(src, src).wait_recv()

    level = lvl_recv[0]
    for s in range(1, n_tm):
        level = level + lvl_recv[s]
    level = level / F

    mask = mask_ref[...]
    onehot = onehot_ref[...]
    for w in range(NWIN):
        re = spec[w, 0:bins_dev, :]
        im = spec[w, bins_dev:2 * bins_dev, :]
        mag = jnp.sqrt(re * re + im * im)
        den = mag + 0.1 * level[w:w + 1, :] + 1e-06
        for p, part in enumerate((re, im)):
            white = (part / den).astype(jnp.bfloat16).astype(jnp.float32) * mask
            white_ref[2 * w + p] = white
            src_send[2 * w + p] = jnp.dot(
                white.astype(jnp.bfloat16), onehot, preferred_element_type=jnp.float32
            )

    def srcc(peer, src_dev):
        return pltpu.make_async_remote_copy(
            src_ref=src_send,
            dst_ref=src_recv.at[src_dev],
            send_sem=src_send_sem.at[peer],
            recv_sem=src_recv_sem.at[src_dev],
            device_id={"chan": peer},
            device_id_type=MESH,
        )

    for i in range(1, n_chan):
        srcc(lax.rem(mc + i, n_chan), mc).start()
    src_recv[mc] = src_send[...]
    for i in range(1, n_chan):
        srcc(lax.rem(mc + i, n_chan), mc).wait_send()
    for i in range(1, n_chan):
        src = lax.rem(mc + n_chan - i, n_chan)
        srcc(src, src).wait_recv()

    total = src_recv[0]
    for s in range(1, n_chan):
        total = total + src_recv[s]
    srcspec_ref[...] = total


def fused_exchange(blocks, onehot, mask, n_tm, n_chan, bins_dev, first, count):
    channels = blocks.shape[-1]
    nsrc = onehot.shape[1]
    vmem = pl.BlockSpec(memory_space=pltpu.VMEM)
    return pl.pallas_call(
        functools.partial(_fused_kernel, n_tm, n_chan, bins_dev, first, count),
        out_shape=(
            jax.ShapeDtypeStruct((NWIN * 2, bins_dev, channels), jnp.float32),
            jax.ShapeDtypeStruct((NWIN * 2, bins_dev, nsrc), jnp.float32),
        ),
        in_specs=[vmem, vmem, vmem],
        out_specs=(vmem, vmem),
        scratch_shapes=[
            pltpu.VMEM(blocks.shape, jnp.float32),
            pltpu.VMEM((NWIN, 2 * bins_dev, channels), jnp.float32),
            pltpu.VMEM((8, channels), jnp.float32),
            pltpu.VMEM((n_tm, 8, channels), jnp.float32),
            pltpu.VMEM((NWIN * 2, bins_dev, nsrc), jnp.float32),
            pltpu.VMEM((n_chan, NWIN * 2, bins_dev, nsrc), jnp.float32),
            pltpu.SemaphoreType.DMA((n_tm, SLOTS)),
            pltpu.SemaphoreType.DMA((n_tm, SLOTS)),
            pltpu.SemaphoreType.DMA((n_tm,)),
            pltpu.SemaphoreType.DMA((n_tm,)),
            pltpu.SemaphoreType.DMA((n_chan,)),
            pltpu.SemaphoreType.DMA((n_chan,)),
        ],
        compiler_params=pltpu.CompilerParams(collective_id=0, has_side_effects=True),
    )(blocks, onehot, mask)


def _dft_kernel(n_tm, bins_dev, ar_ref, ai_ref, c1_ref, c2_ref, x_ref, o_ref, lhs):
    group = lhs.shape[0] // (2 * bins_dev)
    for slot in range(SLOTS):
        c1 = c1_ref[slot]
        c2 = c2_ref[slot]
        x = x_ref[slot]
        for g in range(n_tm // group):
            for dd in range(group):
                d = g * group + dd
                ar = ar_ref[slot, d:d + 1, :]
                ai = ai_ref[slot, d:d + 1, :]
                lhs[dd * 2 * bins_dev:(dd + 1) * 2 * bins_dev, :] = ar * c1 + ai * c2
            res = lax.dot_general(
                lhs[...].astype(jnp.bfloat16), x, (((1,), (1,)), ((), ())),
                preferred_element_type=jnp.float32,
            )
            o_ref[g * group:(g + 1) * group, slot] = res.reshape(group, 2 * bins_dev, x.shape[0])


def dft(ar, ai, c1, c2, x, n_tm, bins_dev):
    channels, span = x.shape[1], x.shape[2]
    group = 8
    vmem = pl.BlockSpec(memory_space=pltpu.VMEM)
    return pl.pallas_call(
        functools.partial(_dft_kernel, n_tm, bins_dev),
        out_shape=jax.ShapeDtypeStruct((n_tm, SLOTS, 2 * bins_dev, channels), jnp.float32),
        in_specs=[vmem] * 5,
        out_specs=vmem,
        scratch_shapes=[pltpu.VMEM((group * 2 * bins_dev, span), jnp.float32)],
    )(ar, ai, c1, c2, x)


def phasor(bins, times):
    phase = bins[:, None] * times[None, :] % W
    angle = phase.astype(jnp.float32) * (2.0 * math.pi / W)
    return jnp.cos(angle), -jnp.sin(angle)


def shards(record, offsets, dead_mask, sources):
    n_tm = lax.axis_size("tm")
    n_chan = lax.axis_size("chan")
    bins_dev = F // n_tm
    channels, span = record.shape
    first, count = window_plan(n_tm, span)
    me = lax.axis_index("tm")
    start = me * span
    local_times = start + jnp.arange(span, dtype=jnp.int32)
    wa = jnp.asarray(first, jnp.int32)[me]
    coarse = FLO + bins_dev * jnp.arange(n_tm, dtype=jnp.int32)
    fine = jnp.arange(bins_dev, dtype=jnp.int32)

    ars, ais, c1s, c2s, xs = [], [], [], [], []
    for slot in range(SLOTS):
        window = wa + slot
        origin = offsets[jnp.minimum(window, NWIN - 1)]
        shifted = local_times - origin
        inside = (shifted >= 0) & (shifted < W) & (window < NWIN)
        times = jnp.where(inside, shifted, 0)
        ar, ai = phasor(coarse, times)
        br, bi = phasor(fine, times)
        ars.append(ar)
        ais.append(ai)
        c1s.append(jnp.concatenate([br, bi], axis=0))
        c2s.append(jnp.concatenate([-bi, br], axis=0))
        xs.append(jnp.where(inside[None, :], record, jnp.zeros_like(record)))
    blocks = dft(jnp.stack(ars), jnp.stack(ais), jnp.stack(c1s), jnp.stack(c2s),
                 jnp.stack(xs), n_tm, bins_dev)

    local_index = sources - lax.axis_index("chan") * channels
    onehot = (jnp.arange(channels, dtype=jnp.int32)[:, None] == local_index[None, :]).astype(
        jnp.bfloat16
    )
    mask = dead_mask.astype(jnp.float32)[None, :]
    white, source_spec = fused_exchange(
        blocks, onehot, mask, n_tm, n_chan, bins_dev, first, count
    )

    left = source_spec.astype(jnp.bfloat16).reshape(NWIN, 2, bins_dev, -1)
    right = white.astype(jnp.bfloat16).reshape(NWIN, 2, bins_dev, channels)
    right_imaginary = jnp.stack([right[:, 1], -right[:, 0]], axis=1)
    real_component = jnp.einsum(
        "wpks,wpkc->ksc", left, right, preferred_element_type=jnp.float32
    )
    imaginary_component = jnp.einsum(
        "wpks,wpkc->ksc", left, right_imaginary, preferred_element_type=jnp.float32
    )
    return jnp.stack([real_component, imaginary_component], axis=1) / NWIN


def solution(mesh):
    return jax.shard_map(
        shards,
        mesh=mesh,
        in_specs=(P("chan", "tm"), P(), P("chan"), P()),
        out_specs=P("tm", None, None, "chan"),
        check_vma=False,
    )
```

```python
import functools
import math

import jax
import jax.numpy as jnp
from jax import lax
from jax.experimental import pallas as pl
from jax.experimental.pallas import tpu as pltpu
from jax.sharding import PartitionSpec as P

W = 12000
F = 640
FLO = 6
NWIN = 4
SLOTS = 2
FA = 64

MESH = pl.DeviceIdType.MESH


def window_plan(n_tm, span):
    total = n_tm * span
    slack = total - NWIN * W
    lows = [0] + [w * W for w in range(1, NWIN - 1)] + [total - W]
    highs = [0] + [w * W + slack for w in range(1, NWIN - 1)] + [total - W]
    first, count = [], []
    for d in range(n_tm):
        meets = [w for w in range(NWIN) if lows[w] < (d + 1) * span and highs[w] + W > d * span]
        assert meets and meets == list(range(meets[0], meets[0] + len(meets)))
        assert len(meets) <= SLOTS
        first.append(meets[0])
        count.append(len(meets))
    return first, count


def _any_of(me, members):
    hit = jnp.bool_(False)
    for m in members:
        hit = hit | (me == m)
    return hit


def _fused_kernel(n_tm, n_chan, bins_dev, first, count,
                  ar_ref, ai_ref, c1_ref, c2_ref, x_ref, onehot_ref, mask_ref,
                  white_ref, srcspec_ref,
                  blocks_ref, lhs, recv, spec, lvl_send, lvl_recv, src_send, src_recv,
                  a2a_send_sem, a2a_recv_sem, lvl_send_sem, lvl_recv_sem,
                  src_send_sem, src_recv_sem):
    me = lax.axis_index("tm")
    mc = lax.axis_index("chan")
    two = [d for d in range(n_tm) if count[d] == 2]
    me_two = _any_of(me, two)
    rows = 2 * bins_dev
    group = lhs.shape[0] // rows

    barrier = pltpu.get_barrier_semaphore()
    for i in range(1, n_tm):
        pl.semaphore_signal(barrier, inc=1, device_id={"tm": lax.rem(me + i, n_tm)},
                            device_id_type=MESH)
    for i in range(1, n_chan):
        pl.semaphore_signal(barrier, inc=1, device_id={"chan": lax.rem(mc + i, n_chan)},
                            device_id_type=MESH)

    def a2a(peer, slot, src_dev):
        return pltpu.make_async_remote_copy(
            src_ref=blocks_ref.at[peer, slot],
            dst_ref=recv.at[src_dev, slot],
            send_sem=a2a_send_sem.at[peer, slot],
            recv_sem=a2a_recv_sem.at[src_dev, slot],
            device_id={"tm": peer},
            device_id_type=MESH,
        )

    def compute(g, slot):
        c1 = c1_ref[slot]
        c2 = c2_ref[slot]
        for dd in range(group):
            d = lax.rem(me + g * group + dd, n_tm)
            ar = ar_ref[slot, pl.ds(d, 1), :]
            ai = ai_ref[slot, pl.ds(d, 1), :]
            lhs[dd * rows:(dd + 1) * rows, :] = ar * c1 + ai * c2
        res = lax.dot_general(
            lhs[...].astype(jnp.bfloat16), x_ref[slot], (((1,), (1,)), ((), ())),
            preferred_element_type=jnp.float32,
        )
        for dd in range(group):
            d = lax.rem(me + g * group + dd, n_tm)
            blocks_ref[d, slot] = res[dd * rows:(dd + 1) * rows, :]

    def send(g, slot):
        for dd in range(group):
            if g == 0 and dd == 0:
                continue
            a2a(lax.rem(me + g * group + dd, n_tm), slot, me).start()

    for g in range(n_tm // group):
        compute(g, 0)
        if g == 0:
            pl.semaphore_wait(barrier, n_tm - 1 + n_chan - 1)
        send(g, 0)

        @pl.when(me_two)
        def _():
            compute(g, 1)
            send(g, 1)

    recv[me, 0] = blocks_ref[me, 0]

    @pl.when(me_two)
    def _():
        recv[me, 1] = blocks_ref[me, 1]

    for i in range(1, n_tm):
        peer = lax.rem(me + i, n_tm)
        a2a(peer, 0, me).wait_send()

        @pl.when(me_two)
        def _():
            a2a(peer, 1, me).wait_send()

    for s in range(n_tm):
        @pl.when(me != s)
        def _():
            a2a(s, 0, s).wait_recv()
            if count[s] == 2:
                a2a(s, 1, s).wait_recv()

    for w in range(NWIN):
        acc = None
        for s in range(n_tm):
            for j in range(count[s]):
                if first[s] + j == w:
                    part = recv[s, j]
                    acc = part if acc is None else acc + part
        spec[w] = acc

    rows = []
    for w in range(NWIN):
        re = spec[w, 0:bins_dev, :]
        im = spec[w, bins_dev:2 * bins_dev, :]
        mag = jnp.sqrt(re * re + im * im)
        rows.append(jnp.sum(mag, axis=0, keepdims=True))
    rows.append(jnp.zeros((8 - NWIN, rows[0].shape[1]), jnp.float32))
    lvl_send[...] = jnp.concatenate(rows, axis=0)

    def lvl(peer, src_dev):
        return pltpu.make_async_remote_copy(
            src_ref=lvl_send,
            dst_ref=lvl_recv.at[src_dev],
            send_sem=lvl_send_sem.at[peer],
            recv_sem=lvl_recv_sem.at[src_dev],
            device_id={"tm": peer},
            device_id_type=MESH,
        )

    for i in range(1, n_tm):
        lvl(lax.rem(me + i, n_tm), me).start()
    lvl_recv[me] = lvl_send[...]
    for i in range(1, n_tm):
        lvl(lax.rem(me + i, n_tm), me).wait_send()
    for i in range(1, n_tm):
        src = lax.rem(me + n_tm - i, n_tm)
        lvl(src, src).wait_recv()

    level = lvl_recv[0]
    for s in range(1, n_tm):
        level = level + lvl_recv[s]
    level = level / F

    mask = mask_ref[...]
    onehot = onehot_ref[...]
    for w in range(NWIN):
        re = spec[w, 0:bins_dev, :]
        im = spec[w, bins_dev:2 * bins_dev, :]
        mag = jnp.sqrt(re * re + im * im)
        den = mag + 0.1 * level[w:w + 1, :] + 1e-06
        for p, part in enumerate((re, im)):
            white = (part / den).astype(jnp.bfloat16).astype(jnp.float32) * mask
            white_ref[2 * w + p] = white
            src_send[2 * w + p] = jnp.dot(
                white.astype(jnp.bfloat16), onehot, preferred_element_type=jnp.float32
            )

    def srcc(peer, src_dev):
        return pltpu.make_async_remote_copy(
            src_ref=src_send,
            dst_ref=src_recv.at[src_dev],
            send_sem=src_send_sem.at[peer],
            recv_sem=src_recv_sem.at[src_dev],
            device_id={"chan": peer},
            device_id_type=MESH,
        )

    for i in range(1, n_chan):
        srcc(lax.rem(mc + i, n_chan), mc).start()
    src_recv[mc] = src_send[...]
    for i in range(1, n_chan):
        srcc(lax.rem(mc + i, n_chan), mc).wait_send()
    for i in range(1, n_chan):
        src = lax.rem(mc + n_chan - i, n_chan)
        srcc(src, src).wait_recv()

    total = src_recv[0]
    for s in range(1, n_chan):
        total = total + src_recv[s]
    srcspec_ref[...] = total


def fused_exchange(ar, ai, c1, c2, x, onehot, mask, n_tm, n_chan, bins_dev, first, count):
    channels, span = x.shape[1], x.shape[2]
    nsrc = onehot.shape[1]
    group = 8
    vmem = pl.BlockSpec(memory_space=pltpu.VMEM)
    return pl.pallas_call(
        functools.partial(_fused_kernel, n_tm, n_chan, bins_dev, first, count),
        out_shape=(
            jax.ShapeDtypeStruct((NWIN * 2, bins_dev, channels), jnp.float32),
            jax.ShapeDtypeStruct((NWIN * 2, bins_dev, nsrc), jnp.float32),
        ),
        in_specs=[vmem] * 7,
        out_specs=(vmem, vmem),
        scratch_shapes=[
            pltpu.VMEM((n_tm, SLOTS, 2 * bins_dev, channels), jnp.float32),
            pltpu.VMEM((group * 2 * bins_dev, span), jnp.float32),
            pltpu.VMEM((n_tm, SLOTS, 2 * bins_dev, channels), jnp.float32),
            pltpu.VMEM((NWIN, 2 * bins_dev, channels), jnp.float32),
            pltpu.VMEM((8, channels), jnp.float32),
            pltpu.VMEM((n_tm, 8, channels), jnp.float32),
            pltpu.VMEM((NWIN * 2, bins_dev, nsrc), jnp.float32),
            pltpu.VMEM((n_chan, NWIN * 2, bins_dev, nsrc), jnp.float32),
            pltpu.SemaphoreType.DMA((n_tm, SLOTS)),
            pltpu.SemaphoreType.DMA((n_tm, SLOTS)),
            pltpu.SemaphoreType.DMA((n_tm,)),
            pltpu.SemaphoreType.DMA((n_tm,)),
            pltpu.SemaphoreType.DMA((n_chan,)),
            pltpu.SemaphoreType.DMA((n_chan,)),
        ],
        compiler_params=pltpu.CompilerParams(collective_id=0, has_side_effects=True),
    )(ar, ai, c1, c2, x, onehot, mask)


def phasor(bins, times):
    phase = bins[:, None] * times[None, :] % W
    angle = phase.astype(jnp.float32) * (2.0 * math.pi / W)
    return jnp.cos(angle), -jnp.sin(angle)


def shards(record, offsets, dead_mask, sources):
    n_tm = lax.axis_size("tm")
    n_chan = lax.axis_size("chan")
    bins_dev = F // n_tm
    channels, span = record.shape
    first, count = window_plan(n_tm, span)
    me = lax.axis_index("tm")
    start = me * span
    local_times = start + jnp.arange(span, dtype=jnp.int32)
    wa = jnp.asarray(first, jnp.int32)[me]
    coarse = FLO + bins_dev * jnp.arange(n_tm, dtype=jnp.int32)
    fine = jnp.arange(bins_dev, dtype=jnp.int32)

    ars, ais, c1s, c2s, xs = [], [], [], [], []
    for slot in range(SLOTS):
        window = wa + slot
        origin = offsets[jnp.minimum(window, NWIN - 1)]
        shifted = local_times - origin
        inside = (shifted >= 0) & (shifted < W) & (window < NWIN)
        times = jnp.where(inside, shifted, 0)
        ar, ai = phasor(coarse, times)
        br, bi = phasor(fine, times)
        ars.append(ar)
        ais.append(ai)
        c1s.append(jnp.concatenate([br, bi], axis=0))
        c2s.append(jnp.concatenate([-bi, br], axis=0))
        xs.append(jnp.where(inside[None, :], record, jnp.zeros_like(record)))

    local_index = sources - lax.axis_index("chan") * channels
    onehot = (jnp.arange(channels, dtype=jnp.int32)[:, None] == local_index[None, :]).astype(
        jnp.bfloat16
    )
    mask = dead_mask.astype(jnp.float32)[None, :]
    white, source_spec = fused_exchange(
        jnp.stack(ars), jnp.stack(ais), jnp.stack(c1s), jnp.stack(c2s), jnp.stack(xs),
        onehot, mask, n_tm, n_chan, bins_dev, first, count
    )

    left = source_spec.astype(jnp.bfloat16).reshape(NWIN, 2, bins_dev, -1)
    right = white.astype(jnp.bfloat16).reshape(NWIN, 2, bins_dev, channels)
    right_imaginary = jnp.stack([right[:, 1], -right[:, 0]], axis=1)
    real_component = jnp.einsum(
        "wpks,wpkc->ksc", left, right, preferred_element_type=jnp.float32
    )
    imaginary_component = jnp.einsum(
        "wpks,wpkc->ksc", left, right_imaginary, preferred_element_type=jnp.float32
    )
    return jnp.stack([real_component, imaginary_component], axis=1) / NWIN


def solution(mesh):
    return jax.shard_map(
        shards,
        mesh=mesh,
        in_specs=(P("chan", "tm"), P(), P("chan"), P()),
        out_specs=P("tm", None, None, "chan"),
        check_vma=False,
    )
```

```python
import functools
import math

import jax
import jax.numpy as jnp
from jax import lax
from jax.experimental import pallas as pl
from jax.experimental.pallas import tpu as pltpu
from jax.sharding import PartitionSpec as P

W = 12000
F = 640
FLO = 6
NWIN = 4
SLOTS = 2
FA = 64

MESH = pl.DeviceIdType.MESH


def window_plan(n_tm, span):
    total = n_tm * span
    slack = total - NWIN * W
    lows = [0] + [w * W for w in range(1, NWIN - 1)] + [total - W]
    highs = [0] + [w * W + slack for w in range(1, NWIN - 1)] + [total - W]
    first, count = [], []
    for d in range(n_tm):
        meets = [w for w in range(NWIN) if lows[w] < (d + 1) * span and highs[w] + W > d * span]
        assert meets and meets == list(range(meets[0], meets[0] + len(meets)))
        assert len(meets) <= SLOTS
        first.append(meets[0])
        count.append(len(meets))
    return first, count


def _any_of(me, members):
    hit = jnp.bool_(False)
    for m in members:
        hit = hit | (me == m)
    return hit


def _fused_kernel(n_tm, n_chan, bins_dev, first, count,
                  ar_ref, ai_ref, c1_ref, c2_ref, x_ref, onehot_ref, mask_ref,
                  white_ref, srcspec_ref,
                  blocks_ref, lhs, recv, spec, lvl_send, lvl_recv, src_send, src_recv,
                  a2a_send_sem, a2a_recv_sem, lvl_send_sem, lvl_recv_sem,
                  src_send_sem, src_recv_sem):
    me = lax.axis_index("tm")
    mc = lax.axis_index("chan")
    two = [d for d in range(n_tm) if count[d] == 2]
    me_two = _any_of(me, two)
    rows = 2 * bins_dev
    group = lhs.shape[0] // rows

    barrier = pltpu.get_barrier_semaphore()
    for i in range(1, n_tm):
        pl.semaphore_signal(barrier, inc=1, device_id={"tm": lax.rem(me + i, n_tm)},
                            device_id_type=MESH)
    for i in range(1, n_chan):
        pl.semaphore_signal(barrier, inc=1, device_id={"chan": lax.rem(mc + i, n_chan)},
                            device_id_type=MESH)

    def a2a(peer, slot, src_dev):
        return pltpu.make_async_remote_copy(
            src_ref=blocks_ref.at[peer, slot],
            dst_ref=recv.at[src_dev, slot],
            send_sem=a2a_send_sem.at[peer, slot],
            recv_sem=a2a_recv_sem.at[src_dev, slot],
            device_id={"tm": peer},
            device_id_type=MESH,
        )

    def compute(g, slot):
        c1 = c1_ref[slot]
        c2 = c2_ref[slot]
        for dd in range(group):
            d = lax.rem(me + g * group + dd, n_tm)
            ar = ar_ref[slot, pl.ds(d, 1), :]
            ai = ai_ref[slot, pl.ds(d, 1), :]
            lhs[dd * rows:(dd + 1) * rows, :] = ar * c1 + ai * c2
        res = lax.dot_general(
            lhs[...].astype(jnp.bfloat16), x_ref[slot], (((1,), (1,)), ((), ())),
            preferred_element_type=jnp.float32,
        )
        for dd in range(group):
            d = lax.rem(me + g * group + dd, n_tm)
            blocks_ref[d, slot] = res[dd * rows:(dd + 1) * rows, :]

    def send(g, slot):
        for dd in range(group):
            if g == 0 and dd == 0:
                continue
            a2a(lax.rem(me + g * group + dd, n_tm), slot, me).start()

    for g in range(n_tm // group):
        compute(g, 0)
        if g == 0:
            pl.semaphore_wait(barrier, n_tm - 1 + n_chan - 1)
        send(g, 0)

        @pl.when(me_two)
        def _():
            compute(g, 1)
            send(g, 1)

    recv[me, 0] = blocks_ref[me, 0]

    @pl.when(me_two)
    def _():
        recv[me, 1] = blocks_ref[me, 1]

    for i in range(1, n_tm):
        peer = lax.rem(me + i, n_tm)
        a2a(peer, 0, me).wait_send()

        @pl.when(me_two)
        def _():
            a2a(peer, 1, me).wait_send()

    for s in range(n_tm):
        @pl.when(me != s)
        def _():
            a2a(s, 0, s).wait_recv()
            if count[s] == 2:
                a2a(s, 1, s).wait_recv()

    for w in range(NWIN):
        acc = None
        for s in range(n_tm):
            for j in range(count[s]):
                if first[s] + j == w:
                    part = recv[s, j]
                    acc = part if acc is None else acc + part
        spec[w] = acc

    rows = []
    for w in range(NWIN):
        re = spec[w, 0:bins_dev, :]
        im = spec[w, bins_dev:2 * bins_dev, :]
        mag = jnp.sqrt(re * re + im * im)
        rows.append(jnp.sum(mag, axis=0, keepdims=True))
    rows.append(jnp.zeros((8 - NWIN, rows[0].shape[1]), jnp.float32))
    lvl_send[...] = jnp.concatenate(rows, axis=0)

    def lvl(peer, src_dev):
        return pltpu.make_async_remote_copy(
            src_ref=lvl_send,
            dst_ref=lvl_recv.at[src_dev],
            send_sem=lvl_send_sem.at[peer],
            recv_sem=lvl_recv_sem.at[src_dev],
            device_id={"tm": peer},
            device_id_type=MESH,
        )

    for i in range(1, n_tm):
        lvl(lax.rem(me + i, n_tm), me).start()
    lvl_recv[me] = lvl_send[...]
    for i in range(1, n_tm):
        lvl(lax.rem(me + i, n_tm), me).wait_send()
    for i in range(1, n_tm):
        src = lax.rem(me + n_tm - i, n_tm)
        lvl(src, src).wait_recv()

    level = lvl_recv[0]
    for s in range(1, n_tm):
        level = level + lvl_recv[s]
    level = level / F

    mask = mask_ref[...]
    onehot = onehot_ref[...]
    for w in range(NWIN):
        re = spec[w, 0:bins_dev, :]
        im = spec[w, bins_dev:2 * bins_dev, :]
        mag = jnp.sqrt(re * re + im * im)
        den = mag + 0.1 * level[w:w + 1, :] + 1e-06
        for p, part in enumerate((re, im)):
            white = (part / den).astype(jnp.bfloat16).astype(jnp.float32) * mask
            white_ref[2 * w + p] = white
            src_send[2 * w + p] = jnp.dot(
                white.astype(jnp.bfloat16), onehot, preferred_element_type=jnp.float32
            ).astype(jnp.bfloat16)

    def srcc(peer, src_dev):
        return pltpu.make_async_remote_copy(
            src_ref=src_send,
            dst_ref=src_recv.at[src_dev],
            send_sem=src_send_sem.at[peer],
            recv_sem=src_recv_sem.at[src_dev],
            device_id={"chan": peer},
            device_id_type=MESH,
        )

    for i in range(1, n_chan):
        srcc(lax.rem(mc + i, n_chan), mc).start()
    src_recv[mc] = src_send[...]
    for i in range(1, n_chan):
        srcc(lax.rem(mc + i, n_chan), mc).wait_send()
    for i in range(1, n_chan):
        src = lax.rem(mc + n_chan - i, n_chan)
        srcc(src, src).wait_recv()

    total = src_recv[0].astype(jnp.float32)
    for s in range(1, n_chan):
        total = total + src_recv[s].astype(jnp.float32)
    srcspec_ref[...] = total


def fused_exchange(ar, ai, c1, c2, x, onehot, mask, n_tm, n_chan, bins_dev, first, count):
    channels, span = x.shape[1], x.shape[2]
    nsrc = onehot.shape[1]
    group = 8
    vmem = pl.BlockSpec(memory_space=pltpu.VMEM)
    return pl.pallas_call(
        functools.partial(_fused_kernel, n_tm, n_chan, bins_dev, first, count),
        out_shape=(
            jax.ShapeDtypeStruct((NWIN * 2, bins_dev, channels), jnp.float32),
            jax.ShapeDtypeStruct((NWIN * 2, bins_dev, nsrc), jnp.float32),
        ),
        in_specs=[vmem] * 7,
        out_specs=(vmem, vmem),
        scratch_shapes=[
            pltpu.VMEM((n_tm, SLOTS, 2 * bins_dev, channels), jnp.float32),
            pltpu.VMEM((group * 2 * bins_dev, span), jnp.float32),
            pltpu.VMEM((n_tm, SLOTS, 2 * bins_dev, channels), jnp.float32),
            pltpu.VMEM((NWIN, 2 * bins_dev, channels), jnp.float32),
            pltpu.VMEM((8, channels), jnp.float32),
            pltpu.VMEM((n_tm, 8, channels), jnp.float32),
            pltpu.VMEM((NWIN * 2, bins_dev, nsrc), jnp.bfloat16),
            pltpu.VMEM((n_chan, NWIN * 2, bins_dev, nsrc), jnp.bfloat16),
            pltpu.SemaphoreType.DMA((n_tm, SLOTS)),
            pltpu.SemaphoreType.DMA((n_tm, SLOTS)),
            pltpu.SemaphoreType.DMA((n_tm,)),
            pltpu.SemaphoreType.DMA((n_tm,)),
            pltpu.SemaphoreType.DMA((n_chan,)),
            pltpu.SemaphoreType.DMA((n_chan,)),
        ],
        compiler_params=pltpu.CompilerParams(collective_id=0, has_side_effects=True),
    )(ar, ai, c1, c2, x, onehot, mask)


def phasor(bins, times):
    phase = bins[:, None] * times[None, :] % W
    angle = phase.astype(jnp.float32) * (2.0 * math.pi / W)
    return jnp.cos(angle), -jnp.sin(angle)


def shards(record, offsets, dead_mask, sources):
    n_tm = lax.axis_size("tm")
    n_chan = lax.axis_size("chan")
    bins_dev = F // n_tm
    channels, span = record.shape
    first, count = window_plan(n_tm, span)
    me = lax.axis_index("tm")
    start = me * span
    local_times = start + jnp.arange(span, dtype=jnp.int32)
    wa = jnp.asarray(first, jnp.int32)[me]
    coarse = FLO + bins_dev * jnp.arange(n_tm, dtype=jnp.int32)
    fine = jnp.arange(bins_dev, dtype=jnp.int32)

    ars, ais, c1s, c2s, xs = [], [], [], [], []
    for slot in range(SLOTS):
        window = wa + slot
        origin = offsets[jnp.minimum(window, NWIN - 1)]
        shifted = local_times - origin
        inside = (shifted >= 0) & (shifted < W) & (window < NWIN)
        times = jnp.where(inside, shifted, 0)
        ar, ai = phasor(coarse, times)
        br, bi = phasor(fine, times)
        ars.append(ar)
        ais.append(ai)
        c1s.append(jnp.concatenate([br, bi], axis=0))
        c2s.append(jnp.concatenate([-bi, br], axis=0))
        xs.append(jnp.where(inside[None, :], record, jnp.zeros_like(record)))

    local_index = sources - lax.axis_index("chan") * channels
    onehot = (jnp.arange(channels, dtype=jnp.int32)[:, None] == local_index[None, :]).astype(
        jnp.bfloat16
    )
    mask = dead_mask.astype(jnp.float32)[None, :]
    white, source_spec = fused_exchange(
        jnp.stack(ars), jnp.stack(ais), jnp.stack(c1s), jnp.stack(c2s), jnp.stack(xs),
        onehot, mask, n_tm, n_chan, bins_dev, first, count
    )

    left = source_spec.astype(jnp.bfloat16).reshape(NWIN, 2, bins_dev, -1)
    right = white.astype(jnp.bfloat16).reshape(NWIN, 2, bins_dev, channels)
    right_imaginary = jnp.stack([right[:, 1], -right[:, 0]], axis=1)
    real_component = jnp.einsum(
        "wpks,wpkc->ksc", left, right, preferred_element_type=jnp.float32
    )
    imaginary_component = jnp.einsum(
        "wpks,wpkc->ksc", left, right_imaginary, preferred_element_type=jnp.float32
    )
    return jnp.stack([real_component, imaginary_component], axis=1) / NWIN


def solution(mesh):
    return jax.shard_map(
        shards,
        mesh=mesh,
        in_specs=(P("chan", "tm"), P(), P("chan"), P()),
        out_specs=P("tm", None, None, "chan"),
        check_vma=False,
    )
```

```python
import functools
import math

import jax
import jax.numpy as jnp
from jax import lax
from jax.experimental import pallas as pl
from jax.experimental.pallas import tpu as pltpu
from jax.sharding import PartitionSpec as P

W = 12000
F = 640
FLO = 6
NWIN = 4
SLOTS = 2
FA = 64

MESH = pl.DeviceIdType.MESH


def window_plan(n_tm, span):
    total = n_tm * span
    slack = total - NWIN * W
    lows = [0] + [w * W for w in range(1, NWIN - 1)] + [total - W]
    highs = [0] + [w * W + slack for w in range(1, NWIN - 1)] + [total - W]
    first, count = [], []
    for d in range(n_tm):
        meets = [w for w in range(NWIN) if lows[w] < (d + 1) * span and highs[w] + W > d * span]
        assert meets and meets == list(range(meets[0], meets[0] + len(meets)))
        assert len(meets) <= SLOTS
        first.append(meets[0])
        count.append(len(meets))
    return first, count


def _any_of(me, members):
    hit = jnp.bool_(False)
    for m in members:
        hit = hit | (me == m)
    return hit


def _fused_kernel(n_tm, n_chan, bins_dev, first, count,
                  offsets_ref, record_ref, dead_ref, sources_ref,
                  white_ref, srcspec_ref,
                  ar_ref, ai_ref, c1_ref, c2_ref, x_ref,
                  blocks_ref, lhs, recv, spec, lvl_send, lvl_recv, src_send, src_recv,
                  a2a_send_sem, a2a_recv_sem, lvl_send_sem, lvl_recv_sem,
                  src_send_sem, src_recv_sem):
    me = lax.axis_index("tm")
    mc = lax.axis_index("chan")
    two = [d for d in range(n_tm) if count[d] == 2]
    me_two = _any_of(me, two)
    rows = 2 * bins_dev
    group = lhs.shape[0] // rows

    barrier = pltpu.get_barrier_semaphore()
    for i in range(1, n_tm):
        pl.semaphore_signal(barrier, inc=1, device_id={"tm": lax.rem(me + i, n_tm)},
                            device_id_type=MESH)
    for i in range(1, n_chan):
        pl.semaphore_signal(barrier, inc=1, device_id={"chan": lax.rem(mc + i, n_chan)},
                            device_id_type=MESH)

    span = record_ref.shape[1]
    wa = jnp.int32(0)
    for d in range(n_tm):
        wa = jnp.where(me == d, first[d], wa)
    local_times = me * span + lax.broadcasted_iota(jnp.int32, (1, span), 1)
    coarse = FLO + bins_dev * lax.broadcasted_iota(jnp.int32, (n_tm, 1), 0)
    fine_row = lax.broadcasted_iota(jnp.int32, (2 * bins_dev, 1), 0)
    fine = lax.rem(fine_row, bins_dev)
    scale = 2.0 * math.pi / W

    def prepare(slot):
        window = wa + slot
        origin = offsets_ref[jnp.minimum(window, NWIN - 1)]
        shifted = local_times - origin
        inside = (shifted >= 0) & (shifted < W) & (window < NWIN)
        times = jnp.where(inside, shifted, 0)
        angle = lax.rem(coarse * times, W).astype(jnp.float32) * scale
        ar_ref[slot] = jnp.cos(angle)
        ai_ref[slot] = -jnp.sin(angle)
        angle = lax.rem(fine * times, W).astype(jnp.float32) * scale
        cos, sin = jnp.cos(angle), jnp.sin(angle)
        top = fine_row < bins_dev
        c1_ref[slot] = jnp.where(top, cos, -sin)
        c2_ref[slot] = jnp.where(top, sin, cos)
        x_ref[slot] = jnp.where(inside, record_ref[...], jnp.zeros_like(record_ref[...]))

    prepare(0)

    @pl.when(me_two)
    def _():
        prepare(1)

    def a2a(peer, slot, src_dev):
        return pltpu.make_async_remote_copy(
            src_ref=blocks_ref.at[peer, slot],
            dst_ref=recv.at[src_dev, slot],
            send_sem=a2a_send_sem.at[peer, slot],
            recv_sem=a2a_recv_sem.at[src_dev, slot],
            device_id={"tm": peer},
            device_id_type=MESH,
        )

    def compute(g, slot):
        c1 = c1_ref[slot]
        c2 = c2_ref[slot]
        for dd in range(group):
            d = lax.rem(me + g * group + dd, n_tm)
            ar = ar_ref[slot, pl.ds(d, 1), :]
            ai = ai_ref[slot, pl.ds(d, 1), :]
            lhs[dd * rows:(dd + 1) * rows, :] = ar * c1 + ai * c2
        res = lax.dot_general(
            lhs[...].astype(jnp.bfloat16), x_ref[slot], (((1,), (1,)), ((), ())),
            preferred_element_type=jnp.float32,
        )
        for dd in range(group):
            d = lax.rem(me + g * group + dd, n_tm)
            blocks_ref[d, slot] = res[dd * rows:(dd + 1) * rows, :]

    def send(g, slot):
        for dd in range(group):
            if g == 0 and dd == 0:
                continue
            a2a(lax.rem(me + g * group + dd, n_tm), slot, me).start()

    for g in range(n_tm // group):
        compute(g, 0)
        if g == 0:
            pl.semaphore_wait(barrier, n_tm - 1 + n_chan - 1)
        send(g, 0)

        @pl.when(me_two)
        def _():
            compute(g, 1)
            send(g, 1)

    recv[me, 0] = blocks_ref[me, 0]

    @pl.when(me_two)
    def _():
        recv[me, 1] = blocks_ref[me, 1]

    for i in range(1, n_tm):
        peer = lax.rem(me + i, n_tm)
        a2a(peer, 0, me).wait_send()

        @pl.when(me_two)
        def _():
            a2a(peer, 1, me).wait_send()

    for s in range(n_tm):
        @pl.when(me != s)
        def _():
            a2a(s, 0, s).wait_recv()
            if count[s] == 2:
                a2a(s, 1, s).wait_recv()

    for w in range(NWIN):
        acc = None
        for s in range(n_tm):
            for j in range(count[s]):
                if first[s] + j == w:
                    part = recv[s, j]
                    acc = part if acc is None else acc + part
        spec[w] = acc

    rows = []
    for w in range(NWIN):
        re = spec[w, 0:bins_dev, :]
        im = spec[w, bins_dev:2 * bins_dev, :]
        mag = jnp.sqrt(re * re + im * im)
        rows.append(jnp.sum(mag, axis=0, keepdims=True))
    rows.append(jnp.zeros((8 - NWIN, rows[0].shape[1]), jnp.float32))
    lvl_send[...] = jnp.concatenate(rows, axis=0)

    def lvl(peer, src_dev):
        return pltpu.make_async_remote_copy(
            src_ref=lvl_send,
            dst_ref=lvl_recv.at[src_dev],
            send_sem=lvl_send_sem.at[peer],
            recv_sem=lvl_recv_sem.at[src_dev],
            device_id={"tm": peer},
            device_id_type=MESH,
        )

    for i in range(1, n_tm):
        lvl(lax.rem(me + i, n_tm), me).start()
    lvl_recv[me] = lvl_send[...]
    for i in range(1, n_tm):
        lvl(lax.rem(me + i, n_tm), me).wait_send()
    for i in range(1, n_tm):
        src = lax.rem(me + n_tm - i, n_tm)
        lvl(src, src).wait_recv()

    level = lvl_recv[0]
    for s in range(1, n_tm):
        level = level + lvl_recv[s]
    level = level / F

    mask = dead_ref[...].astype(jnp.float32)
    channels = record_ref.shape[0]
    local_index = sources_ref[...] - mc * channels
    onehot = (lax.broadcasted_iota(jnp.int32, (channels, local_index.shape[1]), 0)
              == local_index).astype(jnp.bfloat16)
    for w in range(NWIN):
        re = spec[w, 0:bins_dev, :]
        im = spec[w, bins_dev:2 * bins_dev, :]
        mag = jnp.sqrt(re * re + im * im)
        den = mag + 0.1 * level[w:w + 1, :] + 1e-06
        for p, part in enumerate((re, im)):
            white = (part / den).astype(jnp.bfloat16).astype(jnp.float32) * mask
            white_ref[2 * w + p] = white
            src_send[2 * w + p] = jnp.dot(
                white.astype(jnp.bfloat16), onehot, preferred_element_type=jnp.float32
            ).astype(jnp.bfloat16)

    def srcc(peer, src_dev):
        return pltpu.make_async_remote_copy(
            src_ref=src_send,
            dst_ref=src_recv.at[src_dev],
            send_sem=src_send_sem.at[peer],
            recv_sem=src_recv_sem.at[src_dev],
            device_id={"chan": peer},
            device_id_type=MESH,
        )

    for i in range(1, n_chan):
        srcc(lax.rem(mc + i, n_chan), mc).start()
    src_recv[mc] = src_send[...]
    for i in range(1, n_chan):
        srcc(lax.rem(mc + i, n_chan), mc).wait_send()
    for i in range(1, n_chan):
        src = lax.rem(mc + n_chan - i, n_chan)
        srcc(src, src).wait_recv()

    total = src_recv[0].astype(jnp.float32)
    for s in range(1, n_chan):
        total = total + src_recv[s].astype(jnp.float32)
    srcspec_ref[...] = total


def fused_exchange(offsets, record, dead, sources, n_tm, n_chan, bins_dev, first, count):
    channels, span = record.shape
    nsrc = sources.shape[1]
    group = 8
    vmem = pl.BlockSpec(memory_space=pltpu.VMEM)
    return pl.pallas_call(
        functools.partial(_fused_kernel, n_tm, n_chan, bins_dev, first, count),
        out_shape=(
            jax.ShapeDtypeStruct((NWIN * 2, bins_dev, channels), jnp.float32),
            jax.ShapeDtypeStruct((NWIN * 2, bins_dev, nsrc), jnp.float32),
        ),
        in_specs=[pl.BlockSpec(memory_space=pltpu.SMEM), vmem, vmem, vmem],
        out_specs=(vmem, vmem),
        scratch_shapes=[
            pltpu.VMEM((SLOTS, n_tm, span), jnp.float32),
            pltpu.VMEM((SLOTS, n_tm, span), jnp.float32),
            pltpu.VMEM((SLOTS, 2 * bins_dev, span), jnp.float32),
            pltpu.VMEM((SLOTS, 2 * bins_dev, span), jnp.float32),
            pltpu.VMEM((SLOTS, channels, span), jnp.bfloat16),
            pltpu.VMEM((n_tm, SLOTS, 2 * bins_dev, channels), jnp.float32),
            pltpu.VMEM((group * 2 * bins_dev, span), jnp.float32),
            pltpu.VMEM((n_tm, SLOTS, 2 * bins_dev, channels), jnp.float32),
            pltpu.VMEM((NWIN, 2 * bins_dev, channels), jnp.float32),
            pltpu.VMEM((8, channels), jnp.float32),
            pltpu.VMEM((n_tm, 8, channels), jnp.float32),
            pltpu.VMEM((NWIN * 2, bins_dev, nsrc), jnp.bfloat16),
            pltpu.VMEM((n_chan, NWIN * 2, bins_dev, nsrc), jnp.bfloat16),
            pltpu.SemaphoreType.DMA((n_tm, SLOTS)),
            pltpu.SemaphoreType.DMA((n_tm, SLOTS)),
            pltpu.SemaphoreType.DMA((n_tm,)),
            pltpu.SemaphoreType.DMA((n_tm,)),
            pltpu.SemaphoreType.DMA((n_chan,)),
            pltpu.SemaphoreType.DMA((n_chan,)),
        ],
        compiler_params=pltpu.CompilerParams(collective_id=0, has_side_effects=True),
    )(offsets, record, dead, sources)


def shards(record, offsets, dead_mask, sources):
    n_tm = lax.axis_size("tm")
    n_chan = lax.axis_size("chan")
    bins_dev = F // n_tm
    channels, span = record.shape
    first, count = window_plan(n_tm, span)
    white, source_spec = fused_exchange(
        offsets, record, dead_mask.reshape(1, channels), sources.reshape(1, -1),
        n_tm, n_chan, bins_dev, first, count
    )

    left = source_spec.astype(jnp.bfloat16).reshape(NWIN, 2, bins_dev, -1)
    right = white.astype(jnp.bfloat16).reshape(NWIN, 2, bins_dev, channels)
    right_imaginary = jnp.stack([right[:, 1], -right[:, 0]], axis=1)
    real_component = jnp.einsum(
        "wpks,wpkc->ksc", left, right, preferred_element_type=jnp.float32
    )
    imaginary_component = jnp.einsum(
        "wpks,wpkc->ksc", left, right_imaginary, preferred_element_type=jnp.float32
    )
    return jnp.stack([real_component, imaginary_component], axis=1) / NWIN


def solution(mesh):
    return jax.shard_map(
        shards,
        mesh=mesh,
        in_specs=(P("chan", "tm"), P(), P("chan"), P()),
        out_specs=P("tm", None, None, "chan"),
        check_vma=False,
    )
```

```python
import functools
import math

import jax
import jax.numpy as jnp
from jax import lax
from jax.experimental import pallas as pl
from jax.experimental.pallas import tpu as pltpu
from jax.sharding import PartitionSpec as P

W = 12000
F = 640
FLO = 6
NWIN = 4
SLOTS = 2
FA = 64

MESH = pl.DeviceIdType.MESH


def window_plan(n_tm, span):
    total = n_tm * span
    slack = total - NWIN * W
    lows = [0] + [w * W for w in range(1, NWIN - 1)] + [total - W]
    highs = [0] + [w * W + slack for w in range(1, NWIN - 1)] + [total - W]
    first, count = [], []
    for d in range(n_tm):
        meets = [w for w in range(NWIN) if lows[w] < (d + 1) * span and highs[w] + W > d * span]
        assert meets and meets == list(range(meets[0], meets[0] + len(meets)))
        assert len(meets) <= SLOTS
        first.append(meets[0])
        count.append(len(meets))
    return first, count


def _any_of(me, members):
    hit = jnp.bool_(False)
    for m in members:
        hit = hit | (me == m)
    return hit


def _fused_kernel(n_tm, n_chan, bins_dev, first, count,
                  offsets_ref, record_ref, dead_ref, sources_ref,
                  white_ref, srcspec_ref,
                  ar_ref, ai_ref, c1_ref, c2_ref, x_ref,
                  blocks_ref, lhs, recv, spec, lvl_send, lvl_recv, src_send,
                  a2a_send_sem, a2a_recv_sem, lvl_send_sem, lvl_recv_sem,
                  src_send_sem, src_recv_sem, rs_recv, ag_send, ag_send_sem, ag_recv_sem):
    me = lax.axis_index("tm")
    mc = lax.axis_index("chan")
    two = [d for d in range(n_tm) if count[d] == 2]
    me_two = _any_of(me, two)
    rows = 2 * bins_dev
    group = lhs.shape[0] // rows

    barrier = pltpu.get_barrier_semaphore()
    for i in range(1, n_tm):
        pl.semaphore_signal(barrier, inc=1, device_id={"tm": lax.rem(me + i, n_tm)},
                            device_id_type=MESH)
    for i in range(1, n_chan):
        pl.semaphore_signal(barrier, inc=1, device_id={"chan": lax.rem(mc + i, n_chan)},
                            device_id_type=MESH)

    span = record_ref.shape[1]
    wa = jnp.int32(0)
    for d in range(n_tm):
        wa = jnp.where(me == d, first[d], wa)
    local_times = me * span + lax.broadcasted_iota(jnp.int32, (1, span), 1)
    coarse = FLO + bins_dev * lax.broadcasted_iota(jnp.int32, (n_tm, 1), 0)
    fine_row = lax.broadcasted_iota(jnp.int32, (2 * bins_dev, 1), 0)
    fine = lax.rem(fine_row, bins_dev)
    scale = 2.0 * math.pi / W

    def prepare(slot):
        window = wa + slot
        origin = offsets_ref[jnp.minimum(window, NWIN - 1)]
        shifted = local_times - origin
        inside = (shifted >= 0) & (shifted < W) & (window < NWIN)
        times = jnp.where(inside, shifted, 0)
        angle = lax.rem(coarse * times, W).astype(jnp.float32) * scale
        ar_ref[slot] = jnp.cos(angle)
        ai_ref[slot] = -jnp.sin(angle)
        angle = lax.rem(fine * times, W).astype(jnp.float32) * scale
        cos, sin = jnp.cos(angle), jnp.sin(angle)
        top = fine_row < bins_dev
        c1_ref[slot] = jnp.where(top, cos, -sin)
        c2_ref[slot] = jnp.where(top, sin, cos)
        x_ref[slot] = jnp.where(inside, record_ref[...], jnp.zeros_like(record_ref[...]))

    prepare(0)

    @pl.when(me_two)
    def _():
        prepare(1)

    def a2a(peer, slot, src_dev):
        return pltpu.make_async_remote_copy(
            src_ref=blocks_ref.at[peer, slot],
            dst_ref=recv.at[src_dev, slot],
            send_sem=a2a_send_sem.at[peer, slot],
            recv_sem=a2a_recv_sem.at[src_dev, slot],
            device_id={"tm": peer},
            device_id_type=MESH,
        )

    def compute(g, slot):
        c1 = c1_ref[slot]
        c2 = c2_ref[slot]
        for dd in range(group):
            d = lax.rem(me + g * group + dd, n_tm)
            ar = ar_ref[slot, pl.ds(d, 1), :]
            ai = ai_ref[slot, pl.ds(d, 1), :]
            lhs[dd * rows:(dd + 1) * rows, :] = ar * c1 + ai * c2
        res = lax.dot_general(
            lhs[...].astype(jnp.bfloat16), x_ref[slot], (((1,), (1,)), ((), ())),
            preferred_element_type=jnp.float32,
        )
        for dd in range(group):
            d = lax.rem(me + g * group + dd, n_tm)
            blocks_ref[d, slot] = res[dd * rows:(dd + 1) * rows, :]

    def send(g, slot):
        for dd in range(group):
            if g == 0 and dd == 0:
                continue
            a2a(lax.rem(me + g * group + dd, n_tm), slot, me).start()

    for g in range(n_tm // group):
        compute(g, 0)
        if g == 0:
            pl.semaphore_wait(barrier, n_tm - 1 + n_chan - 1)
        send(g, 0)

        @pl.when(me_two)
        def _():
            compute(g, 1)
            send(g, 1)

    recv[me, 0] = blocks_ref[me, 0]

    @pl.when(me_two)
    def _():
        recv[me, 1] = blocks_ref[me, 1]

    for i in range(1, n_tm):
        peer = lax.rem(me + i, n_tm)
        a2a(peer, 0, me).wait_send()

        @pl.when(me_two)
        def _():
            a2a(peer, 1, me).wait_send()

    for s in range(n_tm):
        @pl.when(me != s)
        def _():
            a2a(s, 0, s).wait_recv()
            if count[s] == 2:
                a2a(s, 1, s).wait_recv()

    for w in range(NWIN):
        acc = None
        for s in range(n_tm):
            for j in range(count[s]):
                if first[s] + j == w:
                    part = recv[s, j]
                    acc = part if acc is None else acc + part
        spec[w] = acc

    rows = []
    for w in range(NWIN):
        re = spec[w, 0:bins_dev, :]
        im = spec[w, bins_dev:2 * bins_dev, :]
        mag = jnp.sqrt(re * re + im * im)
        rows.append(jnp.sum(mag, axis=0, keepdims=True))
    rows.append(jnp.zeros((8 - NWIN, rows[0].shape[1]), jnp.float32))
    lvl_send[...] = jnp.concatenate(rows, axis=0)

    def lvl(peer, src_dev):
        return pltpu.make_async_remote_copy(
            src_ref=lvl_send,
            dst_ref=lvl_recv.at[src_dev],
            send_sem=lvl_send_sem.at[peer],
            recv_sem=lvl_recv_sem.at[src_dev],
            device_id={"tm": peer},
            device_id_type=MESH,
        )

    for i in range(1, n_tm):
        lvl(lax.rem(me + i, n_tm), me).start()
    lvl_recv[me] = lvl_send[...]
    for i in range(1, n_tm):
        lvl(lax.rem(me + i, n_tm), me).wait_send()
    for i in range(1, n_tm):
        src = lax.rem(me + n_tm - i, n_tm)
        lvl(src, src).wait_recv()

    level = lvl_recv[0]
    for s in range(1, n_tm):
        level = level + lvl_recv[s]
    level = level / F

    mask = dead_ref[...].astype(jnp.float32)
    channels = record_ref.shape[0]
    local_index = sources_ref[...] - mc * channels
    onehot = (lax.broadcasted_iota(jnp.int32, (channels, local_index.shape[1]), 0)
              == local_index).astype(jnp.bfloat16)
    per = NWIN * 2 * bins_dev // n_chan
    halves = bins_dev // per
    src_send[...] = jnp.zeros_like(src_send)
    for w in range(NWIN):
        re = spec[w, 0:bins_dev, :]
        im = spec[w, bins_dev:2 * bins_dev, :]
        mag = jnp.sqrt(re * re + im * im)
        den = mag + 0.1 * level[w:w + 1, :] + 1e-06
        for p, part in enumerate((re, im)):
            white = (part / den).astype(jnp.bfloat16).astype(jnp.float32) * mask
            white_ref[2 * w + p] = white
            picked = jnp.dot(
                white.astype(jnp.bfloat16), onehot, preferred_element_type=jnp.float32
            )
            for h in range(halves):
                src_send[(2 * w + p) * halves + h, 0:per, :] = picked[h * per:(h + 1) * per, :]

    def rsc(peer, src_dev):
        return pltpu.make_async_remote_copy(
            src_ref=src_send.at[peer],
            dst_ref=rs_recv.at[src_dev],
            send_sem=src_send_sem.at[peer],
            recv_sem=src_recv_sem.at[src_dev],
            device_id={"chan": peer},
            device_id_type=MESH,
        )

    for i in range(1, n_chan):
        rsc(lax.rem(mc + i, n_chan), mc).start()
    rs_recv[mc] = src_send[mc]
    for i in range(1, n_chan):
        rsc(lax.rem(mc + i, n_chan), mc).wait_send()
    for i in range(1, n_chan):
        src = lax.rem(mc + n_chan - i, n_chan)
        rsc(src, src).wait_recv()

    total = rs_recv[0]
    for s in range(1, n_chan):
        total = total + rs_recv[s]
    ag_send[...] = total

    def agc(peer, src_dev):
        return pltpu.make_async_remote_copy(
            src_ref=ag_send,
            dst_ref=srcspec_ref.at[src_dev],
            send_sem=ag_send_sem.at[peer],
            recv_sem=ag_recv_sem.at[src_dev],
            device_id={"chan": peer},
            device_id_type=MESH,
        )

    for i in range(1, n_chan):
        agc(lax.rem(mc + i, n_chan), mc).start()
    srcspec_ref[mc] = ag_send[...]
    for i in range(1, n_chan):
        agc(lax.rem(mc + i, n_chan), mc).wait_send()
    for i in range(1, n_chan):
        src = lax.rem(mc + n_chan - i, n_chan)
        agc(src, src).wait_recv()


def fused_exchange(offsets, record, dead, sources, n_tm, n_chan, bins_dev, first, count):
    channels, span = record.shape
    nsrc = sources.shape[1]
    group = 8
    vmem = pl.BlockSpec(memory_space=pltpu.VMEM)
    return pl.pallas_call(
        functools.partial(_fused_kernel, n_tm, n_chan, bins_dev, first, count),
        out_shape=(
            jax.ShapeDtypeStruct((NWIN * 2, bins_dev, channels), jnp.float32),
            jax.ShapeDtypeStruct((n_chan, 16, nsrc), jnp.float32),
        ),
        in_specs=[pl.BlockSpec(memory_space=pltpu.SMEM), vmem, vmem, vmem],
        out_specs=(vmem, vmem),
        scratch_shapes=[
            pltpu.VMEM((SLOTS, n_tm, span), jnp.float32),
            pltpu.VMEM((SLOTS, n_tm, span), jnp.float32),
            pltpu.VMEM((SLOTS, 2 * bins_dev, span), jnp.float32),
            pltpu.VMEM((SLOTS, 2 * bins_dev, span), jnp.float32),
            pltpu.VMEM((SLOTS, channels, span), jnp.bfloat16),
            pltpu.VMEM((n_tm, SLOTS, 2 * bins_dev, channels), jnp.float32),
            pltpu.VMEM((group * 2 * bins_dev, span), jnp.float32),
            pltpu.VMEM((n_tm, SLOTS, 2 * bins_dev, channels), jnp.float32),
            pltpu.VMEM((NWIN, 2 * bins_dev, channels), jnp.float32),
            pltpu.VMEM((8, channels), jnp.float32),
            pltpu.VMEM((n_tm, 8, channels), jnp.float32),
            pltpu.VMEM((n_chan, 16, nsrc), jnp.float32),
            pltpu.SemaphoreType.DMA((n_tm, SLOTS)),
            pltpu.SemaphoreType.DMA((n_tm, SLOTS)),
            pltpu.SemaphoreType.DMA((n_tm,)),
            pltpu.SemaphoreType.DMA((n_tm,)),
            pltpu.SemaphoreType.DMA((n_chan,)),
            pltpu.SemaphoreType.DMA((n_chan,)),
            pltpu.VMEM((n_chan, 16, nsrc), jnp.float32),
            pltpu.VMEM((16, nsrc), jnp.float32),
            pltpu.SemaphoreType.DMA((n_chan,)),
            pltpu.SemaphoreType.DMA((n_chan,)),
        ],
        compiler_params=pltpu.CompilerParams(collective_id=0, has_side_effects=True),
    )(offsets, record, dead, sources)


def shards(record, offsets, dead_mask, sources):
    n_tm = lax.axis_size("tm")
    n_chan = lax.axis_size("chan")
    bins_dev = F // n_tm
    channels, span = record.shape
    first, count = window_plan(n_tm, span)
    white, source_spec = fused_exchange(
        offsets, record, dead_mask.reshape(1, channels), sources.reshape(1, -1),
        n_tm, n_chan, bins_dev, first, count
    )

    per = NWIN * 2 * bins_dev // n_chan
    assert per * n_chan == NWIN * 2 * bins_dev and bins_dev % per == 0 and per <= 16
    left = source_spec[:, :per].astype(jnp.bfloat16).reshape(NWIN, 2, bins_dev, -1)
    right = white.astype(jnp.bfloat16).reshape(NWIN, 2, bins_dev, channels)
    right_imaginary = jnp.stack([right[:, 1], -right[:, 0]], axis=1)
    real_component = jnp.einsum(
        "wpks,wpkc->ksc", left, right, preferred_element_type=jnp.float32
    )
    imaginary_component = jnp.einsum(
        "wpks,wpkc->ksc", left, right_imaginary, preferred_element_type=jnp.float32
    )
    return jnp.stack([real_component, imaginary_component], axis=1) / NWIN


def solution(mesh):
    return jax.shard_map(
        shards,
        mesh=mesh,
        in_specs=(P("chan", "tm"), P(), P("chan"), P()),
        out_specs=P("tm", None, None, "chan"),
        check_vma=False,
    )
```

```python
import functools
import math

import jax
import jax.numpy as jnp
from jax import lax
from jax.experimental import pallas as pl
from jax.experimental.pallas import tpu as pltpu
from jax.sharding import PartitionSpec as P

W = 12000
F = 640
FLO = 6
NWIN = 4
SLOTS = 2
FA = 64

MESH = pl.DeviceIdType.MESH


def window_plan(n_tm, span):
    total = n_tm * span
    slack = total - NWIN * W
    lows = [0] + [w * W for w in range(1, NWIN - 1)] + [total - W]
    highs = [0] + [w * W + slack for w in range(1, NWIN - 1)] + [total - W]
    first, count = [], []
    for d in range(n_tm):
        meets = [w for w in range(NWIN) if lows[w] < (d + 1) * span and highs[w] + W > d * span]
        assert meets and meets == list(range(meets[0], meets[0] + len(meets)))
        assert len(meets) <= SLOTS
        first.append(meets[0])
        count.append(len(meets))
    return first, count


def _ring_order(n):
    order = [0]
    for i in range(1, n):
        order.append((i + 1) // 2 if i % 2 else n - i // 2)
    assert sorted(order) == list(range(n))
    return order


def _any_of(me, members):
    hit = jnp.bool_(False)
    for m in members:
        hit = hit | (me == m)
    return hit


def _fused_kernel(n_tm, n_chan, bins_dev, first, count,
                  offsets_ref, record_ref, dead_ref, sources_ref,
                  white_ref, srcspec_ref,
                  ar_ref, ai_ref, c1_ref, c2_ref, x_ref,
                  blocks_ref, lhs, recv, spec, lvl_send, lvl_recv, src_send,
                  a2a_send_sem, a2a_recv_sem, lvl_send_sem, lvl_recv_sem,
                  src_send_sem, src_recv_sem, rs_recv, ag_send, ag_send_sem, ag_recv_sem):
    me = lax.axis_index("tm")
    mc = lax.axis_index("chan")
    two = [d for d in range(n_tm) if count[d] == 2]
    me_two = _any_of(me, two)
    rows = 2 * bins_dev
    group = lhs.shape[0] // rows

    order = _ring_order(n_tm)
    corder = _ring_order(n_chan)
    barrier = pltpu.get_barrier_semaphore()
    for i in range(1, n_tm):
        pl.semaphore_signal(barrier, inc=1, device_id={"tm": lax.rem(me + order[i], n_tm)},
                            device_id_type=MESH)
    for i in range(1, n_chan):
        pl.semaphore_signal(barrier, inc=1, device_id={"chan": lax.rem(mc + corder[i], n_chan)},
                            device_id_type=MESH)

    span = record_ref.shape[1]
    wa = jnp.int32(0)
    for d in range(n_tm):
        wa = jnp.where(me == d, first[d], wa)
    local_times = me * span + lax.broadcasted_iota(jnp.int32, (1, span), 1)
    coarse = FLO + bins_dev * lax.broadcasted_iota(jnp.int32, (n_tm, 1), 0)
    fine_row = lax.broadcasted_iota(jnp.int32, (2 * bins_dev, 1), 0)
    fine = lax.rem(fine_row, bins_dev)
    scale = 2.0 * math.pi / W

    def prepare(slot):
        window = wa + slot
        origin = offsets_ref[jnp.minimum(window, NWIN - 1)]
        shifted = local_times - origin
        inside = (shifted >= 0) & (shifted < W) & (window < NWIN)
        times = jnp.where(inside, shifted, 0)
        angle = lax.rem(coarse * times, W).astype(jnp.float32) * scale
        ar_ref[slot] = jnp.cos(angle)
        ai_ref[slot] = -jnp.sin(angle)
        angle = lax.rem(fine * times, W).astype(jnp.float32) * scale
        cos, sin = jnp.cos(angle), jnp.sin(angle)
        top = fine_row < bins_dev
        c1_ref[slot] = jnp.where(top, cos, -sin)
        c2_ref[slot] = jnp.where(top, sin, cos)
        x_ref[slot] = jnp.where(inside, record_ref[...], jnp.zeros_like(record_ref[...]))

    prepare(0)

    @pl.when(me_two)
    def _():
        prepare(1)

    def a2a(peer, slot, src_dev):
        return pltpu.make_async_remote_copy(
            src_ref=blocks_ref.at[peer, slot],
            dst_ref=recv.at[src_dev, slot],
            send_sem=a2a_send_sem.at[peer, slot],
            recv_sem=a2a_recv_sem.at[src_dev, slot],
            device_id={"tm": peer},
            device_id_type=MESH,
        )

    def compute(g, slot):
        c1 = c1_ref[slot]
        c2 = c2_ref[slot]
        for dd in range(group):
            d = lax.rem(me + order[g * group + dd], n_tm)
            ar = ar_ref[slot, pl.ds(d, 1), :]
            ai = ai_ref[slot, pl.ds(d, 1), :]
            lhs[dd * rows:(dd + 1) * rows, :] = ar * c1 + ai * c2
        res = lax.dot_general(
            lhs[...].astype(jnp.bfloat16), x_ref[slot], (((1,), (1,)), ((), ())),
            preferred_element_type=jnp.float32,
        )
        for dd in range(group):
            d = lax.rem(me + order[g * group + dd], n_tm)
            blocks_ref[d, slot] = res[dd * rows:(dd + 1) * rows, :]

    def send(g, slot):
        for dd in range(group):
            if g == 0 and dd == 0:
                continue
            a2a(lax.rem(me + order[g * group + dd], n_tm), slot, me).start()

    for g in range(n_tm // group):
        compute(g, 0)

        @pl.when(me_two)
        def _():
            compute(g, 1)

    pl.semaphore_wait(barrier, n_tm - 1 + n_chan - 1)
    for g in range(n_tm // group):
        send(g, 0)

        @pl.when(me_two)
        def _():
            send(g, 1)

    recv[me, 0] = blocks_ref[me, 0]

    @pl.when(me_two)
    def _():
        recv[me, 1] = blocks_ref[me, 1]

    for i in range(1, n_tm):
        peer = lax.rem(me + order[i], n_tm)
        a2a(peer, 0, me).wait_send()

        @pl.when(me_two)
        def _():
            a2a(peer, 1, me).wait_send()

    for s in range(n_tm):
        @pl.when(me != s)
        def _():
            a2a(s, 0, s).wait_recv()
            if count[s] == 2:
                a2a(s, 1, s).wait_recv()

    for w in range(NWIN):
        acc = None
        for s in range(n_tm):
            for j in range(count[s]):
                if first[s] + j == w:
                    part = recv[s, j]
                    acc = part if acc is None else acc + part
        spec[w] = acc

    rows = []
    for w in range(NWIN):
        re = spec[w, 0:bins_dev, :]
        im = spec[w, bins_dev:2 * bins_dev, :]
        mag = jnp.sqrt(re * re + im * im)
        rows.append(jnp.sum(mag, axis=0, keepdims=True))
    rows.append(jnp.zeros((8 - NWIN, rows[0].shape[1]), jnp.float32))
    lvl_send[...] = jnp.concatenate(rows, axis=0)

    def lvl(peer, src_dev):
        return pltpu.make_async_remote_copy(
            src_ref=lvl_send,
            dst_ref=lvl_recv.at[src_dev],
            send_sem=lvl_send_sem.at[peer],
            recv_sem=lvl_recv_sem.at[src_dev],
            device_id={"tm": peer},
            device_id_type=MESH,
        )

    for i in range(1, n_tm):
        lvl(lax.rem(me + order[i], n_tm), me).start()
    lvl_recv[me] = lvl_send[...]
    for i in range(1, n_tm):
        lvl(lax.rem(me + order[i], n_tm), me).wait_send()
    for i in range(1, n_tm):
        src = lax.rem(me + n_tm - i, n_tm)
        lvl(src, src).wait_recv()

    level = lvl_recv[0]
    for s in range(1, n_tm):
        level = level + lvl_recv[s]
    level = level / F

    mask = dead_ref[...].astype(jnp.float32)
    channels = record_ref.shape[0]
    local_index = sources_ref[...] - mc * channels
    onehot = (lax.broadcasted_iota(jnp.int32, (channels, local_index.shape[1]), 0)
              == local_index).astype(jnp.bfloat16)
    per = NWIN * 2 * bins_dev // n_chan
    halves = bins_dev // per
    src_send[...] = jnp.zeros_like(src_send)
    for w in range(NWIN):
        re = spec[w, 0:bins_dev, :]
        im = spec[w, bins_dev:2 * bins_dev, :]
        mag = jnp.sqrt(re * re + im * im)
        den = mag + 0.1 * level[w:w + 1, :] + 1e-06
        for p, part in enumerate((re, im)):
            white = (part / den).astype(jnp.bfloat16).astype(jnp.float32) * mask
            white_ref[2 * w + p] = white
            picked = jnp.dot(
                white.astype(jnp.bfloat16), onehot, preferred_element_type=jnp.float32
            )
            for h in range(halves):
                src_send[(2 * w + p) * halves + h, 0:per, :] = picked[h * per:(h + 1) * per, :]

    def rsc(peer, src_dev):
        return pltpu.make_async_remote_copy(
            src_ref=src_send.at[peer],
            dst_ref=rs_recv.at[src_dev],
            send_sem=src_send_sem.at[peer],
            recv_sem=src_recv_sem.at[src_dev],
            device_id={"chan": peer},
            device_id_type=MESH,
        )

    for i in range(1, n_chan):
        rsc(lax.rem(mc + corder[i], n_chan), mc).start()
    rs_recv[mc] = src_send[mc]
    for i in range(1, n_chan):
        rsc(lax.rem(mc + corder[i], n_chan), mc).wait_send()
    for i in range(1, n_chan):
        src = lax.rem(mc + n_chan - i, n_chan)
        rsc(src, src).wait_recv()

    total = rs_recv[0]
    for s in range(1, n_chan):
        total = total + rs_recv[s]
    ag_send[...] = total

    def agc(peer, src_dev):
        return pltpu.make_async_remote_copy(
            src_ref=ag_send,
            dst_ref=srcspec_ref.at[src_dev],
            send_sem=ag_send_sem.at[peer],
            recv_sem=ag_recv_sem.at[src_dev],
            device_id={"chan": peer},
            device_id_type=MESH,
        )

    for i in range(1, n_chan):
        agc(lax.rem(mc + corder[i], n_chan), mc).start()
    srcspec_ref[mc] = ag_send[...]
    for i in range(1, n_chan):
        agc(lax.rem(mc + corder[i], n_chan), mc).wait_send()
    for i in range(1, n_chan):
        src = lax.rem(mc + n_chan - i, n_chan)
        agc(src, src).wait_recv()


def fused_exchange(offsets, record, dead, sources, n_tm, n_chan, bins_dev, first, count):
    channels, span = record.shape
    nsrc = sources.shape[1]
    group = 8
    vmem = pl.BlockSpec(memory_space=pltpu.VMEM)
    return pl.pallas_call(
        functools.partial(_fused_kernel, n_tm, n_chan, bins_dev, first, count),
        out_shape=(
            jax.ShapeDtypeStruct((NWIN * 2, bins_dev, channels), jnp.float32),
            jax.ShapeDtypeStruct((n_chan, 16, nsrc), jnp.float32),
        ),
        in_specs=[pl.BlockSpec(memory_space=pltpu.SMEM), vmem, vmem, vmem],
        out_specs=(vmem, vmem),
        scratch_shapes=[
            pltpu.VMEM((SLOTS, n_tm, span), jnp.float32),
            pltpu.VMEM((SLOTS, n_tm, span), jnp.float32),
            pltpu.VMEM((SLOTS, 2 * bins_dev, span), jnp.float32),
            pltpu.VMEM((SLOTS, 2 * bins_dev, span), jnp.float32),
            pltpu.VMEM((SLOTS, channels, span), jnp.bfloat16),
            pltpu.VMEM((n_tm, SLOTS, 2 * bins_dev, channels), jnp.float32),
            pltpu.VMEM((group * 2 * bins_dev, span), jnp.float32),
            pltpu.VMEM((n_tm, SLOTS, 2 * bins_dev, channels), jnp.float32),
            pltpu.VMEM((NWIN, 2 * bins_dev, channels), jnp.float32),
            pltpu.VMEM((8, channels), jnp.float32),
            pltpu.VMEM((n_tm, 8, channels), jnp.float32),
            pltpu.VMEM((n_chan, 16, nsrc), jnp.float32),
            pltpu.SemaphoreType.DMA((n_tm, SLOTS)),
            pltpu.SemaphoreType.DMA((n_tm, SLOTS)),
            pltpu.SemaphoreType.DMA((n_tm,)),
            pltpu.SemaphoreType.DMA((n_tm,)),
            pltpu.SemaphoreType.DMA((n_chan,)),
            pltpu.SemaphoreType.DMA((n_chan,)),
            pltpu.VMEM((n_chan, 16, nsrc), jnp.float32),
            pltpu.VMEM((16, nsrc), jnp.float32),
            pltpu.SemaphoreType.DMA((n_chan,)),
            pltpu.SemaphoreType.DMA((n_chan,)),
        ],
        compiler_params=pltpu.CompilerParams(collective_id=0, has_side_effects=True),
    )(offsets, record, dead, sources)


def shards(record, offsets, dead_mask, sources):
    n_tm = lax.axis_size("tm")
    n_chan = lax.axis_size("chan")
    bins_dev = F // n_tm
    channels, span = record.shape
    first, count = window_plan(n_tm, span)
    white, source_spec = fused_exchange(
        offsets, record, dead_mask.reshape(1, channels), sources.reshape(1, -1),
        n_tm, n_chan, bins_dev, first, count
    )

    per = NWIN * 2 * bins_dev // n_chan
    assert per * n_chan == NWIN * 2 * bins_dev and bins_dev % per == 0 and per <= 16
    left = source_spec[:, :per].astype(jnp.bfloat16).reshape(NWIN, 2, bins_dev, -1)
    right = white.astype(jnp.bfloat16).reshape(NWIN, 2, bins_dev, channels)
    right_imaginary = jnp.stack([right[:, 1], -right[:, 0]], axis=1)
    real_component = jnp.einsum(
        "wpks,wpkc->ksc", left, right, preferred_element_type=jnp.float32
    )
    imaginary_component = jnp.einsum(
        "wpks,wpkc->ksc", left, right_imaginary, preferred_element_type=jnp.float32
    )
    return jnp.stack([real_component, imaginary_component], axis=1) / NWIN


def solution(mesh):
    return jax.shard_map(
        shards,
        mesh=mesh,
        in_specs=(P("chan", "tm"), P(), P("chan"), P()),
        out_specs=P("tm", None, None, "chan"),
        check_vma=False,
    )
```

```python
import functools
import math

import jax
import jax.numpy as jnp
from jax import lax
from jax.experimental import pallas as pl
from jax.experimental.pallas import tpu as pltpu
from jax.sharding import PartitionSpec as P

W = 12000
F = 640
FLO = 6
NWIN = 4
SLOTS = 2
FA = 64

MESH = pl.DeviceIdType.MESH


def window_plan(n_tm, span):
    total = n_tm * span
    slack = total - NWIN * W
    lows = [0] + [w * W for w in range(1, NWIN - 1)] + [total - W]
    highs = [0] + [w * W + slack for w in range(1, NWIN - 1)] + [total - W]
    first, count = [], []
    for d in range(n_tm):
        meets = [w for w in range(NWIN) if lows[w] < (d + 1) * span and highs[w] + W > d * span]
        assert meets and meets == list(range(meets[0], meets[0] + len(meets)))
        assert len(meets) <= SLOTS
        first.append(meets[0])
        count.append(len(meets))
    return first, count


def _ring_order(n):
    order = [0]
    for i in range(1, n):
        order.append((i + 1) // 2 if i % 2 else n - i // 2)
    assert sorted(order) == list(range(n))
    return order


def _any_of(me, members):
    hit = jnp.bool_(False)
    for m in members:
        hit = hit | (me == m)
    return hit


def _fused_kernel(n_tm, n_chan, bins_dev, first, count,
                  offsets_ref, record_ref, dead_ref, sources_ref,
                  white_ref, srcspec_ref,
                  ar_ref, ai_ref, c1_ref, c2_ref, x_ref,
                  blocks_ref, lhs, recv, spec, lvl_send, lvl_recv, src_send,
                  a2a_send_sem, a2a_recv_sem, lvl_send_sem, lvl_recv_sem,
                  src_send_sem, src_recv_sem, rs_recv, ag_send, ag_send_sem, ag_recv_sem):
    me = lax.axis_index("tm")
    mc = lax.axis_index("chan")
    two = [d for d in range(n_tm) if count[d] == 2]
    me_two = _any_of(me, two)
    rows = 2 * bins_dev
    group = lhs.shape[0] // rows

    order = _ring_order(n_tm)
    corder = _ring_order(n_chan)
    barrier = pltpu.get_barrier_semaphore()
    for i in range(1, n_tm):
        pl.semaphore_signal(barrier, inc=1, device_id={"tm": lax.rem(me + order[i], n_tm)},
                            device_id_type=MESH)
    for i in range(1, n_chan):
        pl.semaphore_signal(barrier, inc=1, device_id={"chan": lax.rem(mc + corder[i], n_chan)},
                            device_id_type=MESH)

    span = record_ref.shape[1]
    wa = jnp.int32(0)
    for d in range(n_tm):
        wa = jnp.where(me == d, first[d], wa)
    local_times = me * span + lax.broadcasted_iota(jnp.int32, (1, span), 1)
    coarse = FLO + bins_dev * lax.broadcasted_iota(jnp.int32, (n_tm, 1), 0)
    fine_row = lax.broadcasted_iota(jnp.int32, (2 * bins_dev, 1), 0)
    fine = lax.rem(fine_row, bins_dev)
    scale = 2.0 * math.pi / W

    def prepare(slot):
        window = wa + slot
        origin = offsets_ref[jnp.minimum(window, NWIN - 1)]
        shifted = local_times - origin
        inside = (shifted >= 0) & (shifted < W) & (window < NWIN)
        times = jnp.where(inside, shifted, 0)
        angle = lax.rem(coarse * times, W).astype(jnp.float32) * scale
        ar_ref[slot] = jnp.cos(angle)
        ai_ref[slot] = -jnp.sin(angle)
        angle = lax.rem(fine * times, W).astype(jnp.float32) * scale
        cos, sin = jnp.cos(angle), jnp.sin(angle)
        top = fine_row < bins_dev
        c1_ref[slot] = jnp.where(top, cos, -sin)
        c2_ref[slot] = jnp.where(top, sin, cos)
        x_ref[slot] = jnp.where(inside, record_ref[...], jnp.zeros_like(record_ref[...]))

    prepare(0)

    @pl.when(me_two)
    def _():
        prepare(1)

    def a2a(peer, slot, src_dev):
        return pltpu.make_async_remote_copy(
            src_ref=blocks_ref.at[peer, slot],
            dst_ref=recv.at[src_dev, slot],
            send_sem=a2a_send_sem.at[peer, slot],
            recv_sem=a2a_recv_sem.at[src_dev, slot],
            device_id={"tm": peer},
            device_id_type=MESH,
        )

    def compute(g, slot):
        c1 = c1_ref[slot]
        c2 = c2_ref[slot]
        for dd in range(group):
            d = lax.rem(me + order[g * group + dd], n_tm)
            ar = ar_ref[slot, pl.ds(d, 1), :]
            ai = ai_ref[slot, pl.ds(d, 1), :]
            lhs[dd * rows:(dd + 1) * rows, :] = ar * c1 + ai * c2
        res = lax.dot_general(
            lhs[...].astype(jnp.bfloat16), x_ref[slot], (((1,), (1,)), ((), ())),
            preferred_element_type=jnp.float32,
        )
        for dd in range(group):
            d = lax.rem(me + order[g * group + dd], n_tm)
            blocks_ref[d, slot] = res[dd * rows:(dd + 1) * rows, :]

    def send(g, slot):
        for dd in range(group):
            if g == 0 and dd == 0:
                continue
            a2a(lax.rem(me + order[g * group + dd], n_tm), slot, me).start()

    for g in range(n_tm // group):
        compute(g, 0)
        if g == 0:
            pl.semaphore_wait(barrier, n_tm - 1 + n_chan - 1)
        send(g, 0)

        @pl.when(me_two)
        def _():
            compute(g, 1)
            send(g, 1)

    recv[me, 0] = blocks_ref[me, 0]

    @pl.when(me_two)
    def _():
        recv[me, 1] = blocks_ref[me, 1]

    for i in range(1, n_tm):
        peer = lax.rem(me + order[i], n_tm)
        a2a(peer, 0, me).wait_send()

        @pl.when(me_two)
        def _():
            a2a(peer, 1, me).wait_send()

    for s in range(n_tm):
        @pl.when(me != s)
        def _():
            a2a(s, 0, s).wait_recv()
            if count[s] == 2:
                a2a(s, 1, s).wait_recv()

    for w in range(NWIN):
        acc = None
        for s in range(n_tm):
            for j in range(count[s]):
                if first[s] + j == w:
                    part = recv[s, j]
                    acc = part if acc is None else acc + part
        spec[w] = acc

    rows = []
    for w in range(NWIN):
        re = spec[w, 0:bins_dev, :]
        im = spec[w, bins_dev:2 * bins_dev, :]
        mag = jnp.sqrt(re * re + im * im)
        rows.append(jnp.sum(mag, axis=0, keepdims=True))
    rows.append(jnp.zeros((8 - NWIN, rows[0].shape[1]), jnp.float32))
    lvl_send[...] = jnp.concatenate(rows, axis=0)

    def lvl(peer, src_dev):
        return pltpu.make_async_remote_copy(
            src_ref=lvl_send,
            dst_ref=lvl_recv.at[src_dev],
            send_sem=lvl_send_sem.at[peer],
            recv_sem=lvl_recv_sem.at[src_dev],
            device_id={"tm": peer},
            device_id_type=MESH,
        )

    for i in range(1, n_tm):
        lvl(lax.rem(me + order[i], n_tm), me).start()
    lvl_recv[me] = lvl_send[...]
    for i in range(1, n_tm):
        lvl(lax.rem(me + order[i], n_tm), me).wait_send()
    for i in range(1, n_tm):
        src = lax.rem(me + n_tm - i, n_tm)
        lvl(src, src).wait_recv()

    level = lvl_recv[0]
    for s in range(1, n_tm):
        level = level + lvl_recv[s]
    level = level / F

    mask = dead_ref[...].astype(jnp.float32)
    channels = record_ref.shape[0]
    local_index = sources_ref[...] - mc * channels
    onehot = (lax.broadcasted_iota(jnp.int32, (channels, local_index.shape[1]), 0)
              == local_index).astype(jnp.bfloat16)
    per = NWIN * 2 * bins_dev // n_chan
    halves = bins_dev // per
    src_send[...] = jnp.zeros_like(src_send)
    for w in range(NWIN):
        re = spec[w, 0:bins_dev, :]
        im = spec[w, bins_dev:2 * bins_dev, :]
        mag = jnp.sqrt(re * re + im * im)
        den = mag + 0.1 * level[w:w + 1, :] + 1e-06
        for p, part in enumerate((re, im)):
            white = (part / den).astype(jnp.bfloat16).astype(jnp.float32) * mask
            white_ref[2 * w + p] = white
            picked = jnp.dot(
                white.astype(jnp.bfloat16), onehot, preferred_element_type=jnp.float32
            )
            for h in range(halves):
                src_send[(2 * w + p) * halves + h, 0:per, :] = picked[h * per:(h + 1) * per, :]

    def rsc(peer, src_dev):
        return pltpu.make_async_remote_copy(
            src_ref=src_send.at[peer],
            dst_ref=rs_recv.at[src_dev],
            send_sem=src_send_sem.at[peer],
            recv_sem=src_recv_sem.at[src_dev],
            device_id={"chan": peer},
            device_id_type=MESH,
        )

    for i in range(1, n_chan):
        rsc(lax.rem(mc + corder[i], n_chan), mc).start()
    rs_recv[mc] = src_send[mc]
    for i in range(1, n_chan):
        rsc(lax.rem(mc + corder[i], n_chan), mc).wait_send()
    for i in range(1, n_chan):
        src = lax.rem(mc + n_chan - i, n_chan)
        rsc(src, src).wait_recv()

    total = rs_recv[0]
    for s in range(1, n_chan):
        total = total + rs_recv[s]
    ag_send[...] = total

    def agc(peer, src_dev):
        return pltpu.make_async_remote_copy(
            src_ref=ag_send,
            dst_ref=srcspec_ref.at[src_dev],
            send_sem=ag_send_sem.at[peer],
            recv_sem=ag_recv_sem.at[src_dev],
            device_id={"chan": peer},
            device_id_type=MESH,
        )

    for i in range(1, n_chan):
        agc(lax.rem(mc + corder[i], n_chan), mc).start()
    srcspec_ref[mc] = ag_send[...]
    for i in range(1, n_chan):
        agc(lax.rem(mc + corder[i], n_chan), mc).wait_send()
    for i in range(1, n_chan):
        src = lax.rem(mc + n_chan - i, n_chan)
        agc(src, src).wait_recv()


def fused_exchange(offsets, record, dead, sources, n_tm, n_chan, bins_dev, first, count):
    channels, span = record.shape
    nsrc = sources.shape[1]
    group = 8
    vmem = pl.BlockSpec(memory_space=pltpu.VMEM)
    return pl.pallas_call(
        functools.partial(_fused_kernel, n_tm, n_chan, bins_dev, first, count),
        out_shape=(
            jax.ShapeDtypeStruct((NWIN * 2, bins_dev, channels), jnp.float32),
            jax.ShapeDtypeStruct((n_chan, 16, nsrc), jnp.float32),
        ),
        in_specs=[pl.BlockSpec(memory_space=pltpu.SMEM), vmem, vmem, vmem],
        out_specs=(vmem, vmem),
        scratch_shapes=[
            pltpu.VMEM((SLOTS, n_tm, span), jnp.float32),
            pltpu.VMEM((SLOTS, n_tm, span), jnp.float32),
            pltpu.VMEM((SLOTS, 2 * bins_dev, span), jnp.float32),
            pltpu.VMEM((SLOTS, 2 * bins_dev, span), jnp.float32),
            pltpu.VMEM((SLOTS, channels, span), jnp.bfloat16),
            pltpu.VMEM((n_tm, SLOTS, 2 * bins_dev, channels), jnp.float32),
            pltpu.VMEM((group * 2 * bins_dev, span), jnp.float32),
            pltpu.VMEM((n_tm, SLOTS, 2 * bins_dev, channels), jnp.float32),
            pltpu.VMEM((NWIN, 2 * bins_dev, channels), jnp.float32),
            pltpu.VMEM((8, channels), jnp.float32),
            pltpu.VMEM((n_tm, 8, channels), jnp.float32),
            pltpu.VMEM((n_chan, 16, nsrc), jnp.float32),
            pltpu.SemaphoreType.DMA((n_tm, SLOTS)),
            pltpu.SemaphoreType.DMA((n_tm, SLOTS)),
            pltpu.SemaphoreType.DMA((n_tm,)),
            pltpu.SemaphoreType.DMA((n_tm,)),
            pltpu.SemaphoreType.DMA((n_chan,)),
            pltpu.SemaphoreType.DMA((n_chan,)),
            pltpu.VMEM((n_chan, 16, nsrc), jnp.float32),
            pltpu.VMEM((16, nsrc), jnp.float32),
            pltpu.SemaphoreType.DMA((n_chan,)),
            pltpu.SemaphoreType.DMA((n_chan,)),
        ],
        compiler_params=pltpu.CompilerParams(collective_id=0, has_side_effects=True),
    )(offsets, record, dead, sources)


def shards(record, offsets, dead_mask, sources):
    n_tm = lax.axis_size("tm")
    n_chan = lax.axis_size("chan")
    bins_dev = F // n_tm
    channels, span = record.shape
    first, count = window_plan(n_tm, span)
    white, source_spec = fused_exchange(
        offsets, record, dead_mask.reshape(1, channels), sources.reshape(1, -1),
        n_tm, n_chan, bins_dev, first, count
    )

    per = NWIN * 2 * bins_dev // n_chan
    assert per * n_chan == NWIN * 2 * bins_dev and bins_dev % per == 0 and per <= 16
    left = source_spec[:, :per].astype(jnp.bfloat16).reshape(NWIN, 2, bins_dev, -1)
    right = white.astype(jnp.bfloat16).reshape(NWIN, 2, bins_dev, channels)
    right_imaginary = jnp.stack([right[:, 1], -right[:, 0]], axis=1)
    real_component = jnp.einsum(
        "wpks,wpkc->ksc", left, right, preferred_element_type=jnp.float32
    )
    imaginary_component = jnp.einsum(
        "wpks,wpkc->ksc", left, right_imaginary, preferred_element_type=jnp.float32
    )
    return jnp.stack([real_component, imaginary_component], axis=1) / NWIN


def solution(mesh):
    return jax.shard_map(
        shards,
        mesh=mesh,
        in_specs=(P("chan", "tm"), P(), P("chan"), P()),
        out_specs=P("tm", None, None, "chan"),
        check_vma=False,
    )
```

```python
import functools
import math

import jax
import jax.numpy as jnp
from jax import lax
from jax.experimental import pallas as pl
from jax.experimental.pallas import tpu as pltpu
from jax.sharding import PartitionSpec as P

W = 12000
F = 640
FLO = 6
NWIN = 4
SLOTS = 2
FA = 64

MESH = pl.DeviceIdType.MESH


def window_plan(n_tm, span):
    total = n_tm * span
    slack = total - NWIN * W
    lows = [0] + [w * W for w in range(1, NWIN - 1)] + [total - W]
    highs = [0] + [w * W + slack for w in range(1, NWIN - 1)] + [total - W]
    first, count = [], []
    for d in range(n_tm):
        meets = [w for w in range(NWIN) if lows[w] < (d + 1) * span and highs[w] + W > d * span]
        assert meets and meets == list(range(meets[0], meets[0] + len(meets)))
        assert len(meets) <= SLOTS
        first.append(meets[0])
        count.append(len(meets))
    return first, count


def _any_of(me, members):
    hit = jnp.bool_(False)
    for m in members:
        hit = hit | (me == m)
    return hit


def _fused_kernel(n_tm, n_chan, bins_dev, first, count,
                  offsets_ref, record_ref, dead_ref, sources_ref,
                  white_ref, srcspec_ref,
                  ar_ref, ai_ref, c1_ref, c2_ref, x_ref,
                  blocks_ref, lhs, recv, spec, lvl_send, lvl_recv, src_send,
                  a2a_send_sem, a2a_recv_sem, lvl_send_sem, lvl_recv_sem,
                  src_send_sem, src_recv_sem, rs_recv, ag_send, ag_send_sem, ag_recv_sem,
                  ag_recv):
    me = lax.axis_index("tm")
    mc = lax.axis_index("chan")
    two = [d for d in range(n_tm) if count[d] == 2]
    me_two = _any_of(me, two)
    rows = 2 * bins_dev
    group = lhs.shape[0] // rows

    barrier = pltpu.get_barrier_semaphore()
    for i in range(1, n_tm):
        pl.semaphore_signal(barrier, inc=1, device_id={"tm": lax.rem(me + i, n_tm)},
                            device_id_type=MESH)
    for i in range(1, n_chan):
        pl.semaphore_signal(barrier, inc=1, device_id={"chan": lax.rem(mc + i, n_chan)},
                            device_id_type=MESH)

    span = record_ref.shape[1]
    wa = jnp.int32(0)
    for d in range(n_tm):
        wa = jnp.where(me == d, first[d], wa)
    local_times = me * span + lax.broadcasted_iota(jnp.int32, (1, span), 1)
    coarse = FLO + bins_dev * lax.broadcasted_iota(jnp.int32, (n_tm, 1), 0)
    fine_row = lax.broadcasted_iota(jnp.int32, (2 * bins_dev, 1), 0)
    fine = lax.rem(fine_row, bins_dev)
    scale = 2.0 * math.pi / W

    def prepare(slot):
        window = wa + slot
        origin = offsets_ref[jnp.minimum(window, NWIN - 1)]
        shifted = local_times - origin
        inside = (shifted >= 0) & (shifted < W) & (window < NWIN)
        times = jnp.where(inside, shifted, 0)
        angle = lax.rem(coarse * times, W).astype(jnp.float32) * scale
        ar_ref[slot] = jnp.cos(angle)
        ai_ref[slot] = -jnp.sin(angle)
        angle = lax.rem(fine * times, W).astype(jnp.float32) * scale
        cos, sin = jnp.cos(angle), jnp.sin(angle)
        top = fine_row < bins_dev
        c1_ref[slot] = jnp.where(top, cos, -sin)
        c2_ref[slot] = jnp.where(top, sin, cos)
        x_ref[slot] = jnp.where(inside, record_ref[...], jnp.zeros_like(record_ref[...]))

    prepare(0)

    @pl.when(me_two)
    def _():
        prepare(1)

    def a2a(peer, slot, src_dev):
        return pltpu.make_async_remote_copy(
            src_ref=blocks_ref.at[peer, slot],
            dst_ref=recv.at[src_dev, slot],
            send_sem=a2a_send_sem.at[peer, slot],
            recv_sem=a2a_recv_sem.at[src_dev, slot],
            device_id={"tm": peer},
            device_id_type=MESH,
        )

    def compute(g, slot):
        c1 = c1_ref[slot]
        c2 = c2_ref[slot]
        for dd in range(group):
            d = lax.rem(me + g * group + dd, n_tm)
            ar = ar_ref[slot, pl.ds(d, 1), :]
            ai = ai_ref[slot, pl.ds(d, 1), :]
            lhs[dd * rows:(dd + 1) * rows, :] = ar * c1 + ai * c2
        res = lax.dot_general(
            lhs[...].astype(jnp.bfloat16), x_ref[slot], (((1,), (1,)), ((), ())),
            preferred_element_type=jnp.float32,
        )
        for dd in range(group):
            d = lax.rem(me + g * group + dd, n_tm)
            blocks_ref[d, slot] = res[dd * rows:(dd + 1) * rows, :]

    def send(g, slot):
        for dd in range(group):
            if g == 0 and dd == 0:
                continue
            a2a(lax.rem(me + g * group + dd, n_tm), slot, me).start()

    for g in range(n_tm // group):
        compute(g, 0)
        if g == 0:
            pl.semaphore_wait(barrier, n_tm - 1 + n_chan - 1)
        send(g, 0)

        @pl.when(me_two)
        def _():
            compute(g, 1)
            send(g, 1)

    recv[me, 0] = blocks_ref[me, 0]

    @pl.when(me_two)
    def _():
        recv[me, 1] = blocks_ref[me, 1]

    for i in range(1, n_tm):
        peer = lax.rem(me + i, n_tm)
        a2a(peer, 0, me).wait_send()

        @pl.when(me_two)
        def _():
            a2a(peer, 1, me).wait_send()

    for s in range(n_tm):
        @pl.when(me != s)
        def _():
            a2a(s, 0, s).wait_recv()
            if count[s] == 2:
                a2a(s, 1, s).wait_recv()

    for w in range(NWIN):
        acc = None
        for s in range(n_tm):
            for j in range(count[s]):
                if first[s] + j == w:
                    part = recv[s, j]
                    acc = part if acc is None else acc + part
        spec[w] = acc

    rows = []
    for w in range(NWIN):
        re = spec[w, 0:bins_dev, :]
        im = spec[w, bins_dev:2 * bins_dev, :]
        mag = jnp.sqrt(re * re + im * im)
        rows.append(jnp.sum(mag, axis=0, keepdims=True))
    rows.append(jnp.zeros((8 - NWIN, rows[0].shape[1]), jnp.float32))
    lvl_send[...] = jnp.concatenate(rows, axis=0)

    def lvl(peer, src_dev):
        return pltpu.make_async_remote_copy(
            src_ref=lvl_send,
            dst_ref=lvl_recv.at[src_dev],
            send_sem=lvl_send_sem.at[peer],
            recv_sem=lvl_recv_sem.at[src_dev],
            device_id={"tm": peer},
            device_id_type=MESH,
        )

    for i in range(1, n_tm):
        lvl(lax.rem(me + i, n_tm), me).start()
    lvl_recv[me] = lvl_send[...]
    for i in range(1, n_tm):
        lvl(lax.rem(me + i, n_tm), me).wait_send()
    for i in range(1, n_tm):
        src = lax.rem(me + n_tm - i, n_tm)
        lvl(src, src).wait_recv()

    level = lvl_recv[0]
    for s in range(1, n_tm):
        level = level + lvl_recv[s]
    level = level / F

    mask = dead_ref[...].astype(jnp.float32)
    channels = record_ref.shape[0]
    local_index = sources_ref[...] - mc * channels
    onehot = (lax.broadcasted_iota(jnp.int32, (channels, local_index.shape[1]), 0)
              == local_index).astype(jnp.bfloat16)
    per = NWIN * 2 * bins_dev // n_chan
    halves = bins_dev // per
    src_send[...] = jnp.zeros_like(src_send)
    for w in range(NWIN):
        re = spec[w, 0:bins_dev, :]
        im = spec[w, bins_dev:2 * bins_dev, :]
        mag = jnp.sqrt(re * re + im * im)
        den = mag + 0.1 * level[w:w + 1, :] + 1e-06
        for p, part in enumerate((re, im)):
            white = (part / den).astype(jnp.bfloat16).astype(jnp.float32) * mask
            white_ref[2 * w + p] = white.astype(jnp.bfloat16)
            picked = jnp.dot(
                white.astype(jnp.bfloat16), onehot, preferred_element_type=jnp.float32
            )
            for h in range(halves):
                src_send[(2 * w + p) * halves + h, 0:per, :] = picked[h * per:(h + 1) * per, :]

    def rsc(peer, src_dev):
        return pltpu.make_async_remote_copy(
            src_ref=src_send.at[peer],
            dst_ref=rs_recv.at[src_dev],
            send_sem=src_send_sem.at[peer],
            recv_sem=src_recv_sem.at[src_dev],
            device_id={"chan": peer},
            device_id_type=MESH,
        )

    for i in range(1, n_chan):
        rsc(lax.rem(mc + i, n_chan), mc).start()
    rs_recv[mc] = src_send[mc]
    for i in range(1, n_chan):
        rsc(lax.rem(mc + i, n_chan), mc).wait_send()
    for i in range(1, n_chan):
        src = lax.rem(mc + n_chan - i, n_chan)
        rsc(src, src).wait_recv()

    total = rs_recv[0]
    for s in range(1, n_chan):
        total = total + rs_recv[s]
    ag_send[...] = total

    def agc(peer, src_dev):
        return pltpu.make_async_remote_copy(
            src_ref=ag_send,
            dst_ref=ag_recv.at[src_dev],
            send_sem=ag_send_sem.at[peer],
            recv_sem=ag_recv_sem.at[src_dev],
            device_id={"chan": peer},
            device_id_type=MESH,
        )

    for i in range(1, n_chan):
        agc(lax.rem(mc + i, n_chan), mc).start()
    ag_recv[mc] = ag_send[...]
    for i in range(1, n_chan):
        agc(lax.rem(mc + i, n_chan), mc).wait_send()
    for i in range(1, n_chan):
        src = lax.rem(mc + n_chan - i, n_chan)
        agc(src, src).wait_recv()

    for i in range(NWIN * 2):
        for h in range(halves):
            srcspec_ref[i, h * per:(h + 1) * per, :] = (
                ag_recv[i * halves + h, 0:per, :].astype(jnp.bfloat16))


def fused_exchange(offsets, record, dead, sources, n_tm, n_chan, bins_dev, first, count):
    channels, span = record.shape
    nsrc = sources.shape[1]
    group = 8
    vmem = pl.BlockSpec(memory_space=pltpu.VMEM)
    return pl.pallas_call(
        functools.partial(_fused_kernel, n_tm, n_chan, bins_dev, first, count),
        out_shape=(
            jax.ShapeDtypeStruct((NWIN * 2, bins_dev, channels), jnp.bfloat16),
            jax.ShapeDtypeStruct((NWIN * 2, bins_dev, nsrc), jnp.bfloat16),
        ),
        in_specs=[pl.BlockSpec(memory_space=pltpu.SMEM), vmem, vmem, vmem],
        out_specs=(vmem, vmem),
        scratch_shapes=[
            pltpu.VMEM((SLOTS, n_tm, span), jnp.float32),
            pltpu.VMEM((SLOTS, n_tm, span), jnp.float32),
            pltpu.VMEM((SLOTS, 2 * bins_dev, span), jnp.float32),
            pltpu.VMEM((SLOTS, 2 * bins_dev, span), jnp.float32),
            pltpu.VMEM((SLOTS, channels, span), jnp.bfloat16),
            pltpu.VMEM((n_tm, SLOTS, 2 * bins_dev, channels), jnp.float32),
            pltpu.VMEM((group * 2 * bins_dev, span), jnp.float32),
            pltpu.VMEM((n_tm, SLOTS, 2 * bins_dev, channels), jnp.float32),
            pltpu.VMEM((NWIN, 2 * bins_dev, channels), jnp.float32),
            pltpu.VMEM((8, channels), jnp.float32),
            pltpu.VMEM((n_tm, 8, channels), jnp.float32),
            pltpu.VMEM((n_chan, 16, nsrc), jnp.float32),
            pltpu.SemaphoreType.DMA((n_tm, SLOTS)),
            pltpu.SemaphoreType.DMA((n_tm, SLOTS)),
            pltpu.SemaphoreType.DMA((n_tm,)),
            pltpu.SemaphoreType.DMA((n_tm,)),
            pltpu.SemaphoreType.DMA((n_chan,)),
            pltpu.SemaphoreType.DMA((n_chan,)),
            pltpu.VMEM((n_chan, 16, nsrc), jnp.float32),
            pltpu.VMEM((16, nsrc), jnp.float32),
            pltpu.SemaphoreType.DMA((n_chan,)),
            pltpu.SemaphoreType.DMA((n_chan,)),
            pltpu.VMEM((n_chan, 16, nsrc), jnp.float32),
        ],
        compiler_params=pltpu.CompilerParams(collective_id=0, has_side_effects=True),
    )(offsets, record, dead, sources)


def shards(record, offsets, dead_mask, sources):
    n_tm = lax.axis_size("tm")
    n_chan = lax.axis_size("chan")
    bins_dev = F // n_tm
    channels, span = record.shape
    first, count = window_plan(n_tm, span)
    white, source_spec = fused_exchange(
        offsets, record, dead_mask.reshape(1, channels), sources.reshape(1, -1),
        n_tm, n_chan, bins_dev, first, count
    )

    per = NWIN * 2 * bins_dev // n_chan
    assert per * n_chan == NWIN * 2 * bins_dev and bins_dev % per == 0 and per <= 16
    left = source_spec.reshape(NWIN, 2, bins_dev, -1)
    right = white.reshape(NWIN, 2, bins_dev, channels)
    right_imaginary = jnp.stack([right[:, 1], -right[:, 0]], axis=1)
    real_component = jnp.einsum(
        "wpks,wpkc->ksc", left, right, preferred_element_type=jnp.float32
    )
    imaginary_component = jnp.einsum(
        "wpks,wpkc->ksc", left, right_imaginary, preferred_element_type=jnp.float32
    )
    return jnp.stack([real_component, imaginary_component], axis=1) / NWIN


def solution(mesh):
    return jax.shard_map(
        shards,
        mesh=mesh,
        in_specs=(P("chan", "tm"), P(), P("chan"), P()),
        out_specs=P("tm", None, None, "chan"),
        check_vma=False,
    )
```

```python
import functools
import math

import jax
import jax.numpy as jnp
from jax import lax
from jax.experimental import pallas as pl
from jax.experimental.pallas import tpu as pltpu
from jax.sharding import PartitionSpec as P

W = 12000
F = 640
FLO = 6
NWIN = 4
SLOTS = 2
FA = 64

MESH = pl.DeviceIdType.MESH


def window_plan(n_tm, span):
    total = n_tm * span
    slack = total - NWIN * W
    lows = [0] + [w * W for w in range(1, NWIN - 1)] + [total - W]
    highs = [0] + [w * W + slack for w in range(1, NWIN - 1)] + [total - W]
    first, count = [], []
    for d in range(n_tm):
        meets = [w for w in range(NWIN) if lows[w] < (d + 1) * span and highs[w] + W > d * span]
        assert meets and meets == list(range(meets[0], meets[0] + len(meets)))
        assert len(meets) <= SLOTS
        first.append(meets[0])
        count.append(len(meets))
    return first, count


def _cross_kernel(bins_dev, src_ref, white_ref, rot_ref, out_ref):
    for k in range(bins_dev):
        left = src_ref[k].astype(jnp.bfloat16)
        for p, right_ref in enumerate((white_ref, rot_ref)):
            out_ref[k, p] = lax.dot_general(
                left, right_ref[k].astype(jnp.bfloat16), (((0,), (0,)), ((), ())),
                preferred_element_type=jnp.float32,
            ) / NWIN


def cross_spectra(source_spec, white, rotated):
    bins_dev, _, nsrc = source_spec.shape
    channels = white.shape[2]
    vmem = pl.BlockSpec(memory_space=pltpu.VMEM)
    return pl.pallas_call(
        functools.partial(_cross_kernel, bins_dev),
        out_shape=jax.ShapeDtypeStruct((bins_dev, 2, nsrc, channels), jnp.float32),
        in_specs=[vmem] * 3,
        out_specs=vmem,
    )(source_spec, white, rotated)


def _any_of(me, members):
    hit = jnp.bool_(False)
    for m in members:
        hit = hit | (me == m)
    return hit


def _fused_kernel(n_tm, n_chan, bins_dev, first, count,
                  offsets_ref, record_ref, dead_ref, sources_ref,
                  white_ref, rot_ref, srcspec_ref,
                  ar_ref, ai_ref, c1_ref, c2_ref, x_ref,
                  blocks_ref, lhs, recv, spec, lvl_send, lvl_recv, src_send,
                  a2a_send_sem, a2a_recv_sem, lvl_send_sem, lvl_recv_sem,
                  src_send_sem, src_recv_sem, rs_recv, ag_send, ag_send_sem, ag_recv_sem,
                  ag_recv):
    me = lax.axis_index("tm")
    mc = lax.axis_index("chan")
    two = [d for d in range(n_tm) if count[d] == 2]
    me_two = _any_of(me, two)
    rows = 2 * bins_dev
    group = lhs.shape[0] // rows

    barrier = pltpu.get_barrier_semaphore()
    for i in range(1, n_tm):
        pl.semaphore_signal(barrier, inc=1, device_id={"tm": lax.rem(me + i, n_tm)},
                            device_id_type=MESH)
    for i in range(1, n_chan):
        pl.semaphore_signal(barrier, inc=1, device_id={"chan": lax.rem(mc + i, n_chan)},
                            device_id_type=MESH)

    span = record_ref.shape[1]
    wa = jnp.int32(0)
    for d in range(n_tm):
        wa = jnp.where(me == d, first[d], wa)
    local_times = me * span + lax.broadcasted_iota(jnp.int32, (1, span), 1)
    coarse = FLO + bins_dev * lax.broadcasted_iota(jnp.int32, (n_tm, 1), 0)
    fine_row = lax.broadcasted_iota(jnp.int32, (2 * bins_dev, 1), 0)
    fine = lax.rem(fine_row, bins_dev)
    scale = 2.0 * math.pi / W

    def prepare(slot):
        window = wa + slot
        origin = offsets_ref[jnp.minimum(window, NWIN - 1)]
        shifted = local_times - origin
        inside = (shifted >= 0) & (shifted < W) & (window < NWIN)
        times = jnp.where(inside, shifted, 0)
        angle = lax.rem(coarse * times, W).astype(jnp.float32) * scale
        ar_ref[slot] = jnp.cos(angle)
        ai_ref[slot] = -jnp.sin(angle)
        angle = lax.rem(fine * times, W).astype(jnp.float32) * scale
        cos, sin = jnp.cos(angle), jnp.sin(angle)
        top = fine_row < bins_dev
        c1_ref[slot] = jnp.where(top, cos, -sin)
        c2_ref[slot] = jnp.where(top, sin, cos)
        x_ref[slot] = jnp.where(inside, record_ref[...], jnp.zeros_like(record_ref[...]))

    prepare(0)

    @pl.when(me_two)
    def _():
        prepare(1)

    def a2a(peer, slot, src_dev):
        return pltpu.make_async_remote_copy(
            src_ref=blocks_ref.at[peer, slot],
            dst_ref=recv.at[src_dev, slot],
            send_sem=a2a_send_sem.at[peer, slot],
            recv_sem=a2a_recv_sem.at[src_dev, slot],
            device_id={"tm": peer},
            device_id_type=MESH,
        )

    def compute(g, slot):
        c1 = c1_ref[slot]
        c2 = c2_ref[slot]
        for dd in range(group):
            d = lax.rem(me + g * group + dd, n_tm)
            ar = ar_ref[slot, pl.ds(d, 1), :]
            ai = ai_ref[slot, pl.ds(d, 1), :]
            lhs[dd * rows:(dd + 1) * rows, :] = ar * c1 + ai * c2
        res = lax.dot_general(
            lhs[...].astype(jnp.bfloat16), x_ref[slot], (((1,), (1,)), ((), ())),
            preferred_element_type=jnp.float32,
        )
        for dd in range(group):
            d = lax.rem(me + g * group + dd, n_tm)
            blocks_ref[d, slot] = res[dd * rows:(dd + 1) * rows, :]

    def send(g, slot):
        for dd in range(group):
            if g == 0 and dd == 0:
                continue
            a2a(lax.rem(me + g * group + dd, n_tm), slot, me).start()

    for g in range(n_tm // group):
        compute(g, 0)
        if g == 0:
            pl.semaphore_wait(barrier, n_tm - 1 + n_chan - 1)
        send(g, 0)

        @pl.when(me_two)
        def _():
            compute(g, 1)
            send(g, 1)

    recv[me, 0] = blocks_ref[me, 0]

    @pl.when(me_two)
    def _():
        recv[me, 1] = blocks_ref[me, 1]

    for i in range(1, n_tm):
        peer = lax.rem(me + i, n_tm)
        a2a(peer, 0, me).wait_send()

        @pl.when(me_two)
        def _():
            a2a(peer, 1, me).wait_send()

    for s in range(n_tm):
        @pl.when(me != s)
        def _():
            a2a(s, 0, s).wait_recv()
            if count[s] == 2:
                a2a(s, 1, s).wait_recv()

    for w in range(NWIN):
        acc = None
        for s in range(n_tm):
            for j in range(count[s]):
                if first[s] + j == w:
                    part = recv[s, j]
                    acc = part if acc is None else acc + part
        spec[w] = acc

    rows = []
    for w in range(NWIN):
        re = spec[w, 0:bins_dev, :]
        im = spec[w, bins_dev:2 * bins_dev, :]
        mag = jnp.sqrt(re * re + im * im)
        rows.append(jnp.sum(mag, axis=0, keepdims=True))
    rows.append(jnp.zeros((8 - NWIN, rows[0].shape[1]), jnp.float32))
    lvl_send[...] = jnp.concatenate(rows, axis=0)

    def lvl(peer, src_dev):
        return pltpu.make_async_remote_copy(
            src_ref=lvl_send,
            dst_ref=lvl_recv.at[src_dev],
            send_sem=lvl_send_sem.at[peer],
            recv_sem=lvl_recv_sem.at[src_dev],
            device_id={"tm": peer},
            device_id_type=MESH,
        )

    for i in range(1, n_tm):
        lvl(lax.rem(me + i, n_tm), me).start()
    lvl_recv[me] = lvl_send[...]
    for i in range(1, n_tm):
        lvl(lax.rem(me + i, n_tm), me).wait_send()
    for i in range(1, n_tm):
        src = lax.rem(me + n_tm - i, n_tm)
        lvl(src, src).wait_recv()

    level = lvl_recv[0]
    for s in range(1, n_tm):
        level = level + lvl_recv[s]
    level = level / F

    mask = dead_ref[...].astype(jnp.float32)
    channels = record_ref.shape[0]
    local_index = sources_ref[...] - mc * channels
    onehot = (lax.broadcasted_iota(jnp.int32, (channels, local_index.shape[1]), 0)
              == local_index).astype(jnp.bfloat16)
    per = NWIN * 2 * bins_dev // n_chan
    halves = bins_dev // per
    src_send[...] = jnp.zeros_like(src_send)
    for w in range(NWIN):
        re = spec[w, 0:bins_dev, :]
        im = spec[w, bins_dev:2 * bins_dev, :]
        mag = jnp.sqrt(re * re + im * im)
        den = mag + 0.1 * level[w:w + 1, :] + 1e-06
        for p, part in enumerate((re, im)):
            white = (part / den).astype(jnp.bfloat16).astype(jnp.float32) * mask
            for k in range(bins_dev):
                white_ref[k, 2 * w + p:2 * w + p + 1, :] = white[k:k + 1, :]
                if p == 0:
                    rot_ref[k, 2 * w + 1:2 * w + 2, :] = -white[k:k + 1, :]
                else:
                    rot_ref[k, 2 * w:2 * w + 1, :] = white[k:k + 1, :]
            picked = jnp.dot(
                white.astype(jnp.bfloat16), onehot, preferred_element_type=jnp.float32
            )
            for h in range(halves):
                src_send[(2 * w + p) * halves + h, 0:per, :] = picked[h * per:(h + 1) * per, :]

    def rsc(peer, src_dev):
        return pltpu.make_async_remote_copy(
            src_ref=src_send.at[peer],
            dst_ref=rs_recv.at[src_dev],
            send_sem=src_send_sem.at[peer],
            recv_sem=src_recv_sem.at[src_dev],
            device_id={"chan": peer},
            device_id_type=MESH,
        )

    for i in range(1, n_chan):
        rsc(lax.rem(mc + i, n_chan), mc).start()
    rs_recv[mc] = src_send[mc]
    for i in range(1, n_chan):
        rsc(lax.rem(mc + i, n_chan), mc).wait_send()
    for i in range(1, n_chan):
        src = lax.rem(mc + n_chan - i, n_chan)
        rsc(src, src).wait_recv()

    total = rs_recv[0]
    for s in range(1, n_chan):
        total = total + rs_recv[s]
    ag_send[...] = total

    def agc(peer, src_dev):
        return pltpu.make_async_remote_copy(
            src_ref=ag_send,
            dst_ref=ag_recv.at[src_dev],
            send_sem=ag_send_sem.at[peer],
            recv_sem=ag_recv_sem.at[src_dev],
            device_id={"chan": peer},
            device_id_type=MESH,
        )

    for i in range(1, n_chan):
        agc(lax.rem(mc + i, n_chan), mc).start()
    ag_recv[mc] = ag_send[...]
    for i in range(1, n_chan):
        agc(lax.rem(mc + i, n_chan), mc).wait_send()
    for i in range(1, n_chan):
        src = lax.rem(mc + n_chan - i, n_chan)
        agc(src, src).wait_recv()

    for i in range(NWIN * 2):
        for h in range(halves):
            for r in range(per):
                k = h * per + r
                srcspec_ref[k, i:i + 1, :] = ag_recv[i * halves + h, r:r + 1, :]


def fused_exchange(offsets, record, dead, sources, n_tm, n_chan, bins_dev, first, count):
    channels, span = record.shape
    nsrc = sources.shape[1]
    group = 8
    vmem = pl.BlockSpec(memory_space=pltpu.VMEM)
    return pl.pallas_call(
        functools.partial(_fused_kernel, n_tm, n_chan, bins_dev, first, count),
        out_shape=(
            jax.ShapeDtypeStruct((bins_dev, NWIN * 2, channels), jnp.float32),
            jax.ShapeDtypeStruct((bins_dev, NWIN * 2, channels), jnp.float32),
            jax.ShapeDtypeStruct((bins_dev, NWIN * 2, nsrc), jnp.float32),
        ),
        in_specs=[pl.BlockSpec(memory_space=pltpu.SMEM), vmem, vmem, vmem],
        out_specs=(vmem, vmem, vmem),
        scratch_shapes=[
            pltpu.VMEM((SLOTS, n_tm, span), jnp.float32),
            pltpu.VMEM((SLOTS, n_tm, span), jnp.float32),
            pltpu.VMEM((SLOTS, 2 * bins_dev, span), jnp.float32),
            pltpu.VMEM((SLOTS, 2 * bins_dev, span), jnp.float32),
            pltpu.VMEM((SLOTS, channels, span), jnp.bfloat16),
            pltpu.VMEM((n_tm, SLOTS, 2 * bins_dev, channels), jnp.float32),
            pltpu.VMEM((group * 2 * bins_dev, span), jnp.float32),
            pltpu.VMEM((n_tm, SLOTS, 2 * bins_dev, channels), jnp.float32),
            pltpu.VMEM((NWIN, 2 * bins_dev, channels), jnp.float32),
            pltpu.VMEM((8, channels), jnp.float32),
            pltpu.VMEM((n_tm, 8, channels), jnp.float32),
            pltpu.VMEM((n_chan, 16, nsrc), jnp.float32),
            pltpu.SemaphoreType.DMA((n_tm, SLOTS)),
            pltpu.SemaphoreType.DMA((n_tm, SLOTS)),
            pltpu.SemaphoreType.DMA((n_tm,)),
            pltpu.SemaphoreType.DMA((n_tm,)),
            pltpu.SemaphoreType.DMA((n_chan,)),
            pltpu.SemaphoreType.DMA((n_chan,)),
            pltpu.VMEM((n_chan, 16, nsrc), jnp.float32),
            pltpu.VMEM((16, nsrc), jnp.float32),
            pltpu.SemaphoreType.DMA((n_chan,)),
            pltpu.SemaphoreType.DMA((n_chan,)),
            pltpu.VMEM((n_chan, 16, nsrc), jnp.float32),
        ],
        compiler_params=pltpu.CompilerParams(collective_id=0, has_side_effects=True),
    )(offsets, record, dead, sources)


def shards(record, offsets, dead_mask, sources):
    n_tm = lax.axis_size("tm")
    n_chan = lax.axis_size("chan")
    bins_dev = F // n_tm
    channels, span = record.shape
    first, count = window_plan(n_tm, span)
    per = NWIN * 2 * bins_dev // n_chan
    assert per * n_chan == NWIN * 2 * bins_dev and bins_dev % per == 0 and per <= 16
    white, rotated, source_spec = fused_exchange(
        offsets, record, dead_mask.reshape(1, channels), sources.reshape(1, -1),
        n_tm, n_chan, bins_dev, first, count
    )
    return cross_spectra(source_spec, white, rotated)


def solution(mesh):
    return jax.shard_map(
        shards,
        mesh=mesh,
        in_specs=(P("chan", "tm"), P(), P("chan"), P()),
        out_specs=P("tm", None, None, "chan"),
        check_vma=False,
    )
```

```python
import functools
import math

import jax
import jax.numpy as jnp
from jax import lax
from jax.experimental import pallas as pl
from jax.experimental.pallas import tpu as pltpu
from jax.sharding import PartitionSpec as P

W = 12000
F = 640
FLO = 6
NWIN = 4
SLOTS = 2
FA = 64

MESH = pl.DeviceIdType.MESH


def window_plan(n_tm, span):
    total = n_tm * span
    slack = total - NWIN * W
    lows = [0] + [w * W for w in range(1, NWIN - 1)] + [total - W]
    highs = [0] + [w * W + slack for w in range(1, NWIN - 1)] + [total - W]
    first, count = [], []
    for d in range(n_tm):
        meets = [w for w in range(NWIN) if lows[w] < (d + 1) * span and highs[w] + W > d * span]
        assert meets and meets == list(range(meets[0], meets[0] + len(meets)))
        assert len(meets) <= SLOTS
        first.append(meets[0])
        count.append(len(meets))
    return first, count


def _cross_kernel(bins_dev, src_ref, white_ref, rot_ref, out_ref):
    for k in range(bins_dev):
        left = src_ref[k].astype(jnp.bfloat16)
        for p, right_ref in enumerate((white_ref, rot_ref)):
            out_ref[k, p] = lax.dot_general(
                left, right_ref[k].astype(jnp.bfloat16), (((0,), (0,)), ((), ())),
                preferred_element_type=jnp.float32,
            ) / NWIN


def cross_spectra(source_spec, white, rotated):
    bins_dev, _, nsrc = source_spec.shape
    channels = white.shape[2]
    vmem = pl.BlockSpec(memory_space=pltpu.VMEM)
    return pl.pallas_call(
        functools.partial(_cross_kernel, bins_dev),
        out_shape=jax.ShapeDtypeStruct((bins_dev, 2, nsrc, channels), jnp.float32),
        in_specs=[vmem] * 3,
        out_specs=vmem,
    )(source_spec, white, rotated)


def _any_of(me, members):
    hit = jnp.bool_(False)
    for m in members:
        hit = hit | (me == m)
    return hit


def _fused_kernel(n_tm, n_chan, bins_dev, first, count,
                  offsets_ref, record_ref, dead_ref, sources_ref,
                  white_ref, rot_ref, srcspec_ref,
                  ar_ref, ai_ref, c1_ref, c2_ref, x_ref,
                  blocks_ref, lhs, recv, spec, lvl_send, lvl_recv, src_send,
                  a2a_send_sem, a2a_recv_sem, lvl_send_sem, lvl_recv_sem,
                  src_send_sem, src_recv_sem, rs_recv, ag_send, ag_send_sem, ag_recv_sem,
                  ag_recv):
    me = lax.axis_index("tm")
    mc = lax.axis_index("chan")
    two = [d for d in range(n_tm) if count[d] == 2]
    me_two = _any_of(me, two)
    rows = 2 * bins_dev
    group = lhs.shape[0] // rows

    barrier = pltpu.get_barrier_semaphore()
    for i in range(1, n_tm):
        pl.semaphore_signal(barrier, inc=1, device_id={"tm": lax.rem(me + i, n_tm)},
                            device_id_type=MESH)
    for i in range(1, n_chan):
        pl.semaphore_signal(barrier, inc=1, device_id={"chan": lax.rem(mc + i, n_chan)},
                            device_id_type=MESH)

    span = record_ref.shape[1]
    wa = jnp.int32(0)
    for d in range(n_tm):
        wa = jnp.where(me == d, first[d], wa)
    local_times = me * span + lax.broadcasted_iota(jnp.int32, (1, span), 1)
    coarse = FLO + bins_dev * lax.broadcasted_iota(jnp.int32, (n_tm, 1), 0)
    fine_row = lax.broadcasted_iota(jnp.int32, (2 * bins_dev, 1), 0)
    fine = lax.rem(fine_row, bins_dev)
    scale = 2.0 * math.pi / W

    def prepare(slot):
        window = wa + slot
        origin = offsets_ref[jnp.minimum(window, NWIN - 1)]
        shifted = local_times - origin
        inside = (shifted >= 0) & (shifted < W) & (window < NWIN)
        times = jnp.where(inside, shifted, 0)
        angle = lax.rem(coarse * times, W).astype(jnp.float32) * scale
        ar_ref[slot] = jnp.cos(angle)
        ai_ref[slot] = -jnp.sin(angle)
        angle = lax.rem(fine * times, W).astype(jnp.float32) * scale
        cos, sin = jnp.cos(angle), jnp.sin(angle)
        top = fine_row < bins_dev
        c1_ref[slot] = jnp.where(top, cos, -sin)
        c2_ref[slot] = jnp.where(top, sin, cos)
        x_ref[slot] = jnp.where(inside, record_ref[...], jnp.zeros_like(record_ref[...]))

    prepare(0)

    @pl.when(me_two)
    def _():
        prepare(1)

    def a2a(peer, slot, src_dev):
        return pltpu.make_async_remote_copy(
            src_ref=blocks_ref.at[peer, slot],
            dst_ref=recv.at[src_dev, slot],
            send_sem=a2a_send_sem.at[peer, slot],
            recv_sem=a2a_recv_sem.at[src_dev, slot],
            device_id={"tm": peer},
            device_id_type=MESH,
        )

    def compute(g, slot):
        c1 = c1_ref[slot]
        c2 = c2_ref[slot]
        for dd in range(group):
            d = lax.rem(me + n_tm - (g * group + dd), n_tm)
            ar = ar_ref[slot, pl.ds(d, 1), :]
            ai = ai_ref[slot, pl.ds(d, 1), :]
            lhs[dd * rows:(dd + 1) * rows, :] = ar * c1 + ai * c2
        res = lax.dot_general(
            lhs[...].astype(jnp.bfloat16), x_ref[slot], (((1,), (1,)), ((), ())),
            preferred_element_type=jnp.float32,
        )
        for dd in range(group):
            d = lax.rem(me + n_tm - (g * group + dd), n_tm)
            blocks_ref[d, slot] = res[dd * rows:(dd + 1) * rows, :]

    def send(g, slot):
        for dd in range(group):
            if g == 0 and dd == 0:
                continue
            a2a(lax.rem(me + n_tm - (g * group + dd), n_tm), slot, me).start()

    for g in range(n_tm // group):
        compute(g, 0)
        if g == 0:
            pl.semaphore_wait(barrier, n_tm - 1 + n_chan - 1)
        send(g, 0)

        @pl.when(me_two)
        def _():
            compute(g, 1)
            send(g, 1)

    recv[me, 0] = blocks_ref[me, 0]

    @pl.when(me_two)
    def _():
        recv[me, 1] = blocks_ref[me, 1]

    for i in range(1, n_tm):
        peer = lax.rem(me + i, n_tm)
        a2a(peer, 0, me).wait_send()

        @pl.when(me_two)
        def _():
            a2a(peer, 1, me).wait_send()

    for s in range(n_tm):
        @pl.when(me != s)
        def _():
            a2a(s, 0, s).wait_recv()
            if count[s] == 2:
                a2a(s, 1, s).wait_recv()

    for w in range(NWIN):
        acc = None
        for s in range(n_tm):
            for j in range(count[s]):
                if first[s] + j == w:
                    part = recv[s, j]
                    acc = part if acc is None else acc + part
        spec[w] = acc

    rows = []
    for w in range(NWIN):
        re = spec[w, 0:bins_dev, :]
        im = spec[w, bins_dev:2 * bins_dev, :]
        mag = jnp.sqrt(re * re + im * im)
        rows.append(jnp.sum(mag, axis=0, keepdims=True))
    rows.append(jnp.zeros((8 - NWIN, rows[0].shape[1]), jnp.float32))
    lvl_send[...] = jnp.concatenate(rows, axis=0)

    def lvl(peer, src_dev):
        return pltpu.make_async_remote_copy(
            src_ref=lvl_send,
            dst_ref=lvl_recv.at[src_dev],
            send_sem=lvl_send_sem.at[peer],
            recv_sem=lvl_recv_sem.at[src_dev],
            device_id={"tm": peer},
            device_id_type=MESH,
        )

    for i in range(1, n_tm):
        lvl(lax.rem(me + i, n_tm), me).start()
    lvl_recv[me] = lvl_send[...]
    for i in range(1, n_tm):
        lvl(lax.rem(me + i, n_tm), me).wait_send()
    for i in range(1, n_tm):
        src = lax.rem(me + n_tm - i, n_tm)
        lvl(src, src).wait_recv()

    level = lvl_recv[0]
    for s in range(1, n_tm):
        level = level + lvl_recv[s]
    level = level / F

    mask = dead_ref[...].astype(jnp.float32)
    channels = record_ref.shape[0]
    local_index = sources_ref[...] - mc * channels
    onehot = (lax.broadcasted_iota(jnp.int32, (channels, local_index.shape[1]), 0)
              == local_index).astype(jnp.bfloat16)
    per = NWIN * 2 * bins_dev // n_chan
    halves = bins_dev // per
    src_send[...] = jnp.zeros_like(src_send)
    for w in range(NWIN):
        re = spec[w, 0:bins_dev, :]
        im = spec[w, bins_dev:2 * bins_dev, :]
        mag = jnp.sqrt(re * re + im * im)
        den = mag + 0.1 * level[w:w + 1, :] + 1e-06
        for p, part in enumerate((re, im)):
            white = (part / den).astype(jnp.bfloat16).astype(jnp.float32) * mask
            for k in range(bins_dev):
                white_ref[k, 2 * w + p:2 * w + p + 1, :] = white[k:k + 1, :]
                if p == 0:
                    rot_ref[k, 2 * w + 1:2 * w + 2, :] = -white[k:k + 1, :]
                else:
                    rot_ref[k, 2 * w:2 * w + 1, :] = white[k:k + 1, :]
            picked = jnp.dot(
                white.astype(jnp.bfloat16), onehot, preferred_element_type=jnp.float32
            )
            for h in range(halves):
                src_send[(2 * w + p) * halves + h, 0:per, :] = picked[h * per:(h + 1) * per, :]

    def rsc(peer, src_dev):
        return pltpu.make_async_remote_copy(
            src_ref=src_send.at[peer],
            dst_ref=rs_recv.at[src_dev],
            send_sem=src_send_sem.at[peer],
            recv_sem=src_recv_sem.at[src_dev],
            device_id={"chan": peer},
            device_id_type=MESH,
        )

    for i in range(1, n_chan):
        rsc(lax.rem(mc + i, n_chan), mc).start()
    rs_recv[mc] = src_send[mc]
    for i in range(1, n_chan):
        rsc(lax.rem(mc + i, n_chan), mc).wait_send()
    for i in range(1, n_chan):
        src = lax.rem(mc + n_chan - i, n_chan)
        rsc(src, src).wait_recv()

    total = rs_recv[0]
    for s in range(1, n_chan):
        total = total + rs_recv[s]
    ag_send[...] = total

    def agc(peer, src_dev):
        return pltpu.make_async_remote_copy(
            src_ref=ag_send,
            dst_ref=ag_recv.at[src_dev],
            send_sem=ag_send_sem.at[peer],
            recv_sem=ag_recv_sem.at[src_dev],
            device_id={"chan": peer},
            device_id_type=MESH,
        )

    for i in range(1, n_chan):
        agc(lax.rem(mc + i, n_chan), mc).start()
    ag_recv[mc] = ag_send[...]
    for i in range(1, n_chan):
        agc(lax.rem(mc + i, n_chan), mc).wait_send()
    for i in range(1, n_chan):
        src = lax.rem(mc + n_chan - i, n_chan)
        agc(src, src).wait_recv()

    for i in range(NWIN * 2):
        for h in range(halves):
            for r in range(per):
                k = h * per + r
                srcspec_ref[k, i:i + 1, :] = ag_recv[i * halves + h, r:r + 1, :]


def fused_exchange(offsets, record, dead, sources, n_tm, n_chan, bins_dev, first, count):
    channels, span = record.shape
    nsrc = sources.shape[1]
    group = 8
    vmem = pl.BlockSpec(memory_space=pltpu.VMEM)
    return pl.pallas_call(
        functools.partial(_fused_kernel, n_tm, n_chan, bins_dev, first, count),
        out_shape=(
            jax.ShapeDtypeStruct((bins_dev, NWIN * 2, channels), jnp.float32),
            jax.ShapeDtypeStruct((bins_dev, NWIN * 2, channels), jnp.float32),
            jax.ShapeDtypeStruct((bins_dev, NWIN * 2, nsrc), jnp.float32),
        ),
        in_specs=[pl.BlockSpec(memory_space=pltpu.SMEM), vmem, vmem, vmem],
        out_specs=(vmem, vmem, vmem),
        scratch_shapes=[
            pltpu.VMEM((SLOTS, n_tm, span), jnp.float32),
            pltpu.VMEM((SLOTS, n_tm, span), jnp.float32),
            pltpu.VMEM((SLOTS, 2 * bins_dev, span), jnp.float32),
            pltpu.VMEM((SLOTS, 2 * bins_dev, span), jnp.float32),
            pltpu.VMEM((SLOTS, channels, span), jnp.bfloat16),
            pltpu.VMEM((n_tm, SLOTS, 2 * bins_dev, channels), jnp.float32),
            pltpu.VMEM((group * 2 * bins_dev, span), jnp.float32),
            pltpu.VMEM((n_tm, SLOTS, 2 * bins_dev, channels), jnp.float32),
            pltpu.VMEM((NWIN, 2 * bins_dev, channels), jnp.float32),
            pltpu.VMEM((8, channels), jnp.float32),
            pltpu.VMEM((n_tm, 8, channels), jnp.float32),
            pltpu.VMEM((n_chan, 16, nsrc), jnp.float32),
            pltpu.SemaphoreType.DMA((n_tm, SLOTS)),
            pltpu.SemaphoreType.DMA((n_tm, SLOTS)),
            pltpu.SemaphoreType.DMA((n_tm,)),
            pltpu.SemaphoreType.DMA((n_tm,)),
            pltpu.SemaphoreType.DMA((n_chan,)),
            pltpu.SemaphoreType.DMA((n_chan,)),
            pltpu.VMEM((n_chan, 16, nsrc), jnp.float32),
            pltpu.VMEM((16, nsrc), jnp.float32),
            pltpu.SemaphoreType.DMA((n_chan,)),
            pltpu.SemaphoreType.DMA((n_chan,)),
            pltpu.VMEM((n_chan, 16, nsrc), jnp.float32),
        ],
        compiler_params=pltpu.CompilerParams(collective_id=0, has_side_effects=True),
    )(offsets, record, dead, sources)


def shards(record, offsets, dead_mask, sources):
    n_tm = lax.axis_size("tm")
    n_chan = lax.axis_size("chan")
    bins_dev = F // n_tm
    channels, span = record.shape
    first, count = window_plan(n_tm, span)
    per = NWIN * 2 * bins_dev // n_chan
    assert per * n_chan == NWIN * 2 * bins_dev and bins_dev % per == 0 and per <= 16
    white, rotated, source_spec = fused_exchange(
        offsets, record, dead_mask.reshape(1, channels), sources.reshape(1, -1),
        n_tm, n_chan, bins_dev, first, count
    )
    return cross_spectra(source_spec, white, rotated)


def solution(mesh):
    return jax.shard_map(
        shards,
        mesh=mesh,
        in_specs=(P("chan", "tm"), P(), P("chan"), P()),
        out_specs=P("tm", None, None, "chan"),
        check_vma=False,
    )
```

```python
import functools
import math

import jax
import jax.numpy as jnp
from jax import lax
from jax.experimental import pallas as pl
from jax.experimental.pallas import tpu as pltpu
from jax.sharding import PartitionSpec as P

W = 12000
F = 640
FLO = 6
NWIN = 4
SLOTS = 2
FA = 64

MESH = pl.DeviceIdType.MESH


def window_plan(n_tm, span):
    total = n_tm * span
    slack = total - NWIN * W
    lows = [0] + [w * W for w in range(1, NWIN - 1)] + [total - W]
    highs = [0] + [w * W + slack for w in range(1, NWIN - 1)] + [total - W]
    first, count = [], []
    for d in range(n_tm):
        meets = [w for w in range(NWIN) if lows[w] < (d + 1) * span and highs[w] + W > d * span]
        assert meets and meets == list(range(meets[0], meets[0] + len(meets)))
        assert len(meets) <= SLOTS
        first.append(meets[0])
        count.append(len(meets))
    return first, count


def _cross_kernel(bins_dev, src_ref, white_ref, rot_ref, out_ref):
    for k in range(bins_dev):
        left = src_ref[k].astype(jnp.bfloat16)
        for p, right_ref in enumerate((white_ref, rot_ref)):
            out_ref[k, p] = lax.dot_general(
                left, right_ref[k].astype(jnp.bfloat16), (((0,), (0,)), ((), ())),
                preferred_element_type=jnp.float32,
            ) / NWIN


def cross_spectra(source_spec, white, rotated):
    bins_dev, _, nsrc = source_spec.shape
    channels = white.shape[2]
    vmem = pl.BlockSpec(memory_space=pltpu.VMEM)
    return pl.pallas_call(
        functools.partial(_cross_kernel, bins_dev),
        out_shape=jax.ShapeDtypeStruct((bins_dev, 2, nsrc, channels), jnp.float32),
        in_specs=[vmem] * 3,
        out_specs=vmem,
    )(source_spec, white, rotated)


def _any_of(me, members):
    hit = jnp.bool_(False)
    for m in members:
        hit = hit | (me == m)
    return hit


def _fused_kernel(n_tm, n_chan, bins_dev, first, count,
                  offsets_ref, record_ref, dead_ref, sources_ref,
                  white_ref, rot_ref, srcspec_ref,
                  ar_ref, ai_ref, c1_ref, c2_ref, x_ref,
                  blocks_ref, lhs, recv, spec, lvl_send, lvl_recv, src_send,
                  a2a_send_sem, a2a_recv_sem, lvl_send_sem, lvl_recv_sem,
                  src_send_sem, src_recv_sem, rs_recv, ag_send, ag_send_sem, ag_recv_sem,
                  ag_recv):
    me = lax.axis_index("tm")
    mc = lax.axis_index("chan")
    two = [d for d in range(n_tm) if count[d] == 2]
    me_two = _any_of(me, two)
    rows = 2 * bins_dev
    group = lhs.shape[0] // rows

    barrier = pltpu.get_barrier_semaphore()
    for i in range(1, n_tm):
        pl.semaphore_signal(barrier, inc=1, device_id={"tm": lax.rem(me + i, n_tm)},
                            device_id_type=MESH)
    for i in range(1, n_chan):
        pl.semaphore_signal(barrier, inc=1, device_id={"chan": lax.rem(mc + i, n_chan)},
                            device_id_type=MESH)

    span = record_ref.shape[1]
    wa = jnp.int32(0)
    for d in range(n_tm):
        wa = jnp.where(me == d, first[d], wa)
    local_times = me * span + lax.broadcasted_iota(jnp.int32, (1, span), 1)
    coarse = FLO + bins_dev * lax.broadcasted_iota(jnp.int32, (n_tm, 1), 0)
    fine_row = lax.broadcasted_iota(jnp.int32, (2 * bins_dev, 1), 0)
    fine = lax.rem(fine_row, bins_dev)
    scale = 2.0 * math.pi / W

    def prepare(slot):
        window = wa + slot
        origin = offsets_ref[jnp.minimum(window, NWIN - 1)]
        shifted = local_times - origin
        inside = (shifted >= 0) & (shifted < W) & (window < NWIN)
        times = jnp.where(inside, shifted, 0)
        angle = lax.rem(coarse * times, W).astype(jnp.float32) * scale
        ar_ref[slot] = jnp.cos(angle)
        ai_ref[slot] = -jnp.sin(angle)
        angle = lax.rem(fine * times, W).astype(jnp.float32) * scale
        cos, sin = jnp.cos(angle), jnp.sin(angle)
        top = fine_row < bins_dev
        c1_ref[slot] = jnp.where(top, cos, -sin)
        c2_ref[slot] = jnp.where(top, sin, cos)
        x_ref[slot] = jnp.where(inside, record_ref[...], jnp.zeros_like(record_ref[...]))

    prepare(0)

    @pl.when(me_two)
    def _():
        prepare(1)

    def a2a(peer, slot, src_dev):
        return pltpu.make_async_remote_copy(
            src_ref=blocks_ref.at[peer, slot],
            dst_ref=recv.at[src_dev, slot],
            send_sem=a2a_send_sem.at[peer, slot],
            recv_sem=a2a_recv_sem.at[src_dev, slot],
            device_id={"tm": peer},
            device_id_type=MESH,
        )

    def compute(g, slot):
        c1 = c1_ref[slot]
        c2 = c2_ref[slot]
        for dd in range(group):
            d = lax.rem(me + g * group + dd, n_tm)
            ar = ar_ref[slot, pl.ds(d, 1), :]
            ai = ai_ref[slot, pl.ds(d, 1), :]
            lhs[dd * rows:(dd + 1) * rows, :] = ar * c1 + ai * c2
        res = lax.dot_general(
            lhs[...].astype(jnp.bfloat16), x_ref[slot], (((1,), (1,)), ((), ())),
            preferred_element_type=jnp.float32,
        )
        for dd in range(group):
            d = lax.rem(me + g * group + dd, n_tm)
            blocks_ref[d, slot] = res[dd * rows:(dd + 1) * rows, :]

    def send(g, slot):
        for dd in range(group):
            if g == 0 and dd == 0:
                continue
            a2a(lax.rem(me + g * group + dd, n_tm), slot, me).start()

    for g in range(n_tm // group):
        compute(g, 0)
        if g == 0:
            pl.semaphore_wait(barrier, n_tm - 1 + n_chan - 1)
        send(g, 0)

        @pl.when(me_two)
        def _():
            compute(g, 1)
            send(g, 1)

    recv[me, 0] = blocks_ref[me, 0]

    @pl.when(me_two)
    def _():
        recv[me, 1] = blocks_ref[me, 1]

    for i in range(1, n_tm):
        peer = lax.rem(me + i, n_tm)
        a2a(peer, 0, me).wait_send()

        @pl.when(me_two)
        def _():
            a2a(peer, 1, me).wait_send()

    for s in range(n_tm):
        @pl.when(me != s)
        def _():
            a2a(s, 0, s).wait_recv()
            if count[s] == 2:
                a2a(s, 1, s).wait_recv()

    for w in range(NWIN):
        acc = None
        for s in range(n_tm):
            for j in range(count[s]):
                if first[s] + j == w:
                    part = recv[s, j]
                    acc = part if acc is None else acc + part
        spec[w] = acc

    rows = []
    for w in range(NWIN):
        re = spec[w, 0:bins_dev, :]
        im = spec[w, bins_dev:2 * bins_dev, :]
        mag = jnp.sqrt(re * re + im * im)
        rows.append(jnp.sum(mag, axis=0, keepdims=True))
    rows.append(jnp.zeros((8 - NWIN, rows[0].shape[1]), jnp.float32))
    lvl_send[...] = jnp.concatenate(rows, axis=0)

    def lvl(peer, src_dev):
        return pltpu.make_async_remote_copy(
            src_ref=lvl_send,
            dst_ref=lvl_recv.at[src_dev],
            send_sem=lvl_send_sem.at[peer],
            recv_sem=lvl_recv_sem.at[src_dev],
            device_id={"tm": peer},
            device_id_type=MESH,
        )

    for i in range(1, n_tm):
        lvl(lax.rem(me + i, n_tm), me).start()
    lvl_recv[me] = lvl_send[...]
    for i in range(1, n_tm):
        lvl(lax.rem(me + i, n_tm), me).wait_send()
    for i in range(1, n_tm):
        src = lax.rem(me + n_tm - i, n_tm)
        lvl(src, src).wait_recv()

    level = lvl_recv[0]
    for s in range(1, n_tm):
        level = level + lvl_recv[s]
    level = level / F

    mask = dead_ref[...].astype(jnp.float32)
    channels = record_ref.shape[0]
    local_index = sources_ref[...] - mc * channels
    onehot = (lax.broadcasted_iota(jnp.int32, (channels, local_index.shape[1]), 0)
              == local_index).astype(jnp.bfloat16)
    per = NWIN * 2 * bins_dev // n_chan
    halves = bins_dev // per
    src_send[...] = jnp.zeros_like(src_send)
    for w in range(NWIN):
        re = spec[w, 0:bins_dev, :]
        im = spec[w, bins_dev:2 * bins_dev, :]
        mag = jnp.sqrt(re * re + im * im)
        den = mag + 0.1 * level[w:w + 1, :] + 1e-06
        for p, part in enumerate((re, im)):
            white = (part / den).astype(jnp.bfloat16).astype(jnp.float32) * mask
            for k in range(bins_dev):
                white_ref[k, 2 * w + p:2 * w + p + 1, :] = white[k:k + 1, :]
                if p == 0:
                    rot_ref[k, 2 * w + 1:2 * w + 2, :] = -white[k:k + 1, :]
                else:
                    rot_ref[k, 2 * w:2 * w + 1, :] = white[k:k + 1, :]
            picked = jnp.dot(
                white.astype(jnp.bfloat16), onehot, preferred_element_type=jnp.float32
            )
            for h in range(halves):
                src_send[(2 * w + p) * halves + h, 0:per, :] = picked[h * per:(h + 1) * per, :]

    def rsc(peer, src_dev):
        return pltpu.make_async_remote_copy(
            src_ref=src_send.at[peer],
            dst_ref=rs_recv.at[src_dev],
            send_sem=src_send_sem.at[peer],
            recv_sem=src_recv_sem.at[src_dev],
            device_id={"chan": peer},
            device_id_type=MESH,
        )

    for i in range(1, n_chan):
        rsc(lax.rem(mc + i, n_chan), mc).start()
    rs_recv[mc] = src_send[mc]
    for i in range(1, n_chan):
        rsc(lax.rem(mc + i, n_chan), mc).wait_send()
    for i in range(1, n_chan):
        src = lax.rem(mc + n_chan - i, n_chan)
        rsc(src, src).wait_recv()

    total = rs_recv[0]
    for s in range(1, n_chan):
        total = total + rs_recv[s]
    ag_send[...] = total

    def agc(peer, src_dev):
        return pltpu.make_async_remote_copy(
            src_ref=ag_send,
            dst_ref=ag_recv.at[src_dev],
            send_sem=ag_send_sem.at[peer],
            recv_sem=ag_recv_sem.at[src_dev],
            device_id={"chan": peer},
            device_id_type=MESH,
        )

    for i in range(1, n_chan):
        agc(lax.rem(mc + i, n_chan), mc).start()
    ag_recv[mc] = ag_send[...]
    for i in range(1, n_chan):
        agc(lax.rem(mc + i, n_chan), mc).wait_send()
    for i in range(1, n_chan):
        src = lax.rem(mc + n_chan - i, n_chan)
        agc(src, src).wait_recv()

    for i in range(NWIN * 2):
        for h in range(halves):
            for r in range(per):
                k = h * per + r
                srcspec_ref[k, i:i + 1, :] = ag_recv[i * halves + h, r:r + 1, :]


def fused_exchange(offsets, record, dead, sources, n_tm, n_chan, bins_dev, first, count):
    channels, span = record.shape
    nsrc = sources.shape[1]
    group = 16
    vmem = pl.BlockSpec(memory_space=pltpu.VMEM)
    return pl.pallas_call(
        functools.partial(_fused_kernel, n_tm, n_chan, bins_dev, first, count),
        out_shape=(
            jax.ShapeDtypeStruct((bins_dev, NWIN * 2, channels), jnp.float32),
            jax.ShapeDtypeStruct((bins_dev, NWIN * 2, channels), jnp.float32),
            jax.ShapeDtypeStruct((bins_dev, NWIN * 2, nsrc), jnp.float32),
        ),
        in_specs=[pl.BlockSpec(memory_space=pltpu.SMEM), vmem, vmem, vmem],
        out_specs=(vmem, vmem, vmem),
        scratch_shapes=[
            pltpu.VMEM((SLOTS, n_tm, span), jnp.float32),
            pltpu.VMEM((SLOTS, n_tm, span), jnp.float32),
            pltpu.VMEM((SLOTS, 2 * bins_dev, span), jnp.float32),
            pltpu.VMEM((SLOTS, 2 * bins_dev, span), jnp.float32),
            pltpu.VMEM((SLOTS, channels, span), jnp.bfloat16),
            pltpu.VMEM((n_tm, SLOTS, 2 * bins_dev, channels), jnp.float32),
            pltpu.VMEM((group * 2 * bins_dev, span), jnp.float32),
            pltpu.VMEM((n_tm, SLOTS, 2 * bins_dev, channels), jnp.float32),
            pltpu.VMEM((NWIN, 2 * bins_dev, channels), jnp.float32),
            pltpu.VMEM((8, channels), jnp.float32),
            pltpu.VMEM((n_tm, 8, channels), jnp.float32),
            pltpu.VMEM((n_chan, 16, nsrc), jnp.float32),
            pltpu.SemaphoreType.DMA((n_tm, SLOTS)),
            pltpu.SemaphoreType.DMA((n_tm, SLOTS)),
            pltpu.SemaphoreType.DMA((n_tm,)),
            pltpu.SemaphoreType.DMA((n_tm,)),
            pltpu.SemaphoreType.DMA((n_chan,)),
            pltpu.SemaphoreType.DMA((n_chan,)),
            pltpu.VMEM((n_chan, 16, nsrc), jnp.float32),
            pltpu.VMEM((16, nsrc), jnp.float32),
            pltpu.SemaphoreType.DMA((n_chan,)),
            pltpu.SemaphoreType.DMA((n_chan,)),
            pltpu.VMEM((n_chan, 16, nsrc), jnp.float32),
        ],
        compiler_params=pltpu.CompilerParams(collective_id=0, has_side_effects=True),
    )(offsets, record, dead, sources)


def shards(record, offsets, dead_mask, sources):
    n_tm = lax.axis_size("tm")
    n_chan = lax.axis_size("chan")
    bins_dev = F // n_tm
    channels, span = record.shape
    first, count = window_plan(n_tm, span)
    per = NWIN * 2 * bins_dev // n_chan
    assert per * n_chan == NWIN * 2 * bins_dev and bins_dev % per == 0 and per <= 16
    white, rotated, source_spec = fused_exchange(
        offsets, record, dead_mask.reshape(1, channels), sources.reshape(1, -1),
        n_tm, n_chan, bins_dev, first, count
    )
    return cross_spectra(source_spec, white, rotated)


def solution(mesh):
    return jax.shard_map(
        shards,
        mesh=mesh,
        in_specs=(P("chan", "tm"), P(), P("chan"), P()),
        out_specs=P("tm", None, None, "chan"),
        check_vma=False,
    )
```

```python
import functools
import math

import jax
import jax.numpy as jnp
from jax import lax
from jax.experimental import pallas as pl
from jax.experimental.pallas import tpu as pltpu
from jax.sharding import PartitionSpec as P

W = 12000
F = 640
FLO = 6
NWIN = 4
SLOTS = 2
FA = 64

MESH = pl.DeviceIdType.MESH


def window_plan(n_tm, span):
    total = n_tm * span
    slack = total - NWIN * W
    lows = [0] + [w * W for w in range(1, NWIN - 1)] + [total - W]
    highs = [0] + [w * W + slack for w in range(1, NWIN - 1)] + [total - W]
    first, count = [], []
    for d in range(n_tm):
        meets = [w for w in range(NWIN) if lows[w] < (d + 1) * span and highs[w] + W > d * span]
        assert meets and meets == list(range(meets[0], meets[0] + len(meets)))
        assert len(meets) <= SLOTS
        first.append(meets[0])
        count.append(len(meets))
    return first, count


def _cross_kernel(bins_dev, src_ref, white_ref, rot_ref, out_ref):
    for k in range(bins_dev):
        left = src_ref[k].astype(jnp.bfloat16)
        for p, right_ref in enumerate((white_ref, rot_ref)):
            out_ref[k, p] = lax.dot_general(
                left, right_ref[k].astype(jnp.bfloat16), (((0,), (0,)), ((), ())),
                preferred_element_type=jnp.float32,
            ) / NWIN


def cross_spectra(source_spec, white, rotated):
    bins_dev, _, nsrc = source_spec.shape
    channels = white.shape[2]
    vmem = pl.BlockSpec(memory_space=pltpu.VMEM)
    return pl.pallas_call(
        functools.partial(_cross_kernel, bins_dev),
        out_shape=jax.ShapeDtypeStruct((bins_dev, 2, nsrc, channels), jnp.float32),
        in_specs=[vmem] * 3,
        out_specs=vmem,
    )(source_spec, white, rotated)


def _any_of(me, members):
    hit = jnp.bool_(False)
    for m in members:
        hit = hit | (me == m)
    return hit


def _fused_kernel(n_tm, n_chan, bins_dev, first, count,
                  offsets_ref, record_ref, dead_ref, sources_ref,
                  white_ref, rot_ref, srcspec_ref,
                  ar_ref, ai_ref, c1_ref, c2_ref, x_ref,
                  blocks_ref, lhs, recv, spec, lvl_send, lvl_recv, src_send,
                  a2a_send_sem, a2a_recv_sem, lvl_send_sem, lvl_recv_sem,
                  src_send_sem, src_recv_sem, rs_recv, ag_send, ag_send_sem, ag_recv_sem,
                  ag_recv):
    me = lax.axis_index("tm")
    mc = lax.axis_index("chan")
    two = [d for d in range(n_tm) if count[d] == 2]
    me_two = _any_of(me, two)
    rows = 2 * bins_dev
    group = lhs.shape[0] // rows

    barrier = pltpu.get_barrier_semaphore()
    for i in range(1, n_tm):
        pl.semaphore_signal(barrier, inc=1, device_id={"tm": lax.rem(me + i, n_tm)},
                            device_id_type=MESH)
    for i in range(1, n_chan):
        pl.semaphore_signal(barrier, inc=1, device_id={"chan": lax.rem(mc + i, n_chan)},
                            device_id_type=MESH)

    span = record_ref.shape[1]
    wa = jnp.int32(0)
    for d in range(n_tm):
        wa = jnp.where(me == d, first[d], wa)
    local_times = me * span + lax.broadcasted_iota(jnp.int32, (1, span), 1)
    coarse = FLO + bins_dev * lax.broadcasted_iota(jnp.int32, (n_tm, 1), 0)
    fine_row = lax.broadcasted_iota(jnp.int32, (2 * bins_dev, 1), 0)
    fine = lax.rem(fine_row, bins_dev)
    scale = 2.0 * math.pi / W

    def prepare(slot):
        window = wa + slot
        origin = offsets_ref[jnp.minimum(window, NWIN - 1)]
        shifted = local_times - origin
        inside = (shifted >= 0) & (shifted < W) & (window < NWIN)
        times = jnp.where(inside, shifted, 0)
        angle = lax.rem(coarse * times, W).astype(jnp.float32) * scale
        ar_ref[slot] = jnp.cos(angle)
        ai_ref[slot] = -jnp.sin(angle)
        angle = lax.rem(fine * times, W).astype(jnp.float32) * scale
        cos, sin = jnp.cos(angle), jnp.sin(angle)
        top = fine_row < bins_dev
        c1_ref[slot] = jnp.where(top, cos, -sin)
        c2_ref[slot] = jnp.where(top, sin, cos)
        x_ref[slot] = jnp.where(inside, record_ref[...], jnp.zeros_like(record_ref[...]))

    prepare(0)

    @pl.when(me_two)
    def _():
        prepare(1)

    def a2a(peer, slot, src_dev):
        return pltpu.make_async_remote_copy(
            src_ref=blocks_ref.at[peer, slot],
            dst_ref=recv.at[src_dev, slot],
            send_sem=a2a_send_sem.at[peer, slot],
            recv_sem=a2a_recv_sem.at[src_dev, slot],
            device_id={"tm": peer},
            device_id_type=MESH,
        )

    def compute(g, slot):
        c1 = c1_ref[slot]
        c2 = c2_ref[slot]
        for dd in range(group):
            d = lax.rem(me + g * group + dd, n_tm)
            ar = ar_ref[slot, pl.ds(d, 1), :]
            ai = ai_ref[slot, pl.ds(d, 1), :]
            lhs[dd * rows:(dd + 1) * rows, :] = ar * c1 + ai * c2
        res = lax.dot_general(
            lhs[...].astype(jnp.bfloat16), x_ref[slot], (((1,), (1,)), ((), ())),
            preferred_element_type=jnp.float32,
        )
        for dd in range(group):
            d = lax.rem(me + g * group + dd, n_tm)
            blocks_ref[d, slot] = res[dd * rows:(dd + 1) * rows, :]

    def send(g, slot):
        for dd in range(group):
            if g == 0 and dd == 0:
                continue
            a2a(lax.rem(me + g * group + dd, n_tm), slot, me).start()

    for g in range(n_tm // group):
        compute(g, 0)
        if g == 0:
            pl.semaphore_wait(barrier, n_tm - 1 + n_chan - 1)
        send(g, 0)

        @pl.when(me_two)
        def _():
            compute(g, 1)
            send(g, 1)

    recv[me, 0] = blocks_ref[me, 0]

    @pl.when(me_two)
    def _():
        recv[me, 1] = blocks_ref[me, 1]

    for i in range(1, n_tm):
        peer = lax.rem(me + i, n_tm)
        a2a(peer, 0, me).wait_send()

        @pl.when(me_two)
        def _():
            a2a(peer, 1, me).wait_send()

    for s in range(n_tm):
        @pl.when(me != s)
        def _():
            a2a(s, 0, s).wait_recv()
            if count[s] == 2:
                a2a(s, 1, s).wait_recv()

    for w in range(NWIN):
        acc = None
        for s in range(n_tm):
            for j in range(count[s]):
                if first[s] + j == w:
                    part = recv[s, j]
                    acc = part if acc is None else acc + part
        spec[w] = acc

    rows = []
    for w in range(NWIN):
        re = spec[w, 0:bins_dev, :]
        im = spec[w, bins_dev:2 * bins_dev, :]
        mag = jnp.sqrt(re * re + im * im)
        rows.append(jnp.sum(mag, axis=0, keepdims=True))
    rows.append(jnp.zeros((8 - NWIN, rows[0].shape[1]), jnp.float32))
    lvl_send[...] = jnp.concatenate(rows, axis=0)

    def lvl(peer, src_dev):
        return pltpu.make_async_remote_copy(
            src_ref=lvl_send,
            dst_ref=lvl_recv.at[src_dev],
            send_sem=lvl_send_sem.at[peer],
            recv_sem=lvl_recv_sem.at[src_dev],
            device_id={"tm": peer},
            device_id_type=MESH,
        )

    for i in range(1, n_tm):
        lvl(lax.rem(me + i, n_tm), me).start()
    lvl_recv[me] = lvl_send[...]
    for i in range(1, n_tm):
        lvl(lax.rem(me + i, n_tm), me).wait_send()
    for i in range(1, n_tm):
        src = lax.rem(me + n_tm - i, n_tm)
        lvl(src, src).wait_recv()

    level = lvl_recv[0]
    for s in range(1, n_tm):
        level = level + lvl_recv[s]
    level = level / F

    mask = dead_ref[...].astype(jnp.float32)
    channels = record_ref.shape[0]
    local_index = sources_ref[...] - mc * channels
    onehot = (lax.broadcasted_iota(jnp.int32, (channels, local_index.shape[1]), 0)
              == local_index).astype(jnp.bfloat16)
    per = NWIN * 2 * bins_dev // n_chan
    halves = bins_dev // per
    src_send[...] = jnp.zeros_like(src_send)
    for w in range(NWIN):
        re = spec[w, 0:bins_dev, :]
        im = spec[w, bins_dev:2 * bins_dev, :]
        mag = jnp.sqrt(re * re + im * im)
        den = mag + 0.1 * level[w:w + 1, :] + 1e-06
        for p, part in enumerate((re, im)):
            white = (part / den).astype(jnp.bfloat16).astype(jnp.float32) * mask
            for k in range(bins_dev):
                white_ref[k, 2 * w + p:2 * w + p + 1, :] = white[k:k + 1, :]
                if p == 0:
                    rot_ref[k, 2 * w + 1:2 * w + 2, :] = -white[k:k + 1, :]
                else:
                    rot_ref[k, 2 * w:2 * w + 1, :] = white[k:k + 1, :]
            picked = jnp.dot(
                white.astype(jnp.bfloat16), onehot, preferred_element_type=jnp.float32
            )
            for h in range(halves):
                src_send[(2 * w + p) * halves + h, 0:per, :] = picked[h * per:(h + 1) * per, :]

    def rsc(peer, src_dev):
        return pltpu.make_async_remote_copy(
            src_ref=src_send.at[peer],
            dst_ref=rs_recv.at[src_dev],
            send_sem=src_send_sem.at[peer],
            recv_sem=src_recv_sem.at[src_dev],
            device_id={"chan": peer},
            device_id_type=MESH,
        )

    for i in range(1, n_chan):
        rsc(lax.rem(mc + i, n_chan), mc).start()
    rs_recv[mc] = src_send[mc]
    for i in range(1, n_chan):
        rsc(lax.rem(mc + i, n_chan), mc).wait_send()
    for i in range(1, n_chan):
        src = lax.rem(mc + n_chan - i, n_chan)
        rsc(src, src).wait_recv()

    total = rs_recv[0]
    for s in range(1, n_chan):
        total = total + rs_recv[s]
    ag_send[...] = total

    def agc(peer, src_dev):
        return pltpu.make_async_remote_copy(
            src_ref=ag_send,
            dst_ref=ag_recv.at[src_dev],
            send_sem=ag_send_sem.at[peer],
            recv_sem=ag_recv_sem.at[src_dev],
            device_id={"chan": peer},
            device_id_type=MESH,
        )

    for i in range(1, n_chan):
        agc(lax.rem(mc + i, n_chan), mc).start()
    ag_recv[mc] = ag_send[...]
    for i in range(1, n_chan):
        agc(lax.rem(mc + i, n_chan), mc).wait_send()
    for i in range(1, n_chan):
        src = lax.rem(mc + n_chan - i, n_chan)
        agc(src, src).wait_recv()

    for i in range(NWIN * 2):
        for h in range(halves):
            for r in range(per):
                k = h * per + r
                srcspec_ref[k, i:i + 1, :] = ag_recv[i * halves + h, r:r + 1, :]


def fused_exchange(offsets, record, dead, sources, n_tm, n_chan, bins_dev, first, count):
    channels, span = record.shape
    nsrc = sources.shape[1]
    group = 32
    vmem = pl.BlockSpec(memory_space=pltpu.VMEM)
    return pl.pallas_call(
        functools.partial(_fused_kernel, n_tm, n_chan, bins_dev, first, count),
        out_shape=(
            jax.ShapeDtypeStruct((bins_dev, NWIN * 2, channels), jnp.float32),
            jax.ShapeDtypeStruct((bins_dev, NWIN * 2, channels), jnp.float32),
            jax.ShapeDtypeStruct((bins_dev, NWIN * 2, nsrc), jnp.float32),
        ),
        in_specs=[pl.BlockSpec(memory_space=pltpu.SMEM), vmem, vmem, vmem],
        out_specs=(vmem, vmem, vmem),
        scratch_shapes=[
            pltpu.VMEM((SLOTS, n_tm, span), jnp.float32),
            pltpu.VMEM((SLOTS, n_tm, span), jnp.float32),
            pltpu.VMEM((SLOTS, 2 * bins_dev, span), jnp.float32),
            pltpu.VMEM((SLOTS, 2 * bins_dev, span), jnp.float32),
            pltpu.VMEM((SLOTS, channels, span), jnp.bfloat16),
            pltpu.VMEM((n_tm, SLOTS, 2 * bins_dev, channels), jnp.float32),
            pltpu.VMEM((group * 2 * bins_dev, span), jnp.float32),
            pltpu.VMEM((n_tm, SLOTS, 2 * bins_dev, channels), jnp.float32),
            pltpu.VMEM((NWIN, 2 * bins_dev, channels), jnp.float32),
            pltpu.VMEM((8, channels), jnp.float32),
            pltpu.VMEM((n_tm, 8, channels), jnp.float32),
            pltpu.VMEM((n_chan, 16, nsrc), jnp.float32),
            pltpu.SemaphoreType.DMA((n_tm, SLOTS)),
            pltpu.SemaphoreType.DMA((n_tm, SLOTS)),
            pltpu.SemaphoreType.DMA((n_tm,)),
            pltpu.SemaphoreType.DMA((n_tm,)),
            pltpu.SemaphoreType.DMA((n_chan,)),
            pltpu.SemaphoreType.DMA((n_chan,)),
            pltpu.VMEM((n_chan, 16, nsrc), jnp.float32),
            pltpu.VMEM((16, nsrc), jnp.float32),
            pltpu.SemaphoreType.DMA((n_chan,)),
            pltpu.SemaphoreType.DMA((n_chan,)),
            pltpu.VMEM((n_chan, 16, nsrc), jnp.float32),
        ],
        compiler_params=pltpu.CompilerParams(collective_id=0, has_side_effects=True),
    )(offsets, record, dead, sources)


def shards(record, offsets, dead_mask, sources):
    n_tm = lax.axis_size("tm")
    n_chan = lax.axis_size("chan")
    bins_dev = F // n_tm
    channels, span = record.shape
    first, count = window_plan(n_tm, span)
    per = NWIN * 2 * bins_dev // n_chan
    assert per * n_chan == NWIN * 2 * bins_dev and bins_dev % per == 0 and per <= 16
    white, rotated, source_spec = fused_exchange(
        offsets, record, dead_mask.reshape(1, channels), sources.reshape(1, -1),
        n_tm, n_chan, bins_dev, first, count
    )
    return cross_spectra(source_spec, white, rotated)


def solution(mesh):
    return jax.shard_map(
        shards,
        mesh=mesh,
        in_specs=(P("chan", "tm"), P(), P("chan"), P()),
        out_specs=P("tm", None, None, "chan"),
        check_vma=False,
    )
```

```python
import functools
import math

import jax
import jax.numpy as jnp
from jax import lax
from jax.experimental import pallas as pl
from jax.experimental.pallas import tpu as pltpu
from jax.sharding import PartitionSpec as P

W = 12000
F = 640
FLO = 6
NWIN = 4
SLOTS = 2
FA = 64

MESH = pl.DeviceIdType.MESH


def window_plan(n_tm, span):
    total = n_tm * span
    slack = total - NWIN * W
    lows = [0] + [w * W for w in range(1, NWIN - 1)] + [total - W]
    highs = [0] + [w * W + slack for w in range(1, NWIN - 1)] + [total - W]
    first, count = [], []
    for d in range(n_tm):
        meets = [w for w in range(NWIN) if lows[w] < (d + 1) * span and highs[w] + W > d * span]
        assert meets and meets == list(range(meets[0], meets[0] + len(meets)))
        assert len(meets) <= SLOTS
        first.append(meets[0])
        count.append(len(meets))
    return first, count


def _cross_kernel(src_ref, white_ref, rot_ref, out_ref):
    left = src_ref[0].astype(jnp.bfloat16)
    for p, right_ref in enumerate((white_ref, rot_ref)):
        out_ref[0, p] = lax.dot_general(
            left, right_ref[0].astype(jnp.bfloat16), (((0,), (0,)), ((), ())),
            preferred_element_type=jnp.float32,
        ) / NWIN


def cross_spectra(source_spec, white, rotated):
    bins_dev, rows, nsrc = source_spec.shape
    channels = white.shape[2]
    return pl.pallas_call(
        _cross_kernel,
        out_shape=jax.ShapeDtypeStruct((bins_dev, 2, nsrc, channels), jnp.float32),
        grid=(bins_dev,),
        in_specs=[
            pl.BlockSpec((1, rows, nsrc), lambda k: (k, 0, 0)),
            pl.BlockSpec((1, rows, channels), lambda k: (k, 0, 0)),
            pl.BlockSpec((1, rows, channels), lambda k: (k, 0, 0)),
        ],
        out_specs=pl.BlockSpec((1, 2, nsrc, channels), lambda k: (k, 0, 0, 0)),
    )(source_spec, white, rotated)


def _any_of(me, members):
    hit = jnp.bool_(False)
    for m in members:
        hit = hit | (me == m)
    return hit


def _fused_kernel(n_tm, n_chan, bins_dev, first, count,
                  offsets_ref, record_ref, dead_ref, sources_ref,
                  white_ref, rot_ref, srcspec_ref,
                  ar_ref, ai_ref, c1_ref, c2_ref, x_ref,
                  blocks_ref, lhs, recv, spec, lvl_send, lvl_recv, src_send,
                  a2a_send_sem, a2a_recv_sem, lvl_send_sem, lvl_recv_sem,
                  src_send_sem, src_recv_sem, rs_recv, ag_send, ag_send_sem, ag_recv_sem,
                  ag_recv):
    me = lax.axis_index("tm")
    mc = lax.axis_index("chan")
    two = [d for d in range(n_tm) if count[d] == 2]
    me_two = _any_of(me, two)
    rows = 2 * bins_dev
    group = lhs.shape[0] // rows

    barrier = pltpu.get_barrier_semaphore()
    for i in range(1, n_tm):
        pl.semaphore_signal(barrier, inc=1, device_id={"tm": lax.rem(me + i, n_tm)},
                            device_id_type=MESH)
    for i in range(1, n_chan):
        pl.semaphore_signal(barrier, inc=1, device_id={"chan": lax.rem(mc + i, n_chan)},
                            device_id_type=MESH)

    span = record_ref.shape[1]
    wa = jnp.int32(0)
    for d in range(n_tm):
        wa = jnp.where(me == d, first[d], wa)
    local_times = me * span + lax.broadcasted_iota(jnp.int32, (1, span), 1)
    coarse = FLO + bins_dev * lax.broadcasted_iota(jnp.int32, (n_tm, 1), 0)
    fine_row = lax.broadcasted_iota(jnp.int32, (2 * bins_dev, 1), 0)
    fine = lax.rem(fine_row, bins_dev)
    scale = 2.0 * math.pi / W

    def prepare(slot):
        window = wa + slot
        origin = offsets_ref[jnp.minimum(window, NWIN - 1)]
        shifted = local_times - origin
        inside = (shifted >= 0) & (shifted < W) & (window < NWIN)
        times = jnp.where(inside, shifted, 0)
        angle = lax.rem(coarse * times, W).astype(jnp.float32) * scale
        ar_ref[slot] = jnp.cos(angle)
        ai_ref[slot] = -jnp.sin(angle)
        angle = lax.rem(fine * times, W).astype(jnp.float32) * scale
        cos, sin = jnp.cos(angle), jnp.sin(angle)
        top = fine_row < bins_dev
        c1_ref[slot] = jnp.where(top, cos, -sin)
        c2_ref[slot] = jnp.where(top, sin, cos)
        x_ref[slot] = jnp.where(inside, record_ref[...], jnp.zeros_like(record_ref[...]))

    prepare(0)

    @pl.when(me_two)
    def _():
        prepare(1)

    def a2a(peer, slot, src_dev):
        return pltpu.make_async_remote_copy(
            src_ref=blocks_ref.at[peer, slot],
            dst_ref=recv.at[src_dev, slot],
            send_sem=a2a_send_sem.at[peer, slot],
            recv_sem=a2a_recv_sem.at[src_dev, slot],
            device_id={"tm": peer},
            device_id_type=MESH,
        )

    def compute(g, slot):
        c1 = c1_ref[slot]
        c2 = c2_ref[slot]
        for dd in range(group):
            d = lax.rem(me + g * group + dd, n_tm)
            ar = ar_ref[slot, pl.ds(d, 1), :]
            ai = ai_ref[slot, pl.ds(d, 1), :]
            lhs[dd * rows:(dd + 1) * rows, :] = ar * c1 + ai * c2
        res = lax.dot_general(
            lhs[...].astype(jnp.bfloat16), x_ref[slot], (((1,), (1,)), ((), ())),
            preferred_element_type=jnp.float32,
        )
        for dd in range(group):
            d = lax.rem(me + g * group + dd, n_tm)
            blocks_ref[d, slot] = res[dd * rows:(dd + 1) * rows, :]

    def send(g, slot):
        for dd in range(group):
            if g == 0 and dd == 0:
                continue
            a2a(lax.rem(me + g * group + dd, n_tm), slot, me).start()

    for g in range(n_tm // group):
        compute(g, 0)
        if g == 0:
            pl.semaphore_wait(barrier, n_tm - 1 + n_chan - 1)
        send(g, 0)

        @pl.when(me_two)
        def _():
            compute(g, 1)
            send(g, 1)

    recv[me, 0] = blocks_ref[me, 0]

    @pl.when(me_two)
    def _():
        recv[me, 1] = blocks_ref[me, 1]

    for i in range(1, n_tm):
        peer = lax.rem(me + i, n_tm)
        a2a(peer, 0, me).wait_send()

        @pl.when(me_two)
        def _():
            a2a(peer, 1, me).wait_send()

    for s in range(n_tm):
        @pl.when(me != s)
        def _():
            a2a(s, 0, s).wait_recv()
            if count[s] == 2:
                a2a(s, 1, s).wait_recv()

    for w in range(NWIN):
        acc = None
        for s in range(n_tm):
            for j in range(count[s]):
                if first[s] + j == w:
                    part = recv[s, j]
                    acc = part if acc is None else acc + part
        spec[w] = acc

    rows = []
    for w in range(NWIN):
        re = spec[w, 0:bins_dev, :]
        im = spec[w, bins_dev:2 * bins_dev, :]
        mag = jnp.sqrt(re * re + im * im)
        rows.append(jnp.sum(mag, axis=0, keepdims=True))
    rows.append(jnp.zeros((8 - NWIN, rows[0].shape[1]), jnp.float32))
    lvl_send[...] = jnp.concatenate(rows, axis=0)

    def lvl(peer, src_dev):
        return pltpu.make_async_remote_copy(
            src_ref=lvl_send,
            dst_ref=lvl_recv.at[src_dev],
            send_sem=lvl_send_sem.at[peer],
            recv_sem=lvl_recv_sem.at[src_dev],
            device_id={"tm": peer},
            device_id_type=MESH,
        )

    for i in range(1, n_tm):
        lvl(lax.rem(me + i, n_tm), me).start()
    lvl_recv[me] = lvl_send[...]
    for i in range(1, n_tm):
        lvl(lax.rem(me + i, n_tm), me).wait_send()
    for i in range(1, n_tm):
        src = lax.rem(me + n_tm - i, n_tm)
        lvl(src, src).wait_recv()

    level = lvl_recv[0]
    for s in range(1, n_tm):
        level = level + lvl_recv[s]
    level = level / F

    mask = dead_ref[...].astype(jnp.float32)
    channels = record_ref.shape[0]
    local_index = sources_ref[...] - mc * channels
    onehot = (lax.broadcasted_iota(jnp.int32, (channels, local_index.shape[1]), 0)
              == local_index).astype(jnp.bfloat16)
    per = NWIN * 2 * bins_dev // n_chan
    halves = bins_dev // per
    src_send[...] = jnp.zeros_like(src_send)
    for w in range(NWIN):
        re = spec[w, 0:bins_dev, :]
        im = spec[w, bins_dev:2 * bins_dev, :]
        mag = jnp.sqrt(re * re + im * im)
        den = mag + 0.1 * level[w:w + 1, :] + 1e-06
        for p, part in enumerate((re, im)):
            white = (part / den).astype(jnp.bfloat16).astype(jnp.float32) * mask
            for k in range(bins_dev):
                white_ref[k, 2 * w + p:2 * w + p + 1, :] = white[k:k + 1, :]
                if p == 0:
                    rot_ref[k, 2 * w + 1:2 * w + 2, :] = -white[k:k + 1, :]
                else:
                    rot_ref[k, 2 * w:2 * w + 1, :] = white[k:k + 1, :]
            picked = jnp.dot(
                white.astype(jnp.bfloat16), onehot, preferred_element_type=jnp.float32
            )
            for h in range(halves):
                src_send[(2 * w + p) * halves + h, 0:per, :] = picked[h * per:(h + 1) * per, :]

    def rsc(peer, src_dev):
        return pltpu.make_async_remote_copy(
            src_ref=src_send.at[peer],
            dst_ref=rs_recv.at[src_dev],
            send_sem=src_send_sem.at[peer],
            recv_sem=src_recv_sem.at[src_dev],
            device_id={"chan": peer},
            device_id_type=MESH,
        )

    for i in range(1, n_chan):
        rsc(lax.rem(mc + i, n_chan), mc).start()
    rs_recv[mc] = src_send[mc]
    for i in range(1, n_chan):
        rsc(lax.rem(mc + i, n_chan), mc).wait_send()
    for i in range(1, n_chan):
        src = lax.rem(mc + n_chan - i, n_chan)
        rsc(src, src).wait_recv()

    total = rs_recv[0]
    for s in range(1, n_chan):
        total = total + rs_recv[s]
    ag_send[...] = total

    def agc(peer, src_dev):
        return pltpu.make_async_remote_copy(
            src_ref=ag_send,
            dst_ref=ag_recv.at[src_dev],
            send_sem=ag_send_sem.at[peer],
            recv_sem=ag_recv_sem.at[src_dev],
            device_id={"chan": peer},
            device_id_type=MESH,
        )

    for i in range(1, n_chan):
        agc(lax.rem(mc + i, n_chan), mc).start()
    ag_recv[mc] = ag_send[...]
    for i in range(1, n_chan):
        agc(lax.rem(mc + i, n_chan), mc).wait_send()
    for i in range(1, n_chan):
        src = lax.rem(mc + n_chan - i, n_chan)
        agc(src, src).wait_recv()

    for i in range(NWIN * 2):
        for h in range(halves):
            for r in range(per):
                k = h * per + r
                srcspec_ref[k, i:i + 1, :] = ag_recv[i * halves + h, r:r + 1, :]


def fused_exchange(offsets, record, dead, sources, n_tm, n_chan, bins_dev, first, count):
    channels, span = record.shape
    nsrc = sources.shape[1]
    group = 16
    vmem = pl.BlockSpec(memory_space=pltpu.VMEM)
    return pl.pallas_call(
        functools.partial(_fused_kernel, n_tm, n_chan, bins_dev, first, count),
        out_shape=(
            jax.ShapeDtypeStruct((bins_dev, NWIN * 2, channels), jnp.float32),
            jax.ShapeDtypeStruct((bins_dev, NWIN * 2, channels), jnp.float32),
            jax.ShapeDtypeStruct((bins_dev, NWIN * 2, nsrc), jnp.float32),
        ),
        in_specs=[pl.BlockSpec(memory_space=pltpu.SMEM), vmem, vmem, vmem],
        out_specs=(vmem, vmem, vmem),
        scratch_shapes=[
            pltpu.VMEM((SLOTS, n_tm, span), jnp.float32),
            pltpu.VMEM((SLOTS, n_tm, span), jnp.float32),
            pltpu.VMEM((SLOTS, 2 * bins_dev, span), jnp.float32),
            pltpu.VMEM((SLOTS, 2 * bins_dev, span), jnp.float32),
            pltpu.VMEM((SLOTS, channels, span), jnp.bfloat16),
            pltpu.VMEM((n_tm, SLOTS, 2 * bins_dev, channels), jnp.float32),
            pltpu.VMEM((group * 2 * bins_dev, span), jnp.float32),
            pltpu.VMEM((n_tm, SLOTS, 2 * bins_dev, channels), jnp.float32),
            pltpu.VMEM((NWIN, 2 * bins_dev, channels), jnp.float32),
            pltpu.VMEM((8, channels), jnp.float32),
            pltpu.VMEM((n_tm, 8, channels), jnp.float32),
            pltpu.VMEM((n_chan, 16, nsrc), jnp.float32),
            pltpu.SemaphoreType.DMA((n_tm, SLOTS)),
            pltpu.SemaphoreType.DMA((n_tm, SLOTS)),
            pltpu.SemaphoreType.DMA((n_tm,)),
            pltpu.SemaphoreType.DMA((n_tm,)),
            pltpu.SemaphoreType.DMA((n_chan,)),
            pltpu.SemaphoreType.DMA((n_chan,)),
            pltpu.VMEM((n_chan, 16, nsrc), jnp.float32),
            pltpu.VMEM((16, nsrc), jnp.float32),
            pltpu.SemaphoreType.DMA((n_chan,)),
            pltpu.SemaphoreType.DMA((n_chan,)),
            pltpu.VMEM((n_chan, 16, nsrc), jnp.float32),
        ],
        compiler_params=pltpu.CompilerParams(collective_id=0, has_side_effects=True),
    )(offsets, record, dead, sources)


def shards(record, offsets, dead_mask, sources):
    n_tm = lax.axis_size("tm")
    n_chan = lax.axis_size("chan")
    bins_dev = F // n_tm
    channels, span = record.shape
    first, count = window_plan(n_tm, span)
    per = NWIN * 2 * bins_dev // n_chan
    assert per * n_chan == NWIN * 2 * bins_dev and bins_dev % per == 0 and per <= 16
    white, rotated, source_spec = fused_exchange(
        offsets, record, dead_mask.reshape(1, channels), sources.reshape(1, -1),
        n_tm, n_chan, bins_dev, first, count
    )
    return cross_spectra(source_spec, white, rotated)


def solution(mesh):
    return jax.shard_map(
        shards,
        mesh=mesh,
        in_specs=(P("chan", "tm"), P(), P("chan"), P()),
        out_specs=P("tm", None, None, "chan"),
        check_vma=False,
    )
```

```python
import functools
import math

import jax
import jax.numpy as jnp
from jax import lax
from jax.experimental import pallas as pl
from jax.experimental.pallas import tpu as pltpu
from jax.sharding import PartitionSpec as P

W = 12000
F = 640
FLO = 6
NWIN = 4
SLOTS = 2
FA = 64

MESH = pl.DeviceIdType.MESH


def window_plan(n_tm, span):
    total = n_tm * span
    slack = total - NWIN * W
    lows = [0] + [w * W for w in range(1, NWIN - 1)] + [total - W]
    highs = [0] + [w * W + slack for w in range(1, NWIN - 1)] + [total - W]
    first, count = [], []
    for d in range(n_tm):
        meets = [w for w in range(NWIN) if lows[w] < (d + 1) * span and highs[w] + W > d * span]
        assert meets and meets == list(range(meets[0], meets[0] + len(meets)))
        assert len(meets) <= SLOTS
        first.append(meets[0])
        count.append(len(meets))
    return first, count


def _cross_kernel(bins_dev, src_ref, white_ref, rot_ref, out_ref):
    for k in range(bins_dev):
        left = src_ref[k].astype(jnp.bfloat16)
        for p, right_ref in enumerate((white_ref, rot_ref)):
            out_ref[k, p] = lax.dot_general(
                left, right_ref[k].astype(jnp.bfloat16), (((0,), (0,)), ((), ())),
                preferred_element_type=jnp.float32,
            ) / NWIN


def cross_spectra(source_spec, white, rotated):
    bins_dev, _, nsrc = source_spec.shape
    channels = white.shape[2]
    vmem = pl.BlockSpec(memory_space=pltpu.VMEM)
    return pl.pallas_call(
        functools.partial(_cross_kernel, bins_dev),
        out_shape=jax.ShapeDtypeStruct((bins_dev, 2, nsrc, channels), jnp.float32),
        in_specs=[vmem] * 3,
        out_specs=vmem,
    )(source_spec, white, rotated)


def _any_of(me, members):
    hit = jnp.bool_(False)
    for m in members:
        hit = hit | (me == m)
    return hit


def _fused_kernel(n_tm, n_chan, bins_dev, first, count,
                  offsets_ref, record_ref, dead_ref, sources_ref,
                  white_ref, rot_ref, srcspec_ref,
                  ar_ref, ai_ref, c1_ref, c2_ref, x_ref,
                  blocks_ref, lhs, recv, spec, lvl_send, lvl_recv, src_send,
                  a2a_send_sem, a2a_recv_sem, lvl_send_sem, lvl_recv_sem,
                  src_send_sem, src_recv_sem, rs_recv, ag_send, ag_send_sem, ag_recv_sem,
                  ag_recv):
    me = lax.axis_index("tm")
    mc = lax.axis_index("chan")
    two = [d for d in range(n_tm) if count[d] == 2]
    me_two = _any_of(me, two)
    rows = 2 * bins_dev
    group = lhs.shape[0] // rows

    barrier = pltpu.get_barrier_semaphore()
    for i in range(1, n_tm):
        pl.semaphore_signal(barrier, inc=1, device_id={"tm": lax.rem(me + i, n_tm)},
                            device_id_type=MESH)
    for i in range(1, n_chan):
        pl.semaphore_signal(barrier, inc=1, device_id={"chan": lax.rem(mc + i, n_chan)},
                            device_id_type=MESH)

    span = record_ref.shape[1]
    wa = jnp.int32(0)
    for d in range(n_tm):
        wa = jnp.where(me == d, first[d], wa)
    local_times = me * span + lax.broadcasted_iota(jnp.int32, (1, span), 1)
    coarse = FLO + bins_dev * lax.broadcasted_iota(jnp.int32, (n_tm, 1), 0)
    fine_row = lax.broadcasted_iota(jnp.int32, (2 * bins_dev, 1), 0)
    fine = lax.rem(fine_row, bins_dev)
    scale = 2.0 * math.pi / W

    def prepare(slot):
        window = wa + slot
        origin = offsets_ref[jnp.minimum(window, NWIN - 1)]
        shifted = local_times - origin
        inside = (shifted >= 0) & (shifted < W) & (window < NWIN)
        times = jnp.where(inside, shifted, 0)
        angle = lax.rem(coarse * times, W).astype(jnp.float32) * scale
        ar_ref[slot] = jnp.cos(angle)
        ai_ref[slot] = -jnp.sin(angle)
        angle = lax.rem(fine * times, W).astype(jnp.float32) * scale
        cos, sin = jnp.cos(angle), jnp.sin(angle)
        top = fine_row < bins_dev
        c1_ref[slot] = jnp.where(top, cos, -sin)
        c2_ref[slot] = jnp.where(top, sin, cos)
        x_ref[slot] = jnp.where(inside, record_ref[...], jnp.zeros_like(record_ref[...]))

    prepare(0)

    @pl.when(me_two)
    def _():
        prepare(1)

    def a2a(peer, slot, src_dev):
        return pltpu.make_async_remote_copy(
            src_ref=blocks_ref.at[peer, slot],
            dst_ref=recv.at[src_dev, slot],
            send_sem=a2a_send_sem.at[peer, slot],
            recv_sem=a2a_recv_sem.at[src_dev, slot],
            device_id={"tm": peer},
            device_id_type=MESH,
        )

    def compute(g, slot):
        c1 = c1_ref[slot]
        c2 = c2_ref[slot]
        for dd in range(group):
            d = lax.rem(me + g * group + dd, n_tm)
            ar = ar_ref[slot, pl.ds(d, 1), :]
            ai = ai_ref[slot, pl.ds(d, 1), :]
            lhs[dd * rows:(dd + 1) * rows, :] = ar * c1 + ai * c2
        res = lax.dot_general(
            lhs[...].astype(jnp.bfloat16), x_ref[slot], (((1,), (1,)), ((), ())),
            preferred_element_type=jnp.float32,
        )
        for dd in range(group):
            d = lax.rem(me + g * group + dd, n_tm)
            blocks_ref[d, slot] = res[dd * rows:(dd + 1) * rows, :]

    def send(g, slot):
        for dd in range(group):
            if g == 0 and dd == 0:
                continue
            a2a(lax.rem(me + g * group + dd, n_tm), slot, me).start()

    for g in range(n_tm // group):
        compute(g, 0)
        if g == 0:
            pl.semaphore_wait(barrier, n_tm - 1 + n_chan - 1)
        send(g, 0)

    @pl.when(me_two)
    def _():
        for g in range(n_tm // group):
            compute(g, 1)
            send(g, 1)

    recv[me, 0] = blocks_ref[me, 0]

    @pl.when(me_two)
    def _():
        recv[me, 1] = blocks_ref[me, 1]

    for i in range(1, n_tm):
        peer = lax.rem(me + i, n_tm)
        a2a(peer, 0, me).wait_send()

        @pl.when(me_two)
        def _():
            a2a(peer, 1, me).wait_send()

    for s in range(n_tm):
        @pl.when(me != s)
        def _():
            a2a(s, 0, s).wait_recv()
            if count[s] == 2:
                a2a(s, 1, s).wait_recv()

    for w in range(NWIN):
        acc = None
        for s in range(n_tm):
            for j in range(count[s]):
                if first[s] + j == w:
                    part = recv[s, j]
                    acc = part if acc is None else acc + part
        spec[w] = acc

    rows = []
    for w in range(NWIN):
        re = spec[w, 0:bins_dev, :]
        im = spec[w, bins_dev:2 * bins_dev, :]
        mag = jnp.sqrt(re * re + im * im)
        rows.append(jnp.sum(mag, axis=0, keepdims=True))
    rows.append(jnp.zeros((8 - NWIN, rows[0].shape[1]), jnp.float32))
    lvl_send[...] = jnp.concatenate(rows, axis=0)

    def lvl(peer, src_dev):
        return pltpu.make_async_remote_copy(
            src_ref=lvl_send,
            dst_ref=lvl_recv.at[src_dev],
            send_sem=lvl_send_sem.at[peer],
            recv_sem=lvl_recv_sem.at[src_dev],
            device_id={"tm": peer},
            device_id_type=MESH,
        )

    for i in range(1, n_tm):
        lvl(lax.rem(me + i, n_tm), me).start()
    lvl_recv[me] = lvl_send[...]
    for i in range(1, n_tm):
        lvl(lax.rem(me + i, n_tm), me).wait_send()
    for i in range(1, n_tm):
        src = lax.rem(me + n_tm - i, n_tm)
        lvl(src, src).wait_recv()

    level = lvl_recv[0]
    for s in range(1, n_tm):
        level = level + lvl_recv[s]
    level = level / F

    mask = dead_ref[...].astype(jnp.float32)
    channels = record_ref.shape[0]
    local_index = sources_ref[...] - mc * channels
    onehot = (lax.broadcasted_iota(jnp.int32, (channels, local_index.shape[1]), 0)
              == local_index).astype(jnp.bfloat16)
    per = NWIN * 2 * bins_dev // n_chan
    halves = bins_dev // per
    src_send[...] = jnp.zeros_like(src_send)
    for w in range(NWIN):
        re = spec[w, 0:bins_dev, :]
        im = spec[w, bins_dev:2 * bins_dev, :]
        mag = jnp.sqrt(re * re + im * im)
        den = mag + 0.1 * level[w:w + 1, :] + 1e-06
        for p, part in enumerate((re, im)):
            white = (part / den).astype(jnp.bfloat16).astype(jnp.float32) * mask
            for k in range(bins_dev):
                white_ref[k, 2 * w + p:2 * w + p + 1, :] = white[k:k + 1, :]
                if p == 0:
                    rot_ref[k, 2 * w + 1:2 * w + 2, :] = -white[k:k + 1, :]
                else:
                    rot_ref[k, 2 * w:2 * w + 1, :] = white[k:k + 1, :]
            picked = jnp.dot(
                white.astype(jnp.bfloat16), onehot, preferred_element_type=jnp.float32
            )
            for h in range(halves):
                src_send[(2 * w + p) * halves + h, 0:per, :] = picked[h * per:(h + 1) * per, :]

    def rsc(peer, src_dev):
        return pltpu.make_async_remote_copy(
            src_ref=src_send.at[peer],
            dst_ref=rs_recv.at[src_dev],
            send_sem=src_send_sem.at[peer],
            recv_sem=src_recv_sem.at[src_dev],
            device_id={"chan": peer},
            device_id_type=MESH,
        )

    for i in range(1, n_chan):
        rsc(lax.rem(mc + i, n_chan), mc).start()
    rs_recv[mc] = src_send[mc]
    for i in range(1, n_chan):
        rsc(lax.rem(mc + i, n_chan), mc).wait_send()
    for i in range(1, n_chan):
        src = lax.rem(mc + n_chan - i, n_chan)
        rsc(src, src).wait_recv()

    total = rs_recv[0]
    for s in range(1, n_chan):
        total = total + rs_recv[s]
    ag_send[...] = total

    def agc(peer, src_dev):
        return pltpu.make_async_remote_copy(
            src_ref=ag_send,
            dst_ref=ag_recv.at[src_dev],
            send_sem=ag_send_sem.at[peer],
            recv_sem=ag_recv_sem.at[src_dev],
            device_id={"chan": peer},
            device_id_type=MESH,
        )

    for i in range(1, n_chan):
        agc(lax.rem(mc + i, n_chan), mc).start()
    ag_recv[mc] = ag_send[...]
    for i in range(1, n_chan):
        agc(lax.rem(mc + i, n_chan), mc).wait_send()
    for i in range(1, n_chan):
        src = lax.rem(mc + n_chan - i, n_chan)
        agc(src, src).wait_recv()

    for i in range(NWIN * 2):
        for h in range(halves):
            for r in range(per):
                k = h * per + r
                srcspec_ref[k, i:i + 1, :] = ag_recv[i * halves + h, r:r + 1, :]


def fused_exchange(offsets, record, dead, sources, n_tm, n_chan, bins_dev, first, count):
    channels, span = record.shape
    nsrc = sources.shape[1]
    group = 16
    vmem = pl.BlockSpec(memory_space=pltpu.VMEM)
    return pl.pallas_call(
        functools.partial(_fused_kernel, n_tm, n_chan, bins_dev, first, count),
        out_shape=(
            jax.ShapeDtypeStruct((bins_dev, NWIN * 2, channels), jnp.float32),
            jax.ShapeDtypeStruct((bins_dev, NWIN * 2, channels), jnp.float32),
            jax.ShapeDtypeStruct((bins_dev, NWIN * 2, nsrc), jnp.float32),
        ),
        in_specs=[pl.BlockSpec(memory_space=pltpu.SMEM), vmem, vmem, vmem],
        out_specs=(vmem, vmem, vmem),
        scratch_shapes=[
            pltpu.VMEM((SLOTS, n_tm, span), jnp.float32),
            pltpu.VMEM((SLOTS, n_tm, span), jnp.float32),
            pltpu.VMEM((SLOTS, 2 * bins_dev, span), jnp.float32),
            pltpu.VMEM((SLOTS, 2 * bins_dev, span), jnp.float32),
            pltpu.VMEM((SLOTS, channels, span), jnp.bfloat16),
            pltpu.VMEM((n_tm, SLOTS, 2 * bins_dev, channels), jnp.float32),
            pltpu.VMEM((group * 2 * bins_dev, span), jnp.float32),
            pltpu.VMEM((n_tm, SLOTS, 2 * bins_dev, channels), jnp.float32),
            pltpu.VMEM((NWIN, 2 * bins_dev, channels), jnp.float32),
            pltpu.VMEM((8, channels), jnp.float32),
            pltpu.VMEM((n_tm, 8, channels), jnp.float32),
            pltpu.VMEM((n_chan, 16, nsrc), jnp.float32),
            pltpu.SemaphoreType.DMA((n_tm, SLOTS)),
            pltpu.SemaphoreType.DMA((n_tm, SLOTS)),
            pltpu.SemaphoreType.DMA((n_tm,)),
            pltpu.SemaphoreType.DMA((n_tm,)),
            pltpu.SemaphoreType.DMA((n_chan,)),
            pltpu.SemaphoreType.DMA((n_chan,)),
            pltpu.VMEM((n_chan, 16, nsrc), jnp.float32),
            pltpu.VMEM((16, nsrc), jnp.float32),
            pltpu.SemaphoreType.DMA((n_chan,)),
            pltpu.SemaphoreType.DMA((n_chan,)),
            pltpu.VMEM((n_chan, 16, nsrc), jnp.float32),
        ],
        compiler_params=pltpu.CompilerParams(collective_id=0, has_side_effects=True),
    )(offsets, record, dead, sources)


def shards(record, offsets, dead_mask, sources):
    n_tm = lax.axis_size("tm")
    n_chan = lax.axis_size("chan")
    bins_dev = F // n_tm
    channels, span = record.shape
    first, count = window_plan(n_tm, span)
    per = NWIN * 2 * bins_dev // n_chan
    assert per * n_chan == NWIN * 2 * bins_dev and bins_dev % per == 0 and per <= 16
    white, rotated, source_spec = fused_exchange(
        offsets, record, dead_mask.reshape(1, channels), sources.reshape(1, -1),
        n_tm, n_chan, bins_dev, first, count
    )
    return cross_spectra(source_spec, white, rotated)


def solution(mesh):
    return jax.shard_map(
        shards,
        mesh=mesh,
        in_specs=(P("chan", "tm"), P(), P("chan"), P()),
        out_specs=P("tm", None, None, "chan"),
        check_vma=False,
    )
```

```python
import functools
import math

import jax
import jax.numpy as jnp
from jax import lax
from jax.experimental import pallas as pl
from jax.experimental.pallas import tpu as pltpu
from jax.sharding import PartitionSpec as P

W = 12000
F = 640
FLO = 6
NWIN = 4
SLOTS = 2
FA = 64

MESH = pl.DeviceIdType.MESH


def window_plan(n_tm, span):
    total = n_tm * span
    slack = total - NWIN * W
    lows = [0] + [w * W for w in range(1, NWIN - 1)] + [total - W]
    highs = [0] + [w * W + slack for w in range(1, NWIN - 1)] + [total - W]
    first, count = [], []
    for d in range(n_tm):
        meets = [w for w in range(NWIN) if lows[w] < (d + 1) * span and highs[w] + W > d * span]
        assert meets and meets == list(range(meets[0], meets[0] + len(meets)))
        assert len(meets) <= SLOTS
        first.append(meets[0])
        count.append(len(meets))
    return first, count


def _cross_kernel(bins_dev, src_ref, white_ref, rot_ref, out_ref):
    for k in range(bins_dev):
        left = src_ref[k].astype(jnp.bfloat16)
        for p, right_ref in enumerate((white_ref, rot_ref)):
            out_ref[k, p] = lax.dot_general(
                left, right_ref[k].astype(jnp.bfloat16), (((0,), (0,)), ((), ())),
                preferred_element_type=jnp.float32,
            ) / NWIN


def cross_spectra(source_spec, white, rotated):
    bins_dev, _, nsrc = source_spec.shape
    channels = white.shape[2]
    vmem = pl.BlockSpec(memory_space=pltpu.VMEM)
    return pl.pallas_call(
        functools.partial(_cross_kernel, bins_dev),
        out_shape=jax.ShapeDtypeStruct((bins_dev, 2, nsrc, channels), jnp.float32),
        in_specs=[vmem] * 3,
        out_specs=vmem,
    )(source_spec, white, rotated)


def _any_of(me, members):
    hit = jnp.bool_(False)
    for m in members:
        hit = hit | (me == m)
    return hit


def _fused_kernel(n_tm, n_chan, bins_dev, first, count,
                  offsets_ref, record_ref, dead_ref, sources_ref,
                  white_ref, rot_ref, srcspec_ref,
                  ar_ref, ai_ref, c1_ref, c2_ref, x_ref,
                  blocks_ref, lhs, recv, spec, lvl_send, lvl_recv, src_send,
                  a2a_send_sem, a2a_recv_sem, lvl_send_sem, lvl_recv_sem,
                  src_send_sem, src_recv_sem, rs_recv, ag_send, ag_send_sem, ag_recv_sem,
                  ag_recv):
    me = lax.axis_index("tm")
    mc = lax.axis_index("chan")
    two = [d for d in range(n_tm) if count[d] == 2]
    me_two = _any_of(me, two)
    rows = 2 * bins_dev
    group = lhs.shape[0] // rows

    barrier = pltpu.get_barrier_semaphore()
    for i in range(1, n_chan):
        pl.semaphore_signal(barrier, inc=1, device_id={"chan": lax.rem(mc + i, n_chan)},
                            device_id_type=MESH)
    for i in range(1, n_tm):
        pl.semaphore_signal(barrier, inc=1, device_id={"tm": lax.rem(me + i, n_tm)},
                            device_id_type=MESH)

    span = record_ref.shape[1]
    wa = jnp.int32(0)
    for d in range(n_tm):
        wa = jnp.where(me == d, first[d], wa)
    local_times = me * span + lax.broadcasted_iota(jnp.int32, (1, span), 1)
    coarse = FLO + bins_dev * lax.broadcasted_iota(jnp.int32, (n_tm, 1), 0)
    fine_row = lax.broadcasted_iota(jnp.int32, (2 * bins_dev, 1), 0)
    fine = lax.rem(fine_row, bins_dev)
    scale = 2.0 * math.pi / W

    def prepare(slot):
        window = wa + slot
        origin = offsets_ref[jnp.minimum(window, NWIN - 1)]
        shifted = local_times - origin
        inside = (shifted >= 0) & (shifted < W) & (window < NWIN)
        times = jnp.where(inside, shifted, 0)
        angle = lax.rem(coarse * times, W).astype(jnp.float32) * scale
        ar_ref[slot] = jnp.cos(angle)
        ai_ref[slot] = -jnp.sin(angle)
        angle = lax.rem(fine * times, W).astype(jnp.float32) * scale
        cos, sin = jnp.cos(angle), jnp.sin(angle)
        top = fine_row < bins_dev
        c1_ref[slot] = jnp.where(top, cos, -sin)
        c2_ref[slot] = jnp.where(top, sin, cos)
        x_ref[slot] = jnp.where(inside, record_ref[...], jnp.zeros_like(record_ref[...]))

    prepare(0)

    @pl.when(me_two)
    def _():
        prepare(1)

    def a2a(peer, slot, src_dev):
        return pltpu.make_async_remote_copy(
            src_ref=blocks_ref.at[peer, slot],
            dst_ref=recv.at[src_dev, slot],
            send_sem=a2a_send_sem.at[peer, slot],
            recv_sem=a2a_recv_sem.at[src_dev, slot],
            device_id={"tm": peer},
            device_id_type=MESH,
        )

    def compute(g, slot):
        c1 = c1_ref[slot]
        c2 = c2_ref[slot]
        for dd in range(group):
            d = lax.rem(me + g * group + dd, n_tm)
            ar = ar_ref[slot, pl.ds(d, 1), :]
            ai = ai_ref[slot, pl.ds(d, 1), :]
            lhs[dd * rows:(dd + 1) * rows, :] = ar * c1 + ai * c2
        res = lax.dot_general(
            lhs[...].astype(jnp.bfloat16), x_ref[slot], (((1,), (1,)), ((), ())),
            preferred_element_type=jnp.float32,
        )
        for dd in range(group):
            d = lax.rem(me + g * group + dd, n_tm)
            blocks_ref[d, slot] = res[dd * rows:(dd + 1) * rows, :]

    def send(g, slot):
        for dd in range(group):
            if g == 0 and dd == 0:
                continue
            a2a(lax.rem(me + g * group + dd, n_tm), slot, me).start()

    for g in range(n_tm // group):
        compute(g, 0)
        if g == 0:
            pl.semaphore_wait(barrier, n_tm - 1 + n_chan - 1)
        send(g, 0)

        @pl.when(me_two)
        def _():
            compute(g, 1)
            send(g, 1)

    recv[me, 0] = blocks_ref[me, 0]

    @pl.when(me_two)
    def _():
        recv[me, 1] = blocks_ref[me, 1]

    for i in range(1, n_tm):
        peer = lax.rem(me + i, n_tm)
        a2a(peer, 0, me).wait_send()

        @pl.when(me_two)
        def _():
            a2a(peer, 1, me).wait_send()

    for s in range(n_tm):
        @pl.when(me != s)
        def _():
            a2a(s, 0, s).wait_recv()
            if count[s] == 2:
                a2a(s, 1, s).wait_recv()

    for w in range(NWIN):
        acc = None
        for s in range(n_tm):
            for j in range(count[s]):
                if first[s] + j == w:
                    part = recv[s, j]
                    acc = part if acc is None else acc + part
        spec[w] = acc

    rows = []
    for w in range(NWIN):
        re = spec[w, 0:bins_dev, :]
        im = spec[w, bins_dev:2 * bins_dev, :]
        mag = jnp.sqrt(re * re + im * im)
        rows.append(jnp.sum(mag, axis=0, keepdims=True))
    rows.append(jnp.zeros((8 - NWIN, rows[0].shape[1]), jnp.float32))
    lvl_send[...] = jnp.concatenate(rows, axis=0)

    def lvl(peer, src_dev):
        return pltpu.make_async_remote_copy(
            src_ref=lvl_send,
            dst_ref=lvl_recv.at[src_dev],
            send_sem=lvl_send_sem.at[peer],
            recv_sem=lvl_recv_sem.at[src_dev],
            device_id={"tm": peer},
            device_id_type=MESH,
        )

    for i in range(1, n_tm):
        lvl(lax.rem(me + i, n_tm), me).start()
    lvl_recv[me] = lvl_send[...]
    for i in range(1, n_tm):
        lvl(lax.rem(me + i, n_tm), me).wait_send()
    for i in range(1, n_tm):
        src = lax.rem(me + n_tm - i, n_tm)
        lvl(src, src).wait_recv()

    level = lvl_recv[0]
    for s in range(1, n_tm):
        level = level + lvl_recv[s]
    level = level / F

    mask = dead_ref[...].astype(jnp.float32)
    channels = record_ref.shape[0]
    local_index = sources_ref[...] - mc * channels
    onehot = (lax.broadcasted_iota(jnp.int32, (channels, local_index.shape[1]), 0)
              == local_index).astype(jnp.bfloat16)
    per = NWIN * 2 * bins_dev // n_chan
    halves = bins_dev // per
    src_send[...] = jnp.zeros_like(src_send)
    for w in range(NWIN):
        re = spec[w, 0:bins_dev, :]
        im = spec[w, bins_dev:2 * bins_dev, :]
        mag = jnp.sqrt(re * re + im * im)
        den = mag + 0.1 * level[w:w + 1, :] + 1e-06
        for p, part in enumerate((re, im)):
            white = (part / den).astype(jnp.bfloat16).astype(jnp.float32) * mask
            for k in range(bins_dev):
                white_ref[k, 2 * w + p:2 * w + p + 1, :] = white[k:k + 1, :]
                if p == 0:
                    rot_ref[k, 2 * w + 1:2 * w + 2, :] = -white[k:k + 1, :]
                else:
                    rot_ref[k, 2 * w:2 * w + 1, :] = white[k:k + 1, :]
            picked = jnp.dot(
                white.astype(jnp.bfloat16), onehot, preferred_element_type=jnp.float32
            )
            for h in range(halves):
                src_send[(2 * w + p) * halves + h, 0:per, :] = picked[h * per:(h + 1) * per, :]

    def rsc(peer, src_dev):
        return pltpu.make_async_remote_copy(
            src_ref=src_send.at[peer],
            dst_ref=rs_recv.at[src_dev],
            send_sem=src_send_sem.at[peer],
            recv_sem=src_recv_sem.at[src_dev],
            device_id={"chan": peer},
            device_id_type=MESH,
        )

    for i in range(1, n_chan):
        rsc(lax.rem(mc + i, n_chan), mc).start()
    rs_recv[mc] = src_send[mc]
    for i in range(1, n_chan):
        rsc(lax.rem(mc + i, n_chan), mc).wait_send()
    for i in range(1, n_chan):
        src = lax.rem(mc + n_chan - i, n_chan)
        rsc(src, src).wait_recv()

    total = rs_recv[0]
    for s in range(1, n_chan):
        total = total + rs_recv[s]
    ag_send[...] = total

    def agc(peer, src_dev):
        return pltpu.make_async_remote_copy(
            src_ref=ag_send,
            dst_ref=ag_recv.at[src_dev],
            send_sem=ag_send_sem.at[peer],
            recv_sem=ag_recv_sem.at[src_dev],
            device_id={"chan": peer},
            device_id_type=MESH,
        )

    for i in range(1, n_chan):
        agc(lax.rem(mc + i, n_chan), mc).start()
    ag_recv[mc] = ag_send[...]
    for i in range(1, n_chan):
        agc(lax.rem(mc + i, n_chan), mc).wait_send()
    for i in range(1, n_chan):
        src = lax.rem(mc + n_chan - i, n_chan)
        agc(src, src).wait_recv()

    for i in range(NWIN * 2):
        for h in range(halves):
            for r in range(per):
                k = h * per + r
                srcspec_ref[k, i:i + 1, :] = ag_recv[i * halves + h, r:r + 1, :]


def fused_exchange(offsets, record, dead, sources, n_tm, n_chan, bins_dev, first, count):
    channels, span = record.shape
    nsrc = sources.shape[1]
    group = 16
    vmem = pl.BlockSpec(memory_space=pltpu.VMEM)
    return pl.pallas_call(
        functools.partial(_fused_kernel, n_tm, n_chan, bins_dev, first, count),
        out_shape=(
            jax.ShapeDtypeStruct((bins_dev, NWIN * 2, channels), jnp.float32),
            jax.ShapeDtypeStruct((bins_dev, NWIN * 2, channels), jnp.float32),
            jax.ShapeDtypeStruct((bins_dev, NWIN * 2, nsrc), jnp.float32),
        ),
        in_specs=[pl.BlockSpec(memory_space=pltpu.SMEM), vmem, vmem, vmem],
        out_specs=(vmem, vmem, vmem),
        scratch_shapes=[
            pltpu.VMEM((SLOTS, n_tm, span), jnp.float32),
            pltpu.VMEM((SLOTS, n_tm, span), jnp.float32),
            pltpu.VMEM((SLOTS, 2 * bins_dev, span), jnp.float32),
            pltpu.VMEM((SLOTS, 2 * bins_dev, span), jnp.float32),
            pltpu.VMEM((SLOTS, channels, span), jnp.bfloat16),
            pltpu.VMEM((n_tm, SLOTS, 2 * bins_dev, channels), jnp.float32),
            pltpu.VMEM((group * 2 * bins_dev, span), jnp.float32),
            pltpu.VMEM((n_tm, SLOTS, 2 * bins_dev, channels), jnp.float32),
            pltpu.VMEM((NWIN, 2 * bins_dev, channels), jnp.float32),
            pltpu.VMEM((8, channels), jnp.float32),
            pltpu.VMEM((n_tm, 8, channels), jnp.float32),
            pltpu.VMEM((n_chan, 16, nsrc), jnp.float32),
            pltpu.SemaphoreType.DMA((n_tm, SLOTS)),
            pltpu.SemaphoreType.DMA((n_tm, SLOTS)),
            pltpu.SemaphoreType.DMA((n_tm,)),
            pltpu.SemaphoreType.DMA((n_tm,)),
            pltpu.SemaphoreType.DMA((n_chan,)),
            pltpu.SemaphoreType.DMA((n_chan,)),
            pltpu.VMEM((n_chan, 16, nsrc), jnp.float32),
            pltpu.VMEM((16, nsrc), jnp.float32),
            pltpu.SemaphoreType.DMA((n_chan,)),
            pltpu.SemaphoreType.DMA((n_chan,)),
            pltpu.VMEM((n_chan, 16, nsrc), jnp.float32),
        ],
        compiler_params=pltpu.CompilerParams(collective_id=0, has_side_effects=True),
    )(offsets, record, dead, sources)


def shards(record, offsets, dead_mask, sources):
    n_tm = lax.axis_size("tm")
    n_chan = lax.axis_size("chan")
    bins_dev = F // n_tm
    channels, span = record.shape
    first, count = window_plan(n_tm, span)
    per = NWIN * 2 * bins_dev // n_chan
    assert per * n_chan == NWIN * 2 * bins_dev and bins_dev % per == 0 and per <= 16
    white, rotated, source_spec = fused_exchange(
        offsets, record, dead_mask.reshape(1, channels), sources.reshape(1, -1),
        n_tm, n_chan, bins_dev, first, count
    )
    return cross_spectra(source_spec, white, rotated)


def solution(mesh):
    return jax.shard_map(
        shards,
        mesh=mesh,
        in_specs=(P("chan", "tm"), P(), P("chan"), P()),
        out_specs=P("tm", None, None, "chan"),
        check_vma=False,
    )
```

```python
import functools
import math

import jax
import jax.numpy as jnp
from jax import lax
from jax.experimental import pallas as pl
from jax.experimental.pallas import tpu as pltpu
from jax.sharding import PartitionSpec as P

W = 12000
F = 640
FLO = 6
NWIN = 4
SLOTS = 2
FA = 64

MESH = pl.DeviceIdType.MESH


def window_plan(n_tm, span):
    total = n_tm * span
    slack = total - NWIN * W
    lows = [0] + [w * W for w in range(1, NWIN - 1)] + [total - W]
    highs = [0] + [w * W + slack for w in range(1, NWIN - 1)] + [total - W]
    first, count = [], []
    for d in range(n_tm):
        meets = [w for w in range(NWIN) if lows[w] < (d + 1) * span and highs[w] + W > d * span]
        assert meets and meets == list(range(meets[0], meets[0] + len(meets)))
        assert len(meets) <= SLOTS
        first.append(meets[0])
        count.append(len(meets))
    return first, count


def _cross_kernel(bins_dev, src_ref, white_ref, rot_ref, out_ref):
    for k in range(bins_dev):
        left = src_ref[k].astype(jnp.bfloat16)
        for p, right_ref in enumerate((white_ref, rot_ref)):
            out_ref[k, p] = lax.dot_general(
                left, right_ref[k].astype(jnp.bfloat16), (((0,), (0,)), ((), ())),
                preferred_element_type=jnp.float32,
            ) / NWIN


def cross_spectra(source_spec, white, rotated):
    bins_dev, _, nsrc = source_spec.shape
    channels = white.shape[2]
    vmem = pl.BlockSpec(memory_space=pltpu.VMEM)
    return pl.pallas_call(
        functools.partial(_cross_kernel, bins_dev),
        out_shape=jax.ShapeDtypeStruct((bins_dev, 2, nsrc, channels), jnp.float32),
        in_specs=[vmem] * 3,
        out_specs=vmem,
    )(source_spec, white, rotated)


def _any_of(me, members):
    hit = jnp.bool_(False)
    for m in members:
        hit = hit | (me == m)
    return hit


def _fused_kernel(n_tm, n_chan, bins_dev, first, count,
                  offsets_ref, record_ref, dead_ref, sources_ref,
                  white_ref, rot_ref, srcspec_ref,
                  ar_ref, ai_ref, c1_ref, c2_ref, x_ref,
                  blocks_ref, lhs, recv, spec, lvl_send, lvl_recv, src_send,
                  a2a_send_sem, a2a_recv_sem, lvl_send_sem, lvl_recv_sem,
                  src_send_sem, src_recv_sem, rs_recv, ag_send, ag_send_sem, ag_recv_sem,
                  ag_recv):
    me = lax.axis_index("tm")
    mc = lax.axis_index("chan")
    two = [d for d in range(n_tm) if count[d] == 2]
    me_two = _any_of(me, two)
    rows = 2 * bins_dev
    group = lhs.shape[0] // rows

    barrier = pltpu.get_barrier_semaphore()
    for i in range(1, n_chan):
        pl.semaphore_signal(barrier, inc=1, device_id={"chan": lax.rem(mc + i, n_chan)},
                            device_id_type=MESH)
    for i in range(1, n_tm):
        pl.semaphore_signal(barrier, inc=1, device_id={"tm": lax.rem(me + i, n_tm)},
                            device_id_type=MESH)

    span = record_ref.shape[1]
    wa = jnp.int32(0)
    for d in range(n_tm):
        wa = jnp.where(me == d, first[d], wa)
    local_times = me * span + lax.broadcasted_iota(jnp.int32, (1, span), 1)
    coarse = FLO + bins_dev * lax.broadcasted_iota(jnp.int32, (n_tm, 1), 0)
    fine_row = lax.broadcasted_iota(jnp.int32, (2 * bins_dev, 1), 0)
    fine = lax.rem(fine_row, bins_dev)
    scale = 2.0 * math.pi / W

    def prepare(slot):
        window = wa + slot
        origin = offsets_ref[jnp.minimum(window, NWIN - 1)]
        shifted = local_times - origin
        inside = (shifted >= 0) & (shifted < W) & (window < NWIN)
        times = jnp.where(inside, shifted, 0)
        angle = lax.rem(coarse * times, W).astype(jnp.float32) * scale
        ar_ref[slot] = jnp.cos(angle)
        ai_ref[slot] = -jnp.sin(angle)
        angle = lax.rem(fine * times, W).astype(jnp.float32) * scale
        cos, sin = jnp.cos(angle), jnp.sin(angle)
        top = fine_row < bins_dev
        c1_ref[slot] = jnp.where(top, cos, -sin)
        c2_ref[slot] = jnp.where(top, sin, cos)
        x_ref[slot] = jnp.where(inside, record_ref[...], jnp.zeros_like(record_ref[...]))

    prepare(0)

    @pl.when(me_two)
    def _():
        prepare(1)

    def a2a(peer, slot, src_dev):
        return pltpu.make_async_remote_copy(
            src_ref=blocks_ref.at[peer, slot],
            dst_ref=recv.at[src_dev, slot],
            send_sem=a2a_send_sem.at[peer, slot],
            recv_sem=a2a_recv_sem.at[src_dev, slot],
            device_id={"tm": peer},
            device_id_type=MESH,
        )

    def compute(g, slot):
        c1 = c1_ref[slot]
        c2 = c2_ref[slot]
        for dd in range(group):
            d = lax.rem(me + g * group + dd, n_tm)
            ar = ar_ref[slot, pl.ds(d, 1), :]
            ai = ai_ref[slot, pl.ds(d, 1), :]
            lhs[dd * rows:(dd + 1) * rows, :] = ar * c1 + ai * c2
        res = lax.dot_general(
            lhs[...].astype(jnp.bfloat16), x_ref[slot], (((1,), (1,)), ((), ())),
            preferred_element_type=jnp.float32,
        )
        for dd in range(group):
            d = lax.rem(me + g * group + dd, n_tm)
            blocks_ref[d, slot] = res[dd * rows:(dd + 1) * rows, :]

    def send(g, slot):
        for dd in range(group):
            if g == 0 and dd == 0:
                continue
            a2a(lax.rem(me + g * group + dd, n_tm), slot, me).start()

    for g in range(n_tm // group):
        compute(g, 0)
        if g == 0:
            pl.semaphore_wait(barrier, n_tm - 1 + n_chan - 1)
        send(g, 0)

        @pl.when(me_two)
        def _():
            compute(g, 1)
            send(g, 1)

    recv[me, 0] = blocks_ref[me, 0]

    @pl.when(me_two)
    def _():
        recv[me, 1] = blocks_ref[me, 1]

    for i in range(1, n_tm):
        peer = lax.rem(me + i, n_tm)
        a2a(peer, 0, me).wait_send()

        @pl.when(me_two)
        def _():
            a2a(peer, 1, me).wait_send()

    for s in range(n_tm):
        @pl.when(me != s)
        def _():
            a2a(s, 0, s).wait_recv()
            if count[s] == 2:
                a2a(s, 1, s).wait_recv()

    for w in range(NWIN):
        acc = None
        for s in range(n_tm):
            for j in range(count[s]):
                if first[s] + j == w:
                    part = recv[s, j]
                    acc = part if acc is None else acc + part
        spec[w] = acc

    rows = []
    for w in range(NWIN):
        re = spec[w, 0:bins_dev, :]
        im = spec[w, bins_dev:2 * bins_dev, :]
        mag = jnp.sqrt(re * re + im * im)
        rows.append(jnp.sum(mag, axis=0, keepdims=True))
    rows.append(jnp.zeros((8 - NWIN, rows[0].shape[1]), jnp.float32))
    lvl_send[...] = jnp.concatenate(rows, axis=0)

    def lvl(peer, src_dev):
        return pltpu.make_async_remote_copy(
            src_ref=lvl_send,
            dst_ref=lvl_recv.at[src_dev],
            send_sem=lvl_send_sem.at[peer],
            recv_sem=lvl_recv_sem.at[src_dev],
            device_id={"tm": peer},
            device_id_type=MESH,
        )

    for i in range(1, n_tm):
        lvl(lax.rem(me + i, n_tm), me).start()
    lvl_recv[me] = lvl_send[...]
    for i in range(1, n_tm):
        lvl(lax.rem(me + i, n_tm), me).wait_send()
    for i in range(1, n_tm):
        src = lax.rem(me + n_tm - i, n_tm)
        lvl(src, src).wait_recv()

    level = lvl_recv[0]
    for s in range(1, n_tm):
        level = level + lvl_recv[s]
    level = level / F

    mask = dead_ref[...].astype(jnp.float32)
    channels = record_ref.shape[0]
    local_index = sources_ref[...] - mc * channels
    onehot = (lax.broadcasted_iota(jnp.int32, (channels, local_index.shape[1]), 0)
              == local_index).astype(jnp.bfloat16)
    per = NWIN * 2 * bins_dev // n_chan
    halves = bins_dev // per
    src_send[...] = jnp.zeros_like(src_send)
    for w in range(NWIN):
        re = spec[w, 0:bins_dev, :]
        im = spec[w, bins_dev:2 * bins_dev, :]
        mag = jnp.sqrt(re * re + im * im)
        den = mag + 0.1 * level[w:w + 1, :] + 1e-06
        for p, part in enumerate((re, im)):
            white = (part / den).astype(jnp.bfloat16).astype(jnp.float32) * mask
            stash = 24 * (2 * w + p)
            lhs[stash:stash + bins_dev, 0:channels] = white
            picked = jnp.dot(
                white.astype(jnp.bfloat16), onehot, preferred_element_type=jnp.float32
            )
            for h in range(halves):
                src_send[(2 * w + p) * halves + h, 0:per, :] = picked[h * per:(h + 1) * per, :]

    def rsc(peer, src_dev):
        return pltpu.make_async_remote_copy(
            src_ref=src_send.at[peer],
            dst_ref=rs_recv.at[src_dev],
            send_sem=src_send_sem.at[peer],
            recv_sem=src_recv_sem.at[src_dev],
            device_id={"chan": peer},
            device_id_type=MESH,
        )

    for i in range(1, n_chan):
        rsc(lax.rem(mc + i, n_chan), mc).start()
    rs_recv[mc] = src_send[mc]

    for w in range(NWIN):
        for p in range(2):
            stash = 24 * (2 * w + p)
            white = lhs[stash:stash + bins_dev, 0:channels]
            for k in range(bins_dev):
                white_ref[k, 2 * w + p:2 * w + p + 1, :] = white[k:k + 1, :]
                if p == 0:
                    rot_ref[k, 2 * w + 1:2 * w + 2, :] = -white[k:k + 1, :]
                else:
                    rot_ref[k, 2 * w:2 * w + 1, :] = white[k:k + 1, :]
    for i in range(1, n_chan):
        rsc(lax.rem(mc + i, n_chan), mc).wait_send()
    for i in range(1, n_chan):
        src = lax.rem(mc + n_chan - i, n_chan)
        rsc(src, src).wait_recv()

    total = rs_recv[0]
    for s in range(1, n_chan):
        total = total + rs_recv[s]
    ag_send[...] = total

    def agc(peer, src_dev):
        return pltpu.make_async_remote_copy(
            src_ref=ag_send,
            dst_ref=ag_recv.at[src_dev],
            send_sem=ag_send_sem.at[peer],
            recv_sem=ag_recv_sem.at[src_dev],
            device_id={"chan": peer},
            device_id_type=MESH,
        )

    for i in range(1, n_chan):
        agc(lax.rem(mc + i, n_chan), mc).start()
    ag_recv[mc] = ag_send[...]
    for i in range(1, n_chan):
        agc(lax.rem(mc + i, n_chan), mc).wait_send()
    for i in range(1, n_chan):
        src = lax.rem(mc + n_chan - i, n_chan)
        agc(src, src).wait_recv()

    for i in range(NWIN * 2):
        for h in range(halves):
            for r in range(per):
                k = h * per + r
                srcspec_ref[k, i:i + 1, :] = ag_recv[i * halves + h, r:r + 1, :]


def fused_exchange(offsets, record, dead, sources, n_tm, n_chan, bins_dev, first, count):
    channels, span = record.shape
    nsrc = sources.shape[1]
    group = 16
    vmem = pl.BlockSpec(memory_space=pltpu.VMEM)
    return pl.pallas_call(
        functools.partial(_fused_kernel, n_tm, n_chan, bins_dev, first, count),
        out_shape=(
            jax.ShapeDtypeStruct((bins_dev, NWIN * 2, channels), jnp.float32),
            jax.ShapeDtypeStruct((bins_dev, NWIN * 2, channels), jnp.float32),
            jax.ShapeDtypeStruct((bins_dev, NWIN * 2, nsrc), jnp.float32),
        ),
        in_specs=[pl.BlockSpec(memory_space=pltpu.SMEM), vmem, vmem, vmem],
        out_specs=(vmem, vmem, vmem),
        scratch_shapes=[
            pltpu.VMEM((SLOTS, n_tm, span), jnp.float32),
            pltpu.VMEM((SLOTS, n_tm, span), jnp.float32),
            pltpu.VMEM((SLOTS, 2 * bins_dev, span), jnp.float32),
            pltpu.VMEM((SLOTS, 2 * bins_dev, span), jnp.float32),
            pltpu.VMEM((SLOTS, channels, span), jnp.bfloat16),
            pltpu.VMEM((n_tm, SLOTS, 2 * bins_dev, channels), jnp.float32),
            pltpu.VMEM((group * 2 * bins_dev, span), jnp.float32),
            pltpu.VMEM((n_tm, SLOTS, 2 * bins_dev, channels), jnp.float32),
            pltpu.VMEM((NWIN, 2 * bins_dev, channels), jnp.float32),
            pltpu.VMEM((8, channels), jnp.float32),
            pltpu.VMEM((n_tm, 8, channels), jnp.float32),
            pltpu.VMEM((n_chan, 16, nsrc), jnp.float32),
            pltpu.SemaphoreType.DMA((n_tm, SLOTS)),
            pltpu.SemaphoreType.DMA((n_tm, SLOTS)),
            pltpu.SemaphoreType.DMA((n_tm,)),
            pltpu.SemaphoreType.DMA((n_tm,)),
            pltpu.SemaphoreType.DMA((n_chan,)),
            pltpu.SemaphoreType.DMA((n_chan,)),
            pltpu.VMEM((n_chan, 16, nsrc), jnp.float32),
            pltpu.VMEM((16, nsrc), jnp.float32),
            pltpu.SemaphoreType.DMA((n_chan,)),
            pltpu.SemaphoreType.DMA((n_chan,)),
            pltpu.VMEM((n_chan, 16, nsrc), jnp.float32),
        ],
        compiler_params=pltpu.CompilerParams(collective_id=0, has_side_effects=True),
    )(offsets, record, dead, sources)


def shards(record, offsets, dead_mask, sources):
    n_tm = lax.axis_size("tm")
    n_chan = lax.axis_size("chan")
    bins_dev = F // n_tm
    channels, span = record.shape
    first, count = window_plan(n_tm, span)
    per = NWIN * 2 * bins_dev // n_chan
    assert per * n_chan == NWIN * 2 * bins_dev and bins_dev % per == 0 and per <= 16
    white, rotated, source_spec = fused_exchange(
        offsets, record, dead_mask.reshape(1, channels), sources.reshape(1, -1),
        n_tm, n_chan, bins_dev, first, count
    )
    return cross_spectra(source_spec, white, rotated)


def solution(mesh):
    return jax.shard_map(
        shards,
        mesh=mesh,
        in_specs=(P("chan", "tm"), P(), P("chan"), P()),
        out_specs=P("tm", None, None, "chan"),
        check_vma=False,
    )
```

```python
import functools
import math

import jax
import jax.numpy as jnp
from jax import lax
from jax.experimental import pallas as pl
from jax.experimental.pallas import tpu as pltpu
from jax.sharding import PartitionSpec as P

W = 12000
F = 640
FLO = 6
NWIN = 4
SLOTS = 2
FA = 64

MESH = pl.DeviceIdType.MESH


def window_plan(n_tm, span):
    total = n_tm * span
    slack = total - NWIN * W
    lows = [0] + [w * W for w in range(1, NWIN - 1)] + [total - W]
    highs = [0] + [w * W + slack for w in range(1, NWIN - 1)] + [total - W]
    first, count = [], []
    for d in range(n_tm):
        meets = [w for w in range(NWIN) if lows[w] < (d + 1) * span and highs[w] + W > d * span]
        assert meets and meets == list(range(meets[0], meets[0] + len(meets)))
        assert len(meets) <= SLOTS
        first.append(meets[0])
        count.append(len(meets))
    return first, count


def _cross_kernel(bins_dev, src_ref, white_ref, rot_ref, out_ref, buf, sem):
    copies = []
    for k in range(bins_dev):
        slot = k % 2
        if k >= 2:
            copies[k - 2].wait()
        left = src_ref[k].astype(jnp.bfloat16)
        for p, right_ref in enumerate((white_ref, rot_ref)):
            buf[slot, p] = lax.dot_general(
                left, right_ref[k].astype(jnp.bfloat16), (((0,), (0,)), ((), ())),
                preferred_element_type=jnp.float32,
            ) / NWIN
        copy = pltpu.make_async_copy(buf.at[slot], out_ref.at[k], sem.at[slot])
        copy.start()
        copies.append(copy)
    for copy in copies[-2:]:
        copy.wait()


def cross_spectra(source_spec, white, rotated):
    bins_dev, _, nsrc = source_spec.shape
    channels = white.shape[2]
    vmem = pl.BlockSpec(memory_space=pltpu.VMEM)
    return pl.pallas_call(
        functools.partial(_cross_kernel, bins_dev),
        out_shape=jax.ShapeDtypeStruct((bins_dev, 2, nsrc, channels), jnp.float32),
        in_specs=[vmem] * 3,
        out_specs=pl.BlockSpec(memory_space=pl.ANY),
        scratch_shapes=[
            pltpu.VMEM((2, 2, nsrc, channels), jnp.float32),
            pltpu.SemaphoreType.DMA((2,)),
        ],
    )(source_spec, white, rotated)


def _any_of(me, members):
    hit = jnp.bool_(False)
    for m in members:
        hit = hit | (me == m)
    return hit


def _fused_kernel(n_tm, n_chan, bins_dev, first, count,
                  offsets_ref, record_ref, dead_ref, sources_ref,
                  white_ref, rot_ref, srcspec_ref,
                  ar_ref, ai_ref, c1_ref, c2_ref, x_ref,
                  blocks_ref, lhs, recv, spec, lvl_send, lvl_recv, src_send,
                  a2a_send_sem, a2a_recv_sem, lvl_send_sem, lvl_recv_sem,
                  src_send_sem, src_recv_sem, rs_recv, ag_send, ag_send_sem, ag_recv_sem,
                  ag_recv):
    me = lax.axis_index("tm")
    mc = lax.axis_index("chan")
    two = [d for d in range(n_tm) if count[d] == 2]
    me_two = _any_of(me, two)
    rows = 2 * bins_dev
    group = lhs.shape[0] // rows

    barrier = pltpu.get_barrier_semaphore()
    for i in range(1, n_chan):
        pl.semaphore_signal(barrier, inc=1, device_id={"chan": lax.rem(mc + i, n_chan)},
                            device_id_type=MESH)
    for i in range(1, n_tm):
        pl.semaphore_signal(barrier, inc=1, device_id={"tm": lax.rem(me + i, n_tm)},
                            device_id_type=MESH)

    span = record_ref.shape[1]
    wa = jnp.int32(0)
    for d in range(n_tm):
        wa = jnp.where(me == d, first[d], wa)
    local_times = me * span + lax.broadcasted_iota(jnp.int32, (1, span), 1)
    coarse = FLO + bins_dev * lax.broadcasted_iota(jnp.int32, (n_tm, 1), 0)
    fine_row = lax.broadcasted_iota(jnp.int32, (2 * bins_dev, 1), 0)
    fine = lax.rem(fine_row, bins_dev)
    scale = 2.0 * math.pi / W

    def prepare(slot):
        window = wa + slot
        origin = offsets_ref[jnp.minimum(window, NWIN - 1)]
        shifted = local_times - origin
        inside = (shifted >= 0) & (shifted < W) & (window < NWIN)
        times = jnp.where(inside, shifted, 0)
        angle = lax.rem(coarse * times, W).astype(jnp.float32) * scale
        ar_ref[slot] = jnp.cos(angle)
        ai_ref[slot] = -jnp.sin(angle)
        angle = lax.rem(fine * times, W).astype(jnp.float32) * scale
        cos, sin = jnp.cos(angle), jnp.sin(angle)
        top = fine_row < bins_dev
        c1_ref[slot] = jnp.where(top, cos, -sin)
        c2_ref[slot] = jnp.where(top, sin, cos)
        x_ref[slot] = jnp.where(inside, record_ref[...], jnp.zeros_like(record_ref[...]))

    prepare(0)

    @pl.when(me_two)
    def _():
        prepare(1)

    def a2a(peer, slot, src_dev):
        return pltpu.make_async_remote_copy(
            src_ref=blocks_ref.at[peer, slot],
            dst_ref=recv.at[src_dev, slot],
            send_sem=a2a_send_sem.at[peer, slot],
            recv_sem=a2a_recv_sem.at[src_dev, slot],
            device_id={"tm": peer},
            device_id_type=MESH,
        )

    def compute(g, slot):
        c1 = c1_ref[slot]
        c2 = c2_ref[slot]
        for dd in range(group):
            d = lax.rem(me + g * group + dd, n_tm)
            ar = ar_ref[slot, pl.ds(d, 1), :]
            ai = ai_ref[slot, pl.ds(d, 1), :]
            lhs[dd * rows:(dd + 1) * rows, :] = ar * c1 + ai * c2
        res = lax.dot_general(
            lhs[...].astype(jnp.bfloat16), x_ref[slot], (((1,), (1,)), ((), ())),
            preferred_element_type=jnp.float32,
        )
        for dd in range(group):
            d = lax.rem(me + g * group + dd, n_tm)
            blocks_ref[d, slot] = res[dd * rows:(dd + 1) * rows, :]

    def send(g, slot):
        for dd in range(group):
            if g == 0 and dd == 0:
                continue
            a2a(lax.rem(me + g * group + dd, n_tm), slot, me).start()

    for g in range(n_tm // group):
        compute(g, 0)
        if g == 0:
            pl.semaphore_wait(barrier, n_tm - 1 + n_chan - 1)
        send(g, 0)

        @pl.when(me_two)
        def _():
            compute(g, 1)
            send(g, 1)

    recv[me, 0] = blocks_ref[me, 0]

    @pl.when(me_two)
    def _():
        recv[me, 1] = blocks_ref[me, 1]

    for i in range(1, n_tm):
        peer = lax.rem(me + i, n_tm)
        a2a(peer, 0, me).wait_send()

        @pl.when(me_two)
        def _():
            a2a(peer, 1, me).wait_send()

    for s in range(n_tm):
        @pl.when(me != s)
        def _():
            a2a(s, 0, s).wait_recv()
            if count[s] == 2:
                a2a(s, 1, s).wait_recv()

    for w in range(NWIN):
        acc = None
        for s in range(n_tm):
            for j in range(count[s]):
                if first[s] + j == w:
                    part = recv[s, j]
                    acc = part if acc is None else acc + part
        spec[w] = acc

    rows = []
    for w in range(NWIN):
        re = spec[w, 0:bins_dev, :]
        im = spec[w, bins_dev:2 * bins_dev, :]
        mag = jnp.sqrt(re * re + im * im)
        rows.append(jnp.sum(mag, axis=0, keepdims=True))
    rows.append(jnp.zeros((8 - NWIN, rows[0].shape[1]), jnp.float32))
    lvl_send[...] = jnp.concatenate(rows, axis=0)

    def lvl(peer, src_dev):
        return pltpu.make_async_remote_copy(
            src_ref=lvl_send,
            dst_ref=lvl_recv.at[src_dev],
            send_sem=lvl_send_sem.at[peer],
            recv_sem=lvl_recv_sem.at[src_dev],
            device_id={"tm": peer},
            device_id_type=MESH,
        )

    for i in range(1, n_tm):
        lvl(lax.rem(me + i, n_tm), me).start()
    lvl_recv[me] = lvl_send[...]
    for i in range(1, n_tm):
        lvl(lax.rem(me + i, n_tm), me).wait_send()
    for i in range(1, n_tm):
        src = lax.rem(me + n_tm - i, n_tm)
        lvl(src, src).wait_recv()

    level = lvl_recv[0]
    for s in range(1, n_tm):
        level = level + lvl_recv[s]
    level = level / F

    mask = dead_ref[...].astype(jnp.float32)
    channels = record_ref.shape[0]
    local_index = sources_ref[...] - mc * channels
    onehot = (lax.broadcasted_iota(jnp.int32, (channels, local_index.shape[1]), 0)
              == local_index).astype(jnp.bfloat16)
    per = NWIN * 2 * bins_dev // n_chan
    halves = bins_dev // per
    src_send[...] = jnp.zeros_like(src_send)
    for w in range(NWIN):
        re = spec[w, 0:bins_dev, :]
        im = spec[w, bins_dev:2 * bins_dev, :]
        mag = jnp.sqrt(re * re + im * im)
        den = mag + 0.1 * level[w:w + 1, :] + 1e-06
        for p, part in enumerate((re, im)):
            white = (part / den).astype(jnp.bfloat16).astype(jnp.float32) * mask
            for k in range(bins_dev):
                white_ref[k, 2 * w + p:2 * w + p + 1, :] = white[k:k + 1, :]
                if p == 0:
                    rot_ref[k, 2 * w + 1:2 * w + 2, :] = -white[k:k + 1, :]
                else:
                    rot_ref[k, 2 * w:2 * w + 1, :] = white[k:k + 1, :]
            picked = jnp.dot(
                white.astype(jnp.bfloat16), onehot, preferred_element_type=jnp.float32
            )
            for h in range(halves):
                src_send[(2 * w + p) * halves + h, 0:per, :] = picked[h * per:(h + 1) * per, :]

    def rsc(peer, src_dev):
        return pltpu.make_async_remote_copy(
            src_ref=src_send.at[peer],
            dst_ref=rs_recv.at[src_dev],
            send_sem=src_send_sem.at[peer],
            recv_sem=src_recv_sem.at[src_dev],
            device_id={"chan": peer},
            device_id_type=MESH,
        )

    for i in range(1, n_chan):
        rsc(lax.rem(mc + i, n_chan), mc).start()
    rs_recv[mc] = src_send[mc]
    for i in range(1, n_chan):
        rsc(lax.rem(mc + i, n_chan), mc).wait_send()
    for i in range(1, n_chan):
        src = lax.rem(mc + n_chan - i, n_chan)
        rsc(src, src).wait_recv()

    total = rs_recv[0]
    for s in range(1, n_chan):
        total = total + rs_recv[s]
    ag_send[...] = total

    def agc(peer, src_dev):
        return pltpu.make_async_remote_copy(
            src_ref=ag_send,
            dst_ref=ag_recv.at[src_dev],
            send_sem=ag_send_sem.at[peer],
            recv_sem=ag_recv_sem.at[src_dev],
            device_id={"chan": peer},
            device_id_type=MESH,
        )

    for i in range(1, n_chan):
        agc(lax.rem(mc + i, n_chan), mc).start()
    ag_recv[mc] = ag_send[...]
    for i in range(1, n_chan):
        agc(lax.rem(mc + i, n_chan), mc).wait_send()
    for i in range(1, n_chan):
        src = lax.rem(mc + n_chan - i, n_chan)
        agc(src, src).wait_recv()

    for i in range(NWIN * 2):
        for h in range(halves):
            for r in range(per):
                k = h * per + r
                srcspec_ref[k, i:i + 1, :] = ag_recv[i * halves + h, r:r + 1, :]


def fused_exchange(offsets, record, dead, sources, n_tm, n_chan, bins_dev, first, count):
    channels, span = record.shape
    nsrc = sources.shape[1]
    group = 16
    vmem = pl.BlockSpec(memory_space=pltpu.VMEM)
    return pl.pallas_call(
        functools.partial(_fused_kernel, n_tm, n_chan, bins_dev, first, count),
        out_shape=(
            jax.ShapeDtypeStruct((bins_dev, NWIN * 2, channels), jnp.float32),
            jax.ShapeDtypeStruct((bins_dev, NWIN * 2, channels), jnp.float32),
            jax.ShapeDtypeStruct((bins_dev, NWIN * 2, nsrc), jnp.float32),
        ),
        in_specs=[pl.BlockSpec(memory_space=pltpu.SMEM), vmem, vmem, vmem],
        out_specs=(vmem, vmem, vmem),
        scratch_shapes=[
            pltpu.VMEM((SLOTS, n_tm, span), jnp.float32),
            pltpu.VMEM((SLOTS, n_tm, span), jnp.float32),
            pltpu.VMEM((SLOTS, 2 * bins_dev, span), jnp.float32),
            pltpu.VMEM((SLOTS, 2 * bins_dev, span), jnp.float32),
            pltpu.VMEM((SLOTS, channels, span), jnp.bfloat16),
            pltpu.VMEM((n_tm, SLOTS, 2 * bins_dev, channels), jnp.float32),
            pltpu.VMEM((group * 2 * bins_dev, span), jnp.float32),
            pltpu.VMEM((n_tm, SLOTS, 2 * bins_dev, channels), jnp.float32),
            pltpu.VMEM((NWIN, 2 * bins_dev, channels), jnp.float32),
            pltpu.VMEM((8, channels), jnp.float32),
            pltpu.VMEM((n_tm, 8, channels), jnp.float32),
            pltpu.VMEM((n_chan, 16, nsrc), jnp.float32),
            pltpu.SemaphoreType.DMA((n_tm, SLOTS)),
            pltpu.SemaphoreType.DMA((n_tm, SLOTS)),
            pltpu.SemaphoreType.DMA((n_tm,)),
            pltpu.SemaphoreType.DMA((n_tm,)),
            pltpu.SemaphoreType.DMA((n_chan,)),
            pltpu.SemaphoreType.DMA((n_chan,)),
            pltpu.VMEM((n_chan, 16, nsrc), jnp.float32),
            pltpu.VMEM((16, nsrc), jnp.float32),
            pltpu.SemaphoreType.DMA((n_chan,)),
            pltpu.SemaphoreType.DMA((n_chan,)),
            pltpu.VMEM((n_chan, 16, nsrc), jnp.float32),
        ],
        compiler_params=pltpu.CompilerParams(collective_id=0, has_side_effects=True),
    )(offsets, record, dead, sources)


def shards(record, offsets, dead_mask, sources):
    n_tm = lax.axis_size("tm")
    n_chan = lax.axis_size("chan")
    bins_dev = F // n_tm
    channels, span = record.shape
    first, count = window_plan(n_tm, span)
    per = NWIN * 2 * bins_dev // n_chan
    assert per * n_chan == NWIN * 2 * bins_dev and bins_dev % per == 0 and per <= 16
    white, rotated, source_spec = fused_exchange(
        offsets, record, dead_mask.reshape(1, channels), sources.reshape(1, -1),
        n_tm, n_chan, bins_dev, first, count
    )
    return cross_spectra(source_spec, white, rotated)


def solution(mesh):
    return jax.shard_map(
        shards,
        mesh=mesh,
        in_specs=(P("chan", "tm"), P(), P("chan"), P()),
        out_specs=P("tm", None, None, "chan"),
        check_vma=False,
    )
```

```python
import functools
import math

import jax
import jax.numpy as jnp
from jax import lax
from jax.experimental import pallas as pl
from jax.experimental.pallas import tpu as pltpu
from jax.sharding import PartitionSpec as P

W = 12000
F = 640
FLO = 6
NWIN = 4
SLOTS = 2
FA = 64

MESH = pl.DeviceIdType.MESH


def window_plan(n_tm, span):
    total = n_tm * span
    slack = total - NWIN * W
    lows = [0] + [w * W for w in range(1, NWIN - 1)] + [total - W]
    highs = [0] + [w * W + slack for w in range(1, NWIN - 1)] + [total - W]
    first, count = [], []
    for d in range(n_tm):
        meets = [w for w in range(NWIN) if lows[w] < (d + 1) * span and highs[w] + W > d * span]
        assert meets and meets == list(range(meets[0], meets[0] + len(meets)))
        assert len(meets) <= SLOTS
        first.append(meets[0])
        count.append(len(meets))
    return first, count


def _cross_kernel(bins_dev, src_ref, white_ref, rot_ref, out_ref):
    for k in range(bins_dev):
        left = src_ref[k].astype(jnp.bfloat16)
        for p, right_ref in enumerate((white_ref, rot_ref)):
            out_ref[k, p] = lax.dot_general(
                left, right_ref[k].astype(jnp.bfloat16), (((0,), (0,)), ((), ())),
                preferred_element_type=jnp.float32,
            ) / NWIN


def cross_spectra(source_spec, white, rotated):
    bins_dev, _, nsrc = source_spec.shape
    channels = white.shape[2]
    vmem = pl.BlockSpec(memory_space=pltpu.VMEM)
    return pl.pallas_call(
        functools.partial(_cross_kernel, bins_dev),
        out_shape=jax.ShapeDtypeStruct((bins_dev, 2, nsrc, channels), jnp.float32),
        in_specs=[vmem] * 3,
        out_specs=vmem,
    )(source_spec, white, rotated)


def _any_of(me, members):
    hit = jnp.bool_(False)
    for m in members:
        hit = hit | (me == m)
    return hit


def _fused_kernel(n_tm, n_chan, bins_dev, first, count,
                  offsets_ref, record_ref, dead_ref, sources_ref,
                  white_ref, rot_ref, srcspec_ref,
                  ar_ref, ai_ref, c1_ref, c2_ref, x_ref,
                  blocks_ref, lhs, recv, spec, lvl_send, lvl_recv, src_send,
                  a2a_send_sem, a2a_recv_sem, lvl_send_sem, lvl_recv_sem,
                  src_send_sem, src_recv_sem, rs_recv, ag_send, ag_send_sem, ag_recv_sem,
                  ag_recv):
    me = lax.axis_index("tm")
    mc = lax.axis_index("chan")
    two = [d for d in range(n_tm) if count[d] == 2]
    me_two = _any_of(me, two)
    rows = 2 * bins_dev
    group = lhs.shape[0] // rows

    barrier = pltpu.get_barrier_semaphore()
    for i in range(1, n_chan):
        pl.semaphore_signal(barrier, inc=1, device_id={"chan": lax.rem(mc + i, n_chan)},
                            device_id_type=MESH)
    for i in range(1, n_tm):
        pl.semaphore_signal(barrier, inc=1, device_id={"tm": lax.rem(me + i, n_tm)},
                            device_id_type=MESH)

    span = record_ref.shape[1]
    wa = jnp.int32(0)
    for d in range(n_tm):
        wa = jnp.where(me == d, first[d], wa)
    local_times = me * span + lax.broadcasted_iota(jnp.int32, (1, span), 1)
    coarse = FLO + bins_dev * lax.broadcasted_iota(jnp.int32, (n_tm, 1), 0)
    fine_row = lax.broadcasted_iota(jnp.int32, (2 * bins_dev, 1), 0)
    fine = lax.rem(fine_row, bins_dev)
    scale = 2.0 * math.pi / W

    def prepare(slot):
        window = wa + slot
        origin = offsets_ref[jnp.minimum(window, NWIN - 1)]
        shifted = local_times - origin
        inside = (shifted >= 0) & (shifted < W) & (window < NWIN)
        times = jnp.where(inside, shifted, 0)
        angle = lax.rem(coarse * times, W).astype(jnp.float32) * scale
        ar_ref[slot] = jnp.cos(angle)
        ai_ref[slot] = -jnp.sin(angle)
        angle = lax.rem(fine * times, W).astype(jnp.float32) * scale
        cos, sin = jnp.cos(angle), jnp.sin(angle)
        top = fine_row < bins_dev
        c1_ref[slot] = jnp.where(top, cos, -sin)
        c2_ref[slot] = jnp.where(top, sin, cos)
        x_ref[slot] = jnp.where(inside, record_ref[...], jnp.zeros_like(record_ref[...]))

    prepare(0)

    @pl.when(me_two)
    def _():
        prepare(1)

    def a2a(peer, slot, src_dev):
        return pltpu.make_async_remote_copy(
            src_ref=blocks_ref.at[peer, slot],
            dst_ref=recv.at[src_dev, slot],
            send_sem=a2a_send_sem.at[peer, slot],
            recv_sem=a2a_recv_sem.at[src_dev, slot],
            device_id={"tm": peer},
            device_id_type=MESH,
        )

    def compute(g, slot):
        c1 = c1_ref[slot]
        c2 = c2_ref[slot]
        for dd in range(0, group, 2):
            pair = []
            for e in range(2):
                d = lax.rem(me + g * group + dd + e, n_tm)
                ar = ar_ref[slot, pl.ds(d, 1), :]
                ai = ai_ref[slot, pl.ds(d, 1), :]
                pair.append(ar * c1 + ai * c2)
            lhs[dd * rows:(dd + 2) * rows, :] = jnp.concatenate(pair, axis=0).astype(jnp.bfloat16)
        res = lax.dot_general(
            lhs[...], x_ref[slot], (((1,), (1,)), ((), ())),
            preferred_element_type=jnp.float32,
        )
        for dd in range(group):
            d = lax.rem(me + g * group + dd, n_tm)
            blocks_ref[d, slot] = res[dd * rows:(dd + 1) * rows, :]

    def send(g, slot):
        for dd in range(group):
            if g == 0 and dd == 0:
                continue
            a2a(lax.rem(me + g * group + dd, n_tm), slot, me).start()

    for g in range(n_tm // group):
        compute(g, 0)
        if g == 0:
            pl.semaphore_wait(barrier, n_tm - 1 + n_chan - 1)
        send(g, 0)

        @pl.when(me_two)
        def _():
            compute(g, 1)
            send(g, 1)

    recv[me, 0] = blocks_ref[me, 0]

    @pl.when(me_two)
    def _():
        recv[me, 1] = blocks_ref[me, 1]

    for i in range(1, n_tm):
        peer = lax.rem(me + i, n_tm)
        a2a(peer, 0, me).wait_send()

        @pl.when(me_two)
        def _():
            a2a(peer, 1, me).wait_send()

    for s in range(n_tm):
        @pl.when(me != s)
        def _():
            a2a(s, 0, s).wait_recv()
            if count[s] == 2:
                a2a(s, 1, s).wait_recv()

    for w in range(NWIN):
        acc = None
        for s in range(n_tm):
            for j in range(count[s]):
                if first[s] + j == w:
                    part = recv[s, j]
                    acc = part if acc is None else acc + part
        spec[w] = acc

    rows = []
    for w in range(NWIN):
        re = spec[w, 0:bins_dev, :]
        im = spec[w, bins_dev:2 * bins_dev, :]
        mag = jnp.sqrt(re * re + im * im)
        rows.append(jnp.sum(mag, axis=0, keepdims=True))
    rows.append(jnp.zeros((8 - NWIN, rows[0].shape[1]), jnp.float32))
    lvl_send[...] = jnp.concatenate(rows, axis=0)

    def lvl(peer, src_dev):
        return pltpu.make_async_remote_copy(
            src_ref=lvl_send,
            dst_ref=lvl_recv.at[src_dev],
            send_sem=lvl_send_sem.at[peer],
            recv_sem=lvl_recv_sem.at[src_dev],
            device_id={"tm": peer},
            device_id_type=MESH,
        )

    for i in range(1, n_tm):
        lvl(lax.rem(me + i, n_tm), me).start()
    lvl_recv[me] = lvl_send[...]
    for i in range(1, n_tm):
        lvl(lax.rem(me + i, n_tm), me).wait_send()
    for i in range(1, n_tm):
        src = lax.rem(me + n_tm - i, n_tm)
        lvl(src, src).wait_recv()

    level = lvl_recv[0]
    for s in range(1, n_tm):
        level = level + lvl_recv[s]
    level = level / F

    mask = dead_ref[...].astype(jnp.float32)
    channels = record_ref.shape[0]
    local_index = sources_ref[...] - mc * channels
    onehot = (lax.broadcasted_iota(jnp.int32, (channels, local_index.shape[1]), 0)
              == local_index).astype(jnp.bfloat16)
    per = NWIN * 2 * bins_dev // n_chan
    halves = bins_dev // per
    src_send[...] = jnp.zeros_like(src_send)
    for w in range(NWIN):
        re = spec[w, 0:bins_dev, :]
        im = spec[w, bins_dev:2 * bins_dev, :]
        mag = jnp.sqrt(re * re + im * im)
        den = mag + 0.1 * level[w:w + 1, :] + 1e-06
        for p, part in enumerate((re, im)):
            white = (part / den).astype(jnp.bfloat16).astype(jnp.float32) * mask
            for k in range(bins_dev):
                white_ref[k, 2 * w + p:2 * w + p + 1, :] = white[k:k + 1, :]
                if p == 0:
                    rot_ref[k, 2 * w + 1:2 * w + 2, :] = -white[k:k + 1, :]
                else:
                    rot_ref[k, 2 * w:2 * w + 1, :] = white[k:k + 1, :]
            picked = jnp.dot(
                white.astype(jnp.bfloat16), onehot, preferred_element_type=jnp.float32
            )
            for h in range(halves):
                src_send[(2 * w + p) * halves + h, 0:per, :] = picked[h * per:(h + 1) * per, :]

    def rsc(peer, src_dev):
        return pltpu.make_async_remote_copy(
            src_ref=src_send.at[peer],
            dst_ref=rs_recv.at[src_dev],
            send_sem=src_send_sem.at[peer],
            recv_sem=src_recv_sem.at[src_dev],
            device_id={"chan": peer},
            device_id_type=MESH,
        )

    for i in range(1, n_chan):
        rsc(lax.rem(mc + i, n_chan), mc).start()
    rs_recv[mc] = src_send[mc]
    for i in range(1, n_chan):
        rsc(lax.rem(mc + i, n_chan), mc).wait_send()
    for i in range(1, n_chan):
        src = lax.rem(mc + n_chan - i, n_chan)
        rsc(src, src).wait_recv()

    total = rs_recv[0]
    for s in range(1, n_chan):
        total = total + rs_recv[s]
    ag_send[...] = total

    def agc(peer, src_dev):
        return pltpu.make_async_remote_copy(
            src_ref=ag_send,
            dst_ref=ag_recv.at[src_dev],
            send_sem=ag_send_sem.at[peer],
            recv_sem=ag_recv_sem.at[src_dev],
            device_id={"chan": peer},
            device_id_type=MESH,
        )

    for i in range(1, n_chan):
        agc(lax.rem(mc + i, n_chan), mc).start()
    ag_recv[mc] = ag_send[...]
    for i in range(1, n_chan):
        agc(lax.rem(mc + i, n_chan), mc).wait_send()
    for i in range(1, n_chan):
        src = lax.rem(mc + n_chan - i, n_chan)
        agc(src, src).wait_recv()

    for i in range(NWIN * 2):
        for h in range(halves):
            for r in range(per):
                k = h * per + r
                srcspec_ref[k, i:i + 1, :] = ag_recv[i * halves + h, r:r + 1, :]


def fused_exchange(offsets, record, dead, sources, n_tm, n_chan, bins_dev, first, count):
    channels, span = record.shape
    nsrc = sources.shape[1]
    group = 16
    vmem = pl.BlockSpec(memory_space=pltpu.VMEM)
    return pl.pallas_call(
        functools.partial(_fused_kernel, n_tm, n_chan, bins_dev, first, count),
        out_shape=(
            jax.ShapeDtypeStruct((bins_dev, NWIN * 2, channels), jnp.float32),
            jax.ShapeDtypeStruct((bins_dev, NWIN * 2, channels), jnp.float32),
            jax.ShapeDtypeStruct((bins_dev, NWIN * 2, nsrc), jnp.float32),
        ),
        in_specs=[pl.BlockSpec(memory_space=pltpu.SMEM), vmem, vmem, vmem],
        out_specs=(vmem, vmem, vmem),
        scratch_shapes=[
            pltpu.VMEM((SLOTS, n_tm, span), jnp.float32),
            pltpu.VMEM((SLOTS, n_tm, span), jnp.float32),
            pltpu.VMEM((SLOTS, 2 * bins_dev, span), jnp.float32),
            pltpu.VMEM((SLOTS, 2 * bins_dev, span), jnp.float32),
            pltpu.VMEM((SLOTS, channels, span), jnp.bfloat16),
            pltpu.VMEM((n_tm, SLOTS, 2 * bins_dev, channels), jnp.float32),
            pltpu.VMEM((group * 2 * bins_dev, span), jnp.bfloat16),
            pltpu.VMEM((n_tm, SLOTS, 2 * bins_dev, channels), jnp.float32),
            pltpu.VMEM((NWIN, 2 * bins_dev, channels), jnp.float32),
            pltpu.VMEM((8, channels), jnp.float32),
            pltpu.VMEM((n_tm, 8, channels), jnp.float32),
            pltpu.VMEM((n_chan, 16, nsrc), jnp.float32),
            pltpu.SemaphoreType.DMA((n_tm, SLOTS)),
            pltpu.SemaphoreType.DMA((n_tm, SLOTS)),
            pltpu.SemaphoreType.DMA((n_tm,)),
            pltpu.SemaphoreType.DMA((n_tm,)),
            pltpu.SemaphoreType.DMA((n_chan,)),
            pltpu.SemaphoreType.DMA((n_chan,)),
            pltpu.VMEM((n_chan, 16, nsrc), jnp.float32),
            pltpu.VMEM((16, nsrc), jnp.float32),
            pltpu.SemaphoreType.DMA((n_chan,)),
            pltpu.SemaphoreType.DMA((n_chan,)),
            pltpu.VMEM((n_chan, 16, nsrc), jnp.float32),
        ],
        compiler_params=pltpu.CompilerParams(collective_id=0, has_side_effects=True),
    )(offsets, record, dead, sources)


def shards(record, offsets, dead_mask, sources):
    n_tm = lax.axis_size("tm")
    n_chan = lax.axis_size("chan")
    bins_dev = F // n_tm
    channels, span = record.shape
    first, count = window_plan(n_tm, span)
    per = NWIN * 2 * bins_dev // n_chan
    assert per * n_chan == NWIN * 2 * bins_dev and bins_dev % per == 0 and per <= 16
    white, rotated, source_spec = fused_exchange(
        offsets, record, dead_mask.reshape(1, channels), sources.reshape(1, -1),
        n_tm, n_chan, bins_dev, first, count
    )
    return cross_spectra(source_spec, white, rotated)


def solution(mesh):
    return jax.shard_map(
        shards,
        mesh=mesh,
        in_specs=(P("chan", "tm"), P(), P("chan"), P()),
        out_specs=P("tm", None, None, "chan"),
        check_vma=False,
    )
```

```python
import functools
import math

import jax
import jax.numpy as jnp
from jax import lax
from jax.experimental import pallas as pl
from jax.experimental.pallas import tpu as pltpu
from jax.sharding import PartitionSpec as P

W = 12000
F = 640
FLO = 6
NWIN = 4
SLOTS = 2
FA = 64

MESH = pl.DeviceIdType.MESH


def window_plan(n_tm, span):
    total = n_tm * span
    slack = total - NWIN * W
    lows = [0] + [w * W for w in range(1, NWIN - 1)] + [total - W]
    highs = [0] + [w * W + slack for w in range(1, NWIN - 1)] + [total - W]
    first, count = [], []
    for d in range(n_tm):
        meets = [w for w in range(NWIN) if lows[w] < (d + 1) * span and highs[w] + W > d * span]
        assert meets and meets == list(range(meets[0], meets[0] + len(meets)))
        assert len(meets) <= SLOTS
        first.append(meets[0])
        count.append(len(meets))
    return first, count


def _cross_kernel(bins_dev, src_ref, white_ref, rot_ref, out_ref):
    for k in range(bins_dev):
        left = src_ref[k].astype(jnp.bfloat16)
        for p, right_ref in enumerate((white_ref, rot_ref)):
            out_ref[k, p] = lax.dot_general(
                left, right_ref[k].astype(jnp.bfloat16), (((0,), (0,)), ((), ())),
                preferred_element_type=jnp.float32,
            ) / NWIN


def cross_spectra(source_spec, white, rotated):
    bins_dev, _, nsrc = source_spec.shape
    channels = white.shape[2]
    vmem = pl.BlockSpec(memory_space=pltpu.VMEM)
    return pl.pallas_call(
        functools.partial(_cross_kernel, bins_dev),
        out_shape=jax.ShapeDtypeStruct((bins_dev, 2, nsrc, channels), jnp.float32),
        in_specs=[vmem] * 3,
        out_specs=vmem,
    )(source_spec, white, rotated)


def _any_of(me, members):
    hit = jnp.bool_(False)
    for m in members:
        hit = hit | (me == m)
    return hit


def _fused_kernel(n_tm, n_chan, bins_dev, first, count,
                  offsets_ref, record_ref, dead_ref, sources_ref,
                  white_ref, rot_ref, srcspec_ref,
                  ar_ref, ai_ref, c1_ref, c2_ref, x_ref,
                  blocks_ref, lhs, recv, spec, lvl_send, lvl_recv, src_send,
                  a2a_send_sem, a2a_recv_sem, lvl_send_sem, lvl_recv_sem,
                  src_send_sem, src_recv_sem, rs_recv, ag_send, ag_send_sem, ag_recv_sem,
                  ag_recv):
    me = lax.axis_index("tm")
    mc = lax.axis_index("chan")
    two = [d for d in range(n_tm) if count[d] == 2]
    me_two = _any_of(me, two)
    rows = 2 * bins_dev
    group = lhs.shape[0] // rows

    barrier = pltpu.get_barrier_semaphore()
    for i in range(1, n_chan):
        pl.semaphore_signal(barrier, inc=1, device_id={"chan": lax.rem(mc + i, n_chan)},
                            device_id_type=MESH)
    for i in range(1, n_tm):
        pl.semaphore_signal(barrier, inc=1, device_id={"tm": lax.rem(me + i, n_tm)},
                            device_id_type=MESH)

    span = record_ref.shape[1]
    wa = jnp.int32(0)
    for d in range(n_tm):
        wa = jnp.where(me == d, first[d], wa)
    local_times = me * span + lax.broadcasted_iota(jnp.int32, (1, span), 1)
    coarse = FLO + bins_dev * lax.broadcasted_iota(jnp.int32, (n_tm, 1), 0)
    fine_row = lax.broadcasted_iota(jnp.int32, (2 * bins_dev, 1), 0)
    fine = lax.rem(fine_row, bins_dev)
    scale = 2.0 * math.pi / W

    def prepare(slot):
        window = wa + slot
        origin = offsets_ref[jnp.minimum(window, NWIN - 1)]
        shifted = local_times - origin
        inside = (shifted >= 0) & (shifted < W) & (window < NWIN)
        times = jnp.where(inside, shifted, 0)
        angle = lax.rem(coarse * times, W).astype(jnp.float32) * scale
        ar_ref[slot] = jnp.cos(angle)
        ai_ref[slot] = -jnp.sin(angle)
        angle = lax.rem(fine * times, W).astype(jnp.float32) * scale
        cos, sin = jnp.cos(angle), jnp.sin(angle)
        top = fine_row < bins_dev
        c1_ref[slot] = jnp.where(top, cos, -sin)
        c2_ref[slot] = jnp.where(top, sin, cos)
        x_ref[slot] = jnp.where(inside, record_ref[...], jnp.zeros_like(record_ref[...]))

    prepare(0)

    @pl.when(me_two)
    def _():
        prepare(1)

    def a2a(peer, slot, src_dev):
        return pltpu.make_async_remote_copy(
            src_ref=blocks_ref.at[peer, slot],
            dst_ref=recv.at[src_dev, slot],
            send_sem=a2a_send_sem.at[peer, slot],
            recv_sem=a2a_recv_sem.at[src_dev, slot],
            device_id={"tm": peer},
            device_id_type=MESH,
        )

    def compute(g, slot):
        c1 = c1_ref[slot]
        c2 = c2_ref[slot]
        for dd in range(group):
            d = lax.rem(me + g * group + dd, n_tm)
            ar = ar_ref[slot, pl.ds(d, 1), :]
            ai = ai_ref[slot, pl.ds(d, 1), :]
            lhs[dd * rows:(dd + 1) * rows, :] = ar * c1 + ai * c2
        res = lax.dot_general(
            lhs[...].astype(jnp.bfloat16), x_ref[slot], (((1,), (1,)), ((), ())),
            preferred_element_type=jnp.float32,
        )
        for dd in range(group):
            d = lax.rem(me + g * group + dd, n_tm)
            blocks_ref[d, slot] = res[dd * rows:(dd + 1) * rows, :]

    def send(g, slot):
        for dd in range(group):
            if g == 0 and dd == 0:
                continue
            a2a(lax.rem(me + g * group + dd, n_tm), slot, me).start()

    for g in range(n_tm // group):
        compute(g, 0)
        if g == 0:
            @pl.when(me_two)
            def _():
                compute(0, 1)

            pl.semaphore_wait(barrier, n_tm - 1 + n_chan - 1)
        send(g, 0)

        @pl.when(me_two)
        def _():
            if g > 0:
                compute(g, 1)
            send(g, 1)

    recv[me, 0] = blocks_ref[me, 0]

    @pl.when(me_two)
    def _():
        recv[me, 1] = blocks_ref[me, 1]

    for i in range(1, n_tm):
        peer = lax.rem(me + i, n_tm)
        a2a(peer, 0, me).wait_send()

        @pl.when(me_two)
        def _():
            a2a(peer, 1, me).wait_send()

    for s in range(n_tm):
        @pl.when(me != s)
        def _():
            a2a(s, 0, s).wait_recv()
            if count[s] == 2:
                a2a(s, 1, s).wait_recv()

    for w in range(NWIN):
        acc = None
        for s in range(n_tm):
            for j in range(count[s]):
                if first[s] + j == w:
                    part = recv[s, j]
                    acc = part if acc is None else acc + part
        spec[w] = acc

    rows = []
    for w in range(NWIN):
        re = spec[w, 0:bins_dev, :]
        im = spec[w, bins_dev:2 * bins_dev, :]
        mag = jnp.sqrt(re * re + im * im)
        rows.append(jnp.sum(mag, axis=0, keepdims=True))
    rows.append(jnp.zeros((8 - NWIN, rows[0].shape[1]), jnp.float32))
    lvl_send[...] = jnp.concatenate(rows, axis=0)

    def lvl(peer, src_dev):
        return pltpu.make_async_remote_copy(
            src_ref=lvl_send,
            dst_ref=lvl_recv.at[src_dev],
            send_sem=lvl_send_sem.at[peer],
            recv_sem=lvl_recv_sem.at[src_dev],
            device_id={"tm": peer},
            device_id_type=MESH,
        )

    for i in range(1, n_tm):
        lvl(lax.rem(me + i, n_tm), me).start()
    lvl_recv[me] = lvl_send[...]
    for i in range(1, n_tm):
        lvl(lax.rem(me + i, n_tm), me).wait_send()
    for i in range(1, n_tm):
        src = lax.rem(me + n_tm - i, n_tm)
        lvl(src, src).wait_recv()

    level = lvl_recv[0]
    for s in range(1, n_tm):
        level = level + lvl_recv[s]
    level = level / F

    mask = dead_ref[...].astype(jnp.float32)
    channels = record_ref.shape[0]
    local_index = sources_ref[...] - mc * channels
    onehot = (lax.broadcasted_iota(jnp.int32, (channels, local_index.shape[1]), 0)
              == local_index).astype(jnp.bfloat16)
    per = NWIN * 2 * bins_dev // n_chan
    halves = bins_dev // per
    src_send[...] = jnp.zeros_like(src_send)
    for w in range(NWIN):
        re = spec[w, 0:bins_dev, :]
        im = spec[w, bins_dev:2 * bins_dev, :]
        mag = jnp.sqrt(re * re + im * im)
        den = mag + 0.1 * level[w:w + 1, :] + 1e-06
        for p, part in enumerate((re, im)):
            white = (part / den).astype(jnp.bfloat16).astype(jnp.float32) * mask
            for k in range(bins_dev):
                white_ref[k, 2 * w + p:2 * w + p + 1, :] = white[k:k + 1, :]
                if p == 0:
                    rot_ref[k, 2 * w + 1:2 * w + 2, :] = -white[k:k + 1, :]
                else:
                    rot_ref[k, 2 * w:2 * w + 1, :] = white[k:k + 1, :]
            picked = jnp.dot(
                white.astype(jnp.bfloat16), onehot, preferred_element_type=jnp.float32
            )
            for h in range(halves):
                src_send[(2 * w + p) * halves + h, 0:per, :] = picked[h * per:(h + 1) * per, :]

    def rsc(peer, src_dev):
        return pltpu.make_async_remote_copy(
            src_ref=src_send.at[peer],
            dst_ref=rs_recv.at[src_dev],
            send_sem=src_send_sem.at[peer],
            recv_sem=src_recv_sem.at[src_dev],
            device_id={"chan": peer},
            device_id_type=MESH,
        )

    for i in range(1, n_chan):
        rsc(lax.rem(mc + i, n_chan), mc).start()
    rs_recv[mc] = src_send[mc]
    for i in range(1, n_chan):
        rsc(lax.rem(mc + i, n_chan), mc).wait_send()
    for i in range(1, n_chan):
        src = lax.rem(mc + n_chan - i, n_chan)
        rsc(src, src).wait_recv()

    total = rs_recv[0]
    for s in range(1, n_chan):
        total = total + rs_recv[s]
    ag_send[...] = total

    def agc(peer, src_dev):
        return pltpu.make_async_remote_copy(
            src_ref=ag_send,
            dst_ref=ag_recv.at[src_dev],
            send_sem=ag_send_sem.at[peer],
            recv_sem=ag_recv_sem.at[src_dev],
            device_id={"chan": peer},
            device_id_type=MESH,
        )

    for i in range(1, n_chan):
        agc(lax.rem(mc + i, n_chan), mc).start()
    ag_recv[mc] = ag_send[...]
    for i in range(1, n_chan):
        agc(lax.rem(mc + i, n_chan), mc).wait_send()
    for i in range(1, n_chan):
        src = lax.rem(mc + n_chan - i, n_chan)
        agc(src, src).wait_recv()

    for i in range(NWIN * 2):
        for h in range(halves):
            for r in range(per):
                k = h * per + r
                srcspec_ref[k, i:i + 1, :] = ag_recv[i * halves + h, r:r + 1, :]


def fused_exchange(offsets, record, dead, sources, n_tm, n_chan, bins_dev, first, count):
    channels, span = record.shape
    nsrc = sources.shape[1]
    group = 16
    vmem = pl.BlockSpec(memory_space=pltpu.VMEM)
    return pl.pallas_call(
        functools.partial(_fused_kernel, n_tm, n_chan, bins_dev, first, count),
        out_shape=(
            jax.ShapeDtypeStruct((bins_dev, NWIN * 2, channels), jnp.float32),
            jax.ShapeDtypeStruct((bins_dev, NWIN * 2, channels), jnp.float32),
            jax.ShapeDtypeStruct((bins_dev, NWIN * 2, nsrc), jnp.float32),
        ),
        in_specs=[pl.BlockSpec(memory_space=pltpu.SMEM), vmem, vmem, vmem],
        out_specs=(vmem, vmem, vmem),
        scratch_shapes=[
            pltpu.VMEM((SLOTS, n_tm, span), jnp.float32),
            pltpu.VMEM((SLOTS, n_tm, span), jnp.float32),
            pltpu.VMEM((SLOTS, 2 * bins_dev, span), jnp.float32),
            pltpu.VMEM((SLOTS, 2 * bins_dev, span), jnp.float32),
            pltpu.VMEM((SLOTS, channels, span), jnp.bfloat16),
            pltpu.VMEM((n_tm, SLOTS, 2 * bins_dev, channels), jnp.float32),
            pltpu.VMEM((group * 2 * bins_dev, span), jnp.float32),
            pltpu.VMEM((n_tm, SLOTS, 2 * bins_dev, channels), jnp.float32),
            pltpu.VMEM((NWIN, 2 * bins_dev, channels), jnp.float32),
            pltpu.VMEM((8, channels), jnp.float32),
            pltpu.VMEM((n_tm, 8, channels), jnp.float32),
            pltpu.VMEM((n_chan, 16, nsrc), jnp.float32),
            pltpu.SemaphoreType.DMA((n_tm, SLOTS)),
            pltpu.SemaphoreType.DMA((n_tm, SLOTS)),
            pltpu.SemaphoreType.DMA((n_tm,)),
            pltpu.SemaphoreType.DMA((n_tm,)),
            pltpu.SemaphoreType.DMA((n_chan,)),
            pltpu.SemaphoreType.DMA((n_chan,)),
            pltpu.VMEM((n_chan, 16, nsrc), jnp.float32),
            pltpu.VMEM((16, nsrc), jnp.float32),
            pltpu.SemaphoreType.DMA((n_chan,)),
            pltpu.SemaphoreType.DMA((n_chan,)),
            pltpu.VMEM((n_chan, 16, nsrc), jnp.float32),
        ],
        compiler_params=pltpu.CompilerParams(collective_id=0, has_side_effects=True),
    )(offsets, record, dead, sources)


def shards(record, offsets, dead_mask, sources):
    n_tm = lax.axis_size("tm")
    n_chan = lax.axis_size("chan")
    bins_dev = F // n_tm
    channels, span = record.shape
    first, count = window_plan(n_tm, span)
    per = NWIN * 2 * bins_dev // n_chan
    assert per * n_chan == NWIN * 2 * bins_dev and bins_dev % per == 0 and per <= 16
    white, rotated, source_spec = fused_exchange(
        offsets, record, dead_mask.reshape(1, channels), sources.reshape(1, -1),
        n_tm, n_chan, bins_dev, first, count
    )
    return cross_spectra(source_spec, white, rotated)


def solution(mesh):
    return jax.shard_map(
        shards,
        mesh=mesh,
        in_specs=(P("chan", "tm"), P(), P("chan"), P()),
        out_specs=P("tm", None, None, "chan"),
        check_vma=False,
    )
```

```python
import functools
import math

import jax
import jax.numpy as jnp
from jax import lax
from jax.experimental import pallas as pl
from jax.experimental.pallas import tpu as pltpu
from jax.sharding import PartitionSpec as P

W = 12000
F = 640
FLO = 6
NWIN = 4
SLOTS = 2
FA = 64

MESH = pl.DeviceIdType.MESH


def window_plan(n_tm, span):
    total = n_tm * span
    slack = total - NWIN * W
    lows = [0] + [w * W for w in range(1, NWIN - 1)] + [total - W]
    highs = [0] + [w * W + slack for w in range(1, NWIN - 1)] + [total - W]
    first, count = [], []
    for d in range(n_tm):
        meets = [w for w in range(NWIN) if lows[w] < (d + 1) * span and highs[w] + W > d * span]
        assert meets and meets == list(range(meets[0], meets[0] + len(meets)))
        assert len(meets) <= SLOTS
        first.append(meets[0])
        count.append(len(meets))
    return first, count


def _cross_kernel(bins_dev, src_ref, white_ref, rot_ref, out_ref):
    for k in range(bins_dev):
        left = src_ref[k].astype(jnp.bfloat16)
        for p, right_ref in enumerate((white_ref, rot_ref)):
            out_ref[k, p] = lax.dot_general(
                left, right_ref[k].astype(jnp.bfloat16), (((0,), (0,)), ((), ())),
                preferred_element_type=jnp.float32,
            ) / NWIN


def cross_spectra(source_spec, white, rotated):
    bins_dev, _, nsrc = source_spec.shape
    channels = white.shape[2]
    vmem = pl.BlockSpec(memory_space=pltpu.VMEM)
    return pl.pallas_call(
        functools.partial(_cross_kernel, bins_dev),
        out_shape=jax.ShapeDtypeStruct((bins_dev, 2, nsrc, channels), jnp.float32),
        in_specs=[vmem] * 3,
        out_specs=vmem,
    )(source_spec, white, rotated)


def _any_of(me, members):
    hit = jnp.bool_(False)
    for m in members:
        hit = hit | (me == m)
    return hit


def _fused_kernel(n_tm, n_chan, bins_dev, first, count,
                  offsets_ref, record_ref, dead_ref, sources_ref,
                  white_ref, rot_ref, srcspec_ref,
                  ar_ref, ai_ref, c1_ref, c2_ref, x_ref,
                  blocks_ref, lhs, recv, spec, lvl_send, lvl_recv, src_send,
                  a2a_send_sem, a2a_recv_sem, lvl_send_sem, lvl_recv_sem,
                  src_send_sem, src_recv_sem, rs_recv, ag_send, ag_send_sem, ag_recv_sem,
                  ag_recv):
    me = lax.axis_index("tm")
    mc = lax.axis_index("chan")
    two = [d for d in range(n_tm) if count[d] == 2]
    me_two = _any_of(me, two)
    rows = 2 * bins_dev
    group = lhs.shape[0] // rows

    barrier = pltpu.get_barrier_semaphore()
    for i in range(1, n_chan):
        pl.semaphore_signal(barrier, inc=1, device_id={"chan": lax.rem(mc + i, n_chan)},
                            device_id_type=MESH)
    for i in range(1, n_tm):
        pl.semaphore_signal(barrier, inc=1, device_id={"tm": lax.rem(me + i, n_tm)},
                            device_id_type=MESH)

    span = record_ref.shape[1]
    wa = jnp.int32(0)
    for d in range(n_tm):
        wa = jnp.where(me == d, first[d], wa)
    local_times = me * span + lax.broadcasted_iota(jnp.int32, (1, span), 1)
    coarse = FLO + bins_dev * lax.broadcasted_iota(jnp.int32, (n_tm, 1), 0)
    fine_row = lax.broadcasted_iota(jnp.int32, (2 * bins_dev, 1), 0)
    fine = lax.rem(fine_row, bins_dev)
    scale = 2.0 * math.pi / W

    def prepare(slot):
        window = wa + slot
        origin = offsets_ref[jnp.minimum(window, NWIN - 1)]
        shifted = local_times - origin
        inside = (shifted >= 0) & (shifted < W) & (window < NWIN)
        times = jnp.where(inside, shifted, 0)
        angle = lax.rem(coarse * times, W).astype(jnp.float32) * scale
        ar_ref[slot] = jnp.cos(angle)
        ai_ref[slot] = -jnp.sin(angle)
        angle = lax.rem(fine * times, W).astype(jnp.float32) * scale
        cos, sin = jnp.cos(angle), jnp.sin(angle)
        top = fine_row < bins_dev
        c1_ref[slot] = jnp.where(top, cos, -sin)
        c2_ref[slot] = jnp.where(top, sin, cos)
        x_ref[slot] = jnp.where(inside, record_ref[...], jnp.zeros_like(record_ref[...]))

    prepare(0)

    @pl.when(me_two)
    def _():
        prepare(1)

    def a2a(peer, slot, src_dev):
        return pltpu.make_async_remote_copy(
            src_ref=blocks_ref.at[peer, slot],
            dst_ref=recv.at[src_dev, slot],
            send_sem=a2a_send_sem.at[peer, slot],
            recv_sem=a2a_recv_sem.at[src_dev, slot],
            device_id={"tm": peer},
            device_id_type=MESH,
        )

    def compute(g, slot):
        c1 = c1_ref[slot]
        c2 = c2_ref[slot]
        for dd in range(group):
            d = lax.rem(me + g * group + dd, n_tm)
            ar = ar_ref[slot, pl.ds(d, 1), :]
            ai = ai_ref[slot, pl.ds(d, 1), :]
            lhs[dd * rows:(dd + 1) * rows, :] = ar * c1 + ai * c2
        res = lax.dot_general(
            lhs[...].astype(jnp.bfloat16), x_ref[slot], (((1,), (1,)), ((), ())),
            preferred_element_type=jnp.float32,
        )
        for dd in range(group):
            d = lax.rem(me + g * group + dd, n_tm)
            blocks_ref[d, slot] = res[dd * rows:(dd + 1) * rows, :]

    def send(g, slot):
        for dd in range(group):
            if g == 0 and dd == 0:
                continue
            a2a(lax.rem(me + g * group + dd, n_tm), slot, me).start()

    for g in range(n_tm // group):
        compute(g, 0)
        if g == 0:
            pl.semaphore_wait(barrier, n_tm - 1 + n_chan - 1)
        send(g, 0)

        @pl.when(me_two)
        def _():
            compute(g, 1)
            send(g, 1)

    recv[me, 0] = blocks_ref[me, 0]

    @pl.when(me_two)
    def _():
        recv[me, 1] = blocks_ref[me, 1]

    for i in range(1, n_tm):
        peer = lax.rem(me + i, n_tm)
        a2a(peer, 0, me).wait_send()

        @pl.when(me_two)
        def _():
            a2a(peer, 1, me).wait_send()

    for s in range(n_tm):
        @pl.when(me != s)
        def _():
            a2a(s, 0, s).wait_recv()
            if count[s] == 2:
                a2a(s, 1, s).wait_recv()

    for w in range(NWIN):
        acc = None
        for s in range(n_tm):
            for j in range(count[s]):
                if first[s] + j == w:
                    part = recv[s, j]
                    acc = part if acc is None else acc + part
        spec[w] = acc

    rows = []
    for w in range(NWIN):
        re = spec[w, 0:bins_dev, :]
        im = spec[w, bins_dev:2 * bins_dev, :]
        mag = jnp.sqrt(re * re + im * im)
        rows.append(jnp.sum(mag, axis=0, keepdims=True))
    lvl_send[...] = jnp.concatenate(rows, axis=0)

    def lvl(peer, src_dev):
        return pltpu.make_async_remote_copy(
            src_ref=lvl_send,
            dst_ref=lvl_recv.at[src_dev],
            send_sem=lvl_send_sem.at[peer],
            recv_sem=lvl_recv_sem.at[src_dev],
            device_id={"tm": peer},
            device_id_type=MESH,
        )

    for i in range(1, n_tm):
        lvl(lax.rem(me + i, n_tm), me).start()
    lvl_recv[me] = lvl_send[...]
    for i in range(1, n_tm):
        lvl(lax.rem(me + i, n_tm), me).wait_send()
    for i in range(1, n_tm):
        src = lax.rem(me + n_tm - i, n_tm)
        lvl(src, src).wait_recv()

    level = lvl_recv[0]
    for s in range(1, n_tm):
        level = level + lvl_recv[s]
    level = level / F

    mask = dead_ref[...].astype(jnp.float32)
    channels = record_ref.shape[0]
    local_index = sources_ref[...] - mc * channels
    onehot = (lax.broadcasted_iota(jnp.int32, (channels, local_index.shape[1]), 0)
              == local_index).astype(jnp.bfloat16)
    per = NWIN * 2 * bins_dev // n_chan
    halves = bins_dev // per
    src_send[...] = jnp.zeros_like(src_send)
    for w in range(NWIN):
        re = spec[w, 0:bins_dev, :]
        im = spec[w, bins_dev:2 * bins_dev, :]
        mag = jnp.sqrt(re * re + im * im)
        den = mag + 0.1 * level[w:w + 1, :] + 1e-06
        for p, part in enumerate((re, im)):
            white = (part / den).astype(jnp.bfloat16).astype(jnp.float32) * mask
            for k in range(bins_dev):
                white_ref[k, 2 * w + p:2 * w + p + 1, :] = white[k:k + 1, :]
                if p == 0:
                    rot_ref[k, 2 * w + 1:2 * w + 2, :] = -white[k:k + 1, :]
                else:
                    rot_ref[k, 2 * w:2 * w + 1, :] = white[k:k + 1, :]
            picked = jnp.dot(
                white.astype(jnp.bfloat16), onehot, preferred_element_type=jnp.float32
            )
            for h in range(halves):
                src_send[(2 * w + p) * halves + h, 0:per, :] = picked[h * per:(h + 1) * per, :]

    def rsc(peer, src_dev):
        return pltpu.make_async_remote_copy(
            src_ref=src_send.at[peer],
            dst_ref=rs_recv.at[src_dev],
            send_sem=src_send_sem.at[peer],
            recv_sem=src_recv_sem.at[src_dev],
            device_id={"chan": peer},
            device_id_type=MESH,
        )

    for i in range(1, n_chan):
        rsc(lax.rem(mc + i, n_chan), mc).start()
    rs_recv[mc] = src_send[mc]
    for i in range(1, n_chan):
        rsc(lax.rem(mc + i, n_chan), mc).wait_send()
    for i in range(1, n_chan):
        src = lax.rem(mc + n_chan - i, n_chan)
        rsc(src, src).wait_recv()

    total = rs_recv[0]
    for s in range(1, n_chan):
        total = total + rs_recv[s]
    ag_send[...] = total

    def agc(peer, src_dev):
        return pltpu.make_async_remote_copy(
            src_ref=ag_send,
            dst_ref=ag_recv.at[src_dev],
            send_sem=ag_send_sem.at[peer],
            recv_sem=ag_recv_sem.at[src_dev],
            device_id={"chan": peer},
            device_id_type=MESH,
        )

    for i in range(1, n_chan):
        agc(lax.rem(mc + i, n_chan), mc).start()
    ag_recv[mc] = ag_send[...]
    for i in range(1, n_chan):
        agc(lax.rem(mc + i, n_chan), mc).wait_send()
    for i in range(1, n_chan):
        src = lax.rem(mc + n_chan - i, n_chan)
        agc(src, src).wait_recv()

    for i in range(NWIN * 2):
        for h in range(halves):
            for r in range(per):
                k = h * per + r
                srcspec_ref[k, i:i + 1, :] = ag_recv[i * halves + h, r:r + 1, :]


def fused_exchange(offsets, record, dead, sources, n_tm, n_chan, bins_dev, first, count):
    channels, span = record.shape
    nsrc = sources.shape[1]
    group = 16
    vmem = pl.BlockSpec(memory_space=pltpu.VMEM)
    return pl.pallas_call(
        functools.partial(_fused_kernel, n_tm, n_chan, bins_dev, first, count),
        out_shape=(
            jax.ShapeDtypeStruct((bins_dev, NWIN * 2, channels), jnp.float32),
            jax.ShapeDtypeStruct((bins_dev, NWIN * 2, channels), jnp.float32),
            jax.ShapeDtypeStruct((bins_dev, NWIN * 2, nsrc), jnp.float32),
        ),
        in_specs=[pl.BlockSpec(memory_space=pltpu.SMEM), vmem, vmem, vmem],
        out_specs=(vmem, vmem, vmem),
        scratch_shapes=[
            pltpu.VMEM((SLOTS, n_tm, span), jnp.float32),
            pltpu.VMEM((SLOTS, n_tm, span), jnp.float32),
            pltpu.VMEM((SLOTS, 2 * bins_dev, span), jnp.float32),
            pltpu.VMEM((SLOTS, 2 * bins_dev, span), jnp.float32),
            pltpu.VMEM((SLOTS, channels, span), jnp.bfloat16),
            pltpu.VMEM((n_tm, SLOTS, 2 * bins_dev, channels), jnp.float32),
            pltpu.VMEM((group * 2 * bins_dev, span), jnp.float32),
            pltpu.VMEM((n_tm, SLOTS, 2 * bins_dev, channels), jnp.float32),
            pltpu.VMEM((NWIN, 2 * bins_dev, channels), jnp.float32),
            pltpu.VMEM((NWIN, channels), jnp.float32),
            pltpu.VMEM((n_tm, NWIN, channels), jnp.float32),
            pltpu.VMEM((n_chan, 16, nsrc), jnp.float32),
            pltpu.SemaphoreType.DMA((n_tm, SLOTS)),
            pltpu.SemaphoreType.DMA((n_tm, SLOTS)),
            pltpu.SemaphoreType.DMA((n_tm,)),
            pltpu.SemaphoreType.DMA((n_tm,)),
            pltpu.SemaphoreType.DMA((n_chan,)),
            pltpu.SemaphoreType.DMA((n_chan,)),
            pltpu.VMEM((n_chan, 16, nsrc), jnp.float32),
            pltpu.VMEM((16, nsrc), jnp.float32),
            pltpu.SemaphoreType.DMA((n_chan,)),
            pltpu.SemaphoreType.DMA((n_chan,)),
            pltpu.VMEM((n_chan, 16, nsrc), jnp.float32),
        ],
        compiler_params=pltpu.CompilerParams(collective_id=0, has_side_effects=True),
    )(offsets, record, dead, sources)


def shards(record, offsets, dead_mask, sources):
    n_tm = lax.axis_size("tm")
    n_chan = lax.axis_size("chan")
    bins_dev = F // n_tm
    channels, span = record.shape
    first, count = window_plan(n_tm, span)
    per = NWIN * 2 * bins_dev // n_chan
    assert per * n_chan == NWIN * 2 * bins_dev and bins_dev % per == 0 and per <= 16
    white, rotated, source_spec = fused_exchange(
        offsets, record, dead_mask.reshape(1, channels), sources.reshape(1, -1),
        n_tm, n_chan, bins_dev, first, count
    )
    return cross_spectra(source_spec, white, rotated)


def solution(mesh):
    return jax.shard_map(
        shards,
        mesh=mesh,
        in_specs=(P("chan", "tm"), P(), P("chan"), P()),
        out_specs=P("tm", None, None, "chan"),
        check_vma=False,
    )
```
